32 devices in a mesh: ctx: 16 (over z, y, core), tp: 2 (over x).
Axes of the slice: x: 2, y: 2, z: 4, core: 2. Of those that a mesh axis runs over, the one named last changes fastest.
Arguments:
- qkv: bfloat16 [2048, 32, 3, 128], P('ctx', 'tp'), may hold values from -5 to 5
- grad_out: bfloat16 [2048, 8192], P(('ctx', 'tp')), may hold values from -6 to 6
- attn_out: bfloat16 [4096, 8192], P('tp'), may hold values from -0.09375 to 0.09375
Outputs:
- mixed_out: float32 [2048, 8192], P(('ctx', 'tp'))
- grad_qkv: float32 [2048, 32, 3, 128], P('ctx', 'tp')
The draws below stay inside these ranges and needn't reach their ends.
All inputs are finite; a program needn't handle non-finite values.
Results may differ from the reference program's by a relative error of at most 0.0063.
Values may be sent and summed in bfloat16 or wider, within the bound.
No kernel may reach another device: no remote copies, remote signals or barrier semaphores. Data moves between devices by JAX's collectives and lax.ppermute only.
A program may use at most 192 MiB of HBM per device.

```python
import math
import jax
import jax.numpy as jnp
from jax import lax

D = 8192
HD = 128
HEADS = 32
SEQ = 2048


def draw_qkv(key, part):
    keys_all = jax.random.split(key, 1)
    full_shape = (SEQ, HEADS, 3, HD)
    return jnp.clip(jax.random.normal(keys_all[0], full_shape, jnp.float32), -5.0, 5.0).astype(jnp.bfloat16)


def block_levels(stream_key, extent, shards, low, high):
    def one(axis_at, shards_of):
        steps = jax.random.uniform(jax.random.fold_in(jax.random.fold_in(stream_key, 6), axis_at), (shards_of,), jnp.float32, low / len(shards), high / len(shards))
        return jnp.repeat(jnp.exp(steps), extent[axis_at] // shards_of).reshape((-1,) + (1,) * (len(extent) - axis_at - 1))

    level = one(*shards[0])
    for cut in shards[1:]:
        level = level * one(*cut)
    return level


def normal_values(own_key, shape, width, limit, cuts=(), kind=jnp.bfloat16):
    result = width * jax.random.normal(own_key, shape, jnp.float32)
    if cuts:
        result = result * block_levels(own_key, shape, cuts, -0.22, 0.18)
    return jnp.clip(result, -limit, limit).astype(kind)


def setup_inputs(seed: int = 0) -> dict:
    arg_keys = jax.random.split(jax.random.key(seed), 4)
    return {
        "qkv": draw_qkv(jax.random.fold_in(arg_keys[3], 71), 0),
        "grad_out": normal_values(arg_keys[1], (SEQ, D), 1.0, 6.0, ((0, 32),)),
        "attn_out": normal_values(arg_keys[2], (HEADS * HD, D), (HEADS * HD) ** -0.5, 0.09375, ((0, 2),)),
    }


def head_pass(operands):
    queries, keys_in, values_in, grad_att = operands
    factor = 1.0 / math.sqrt(HD)
    positions = jnp.arange(queries.shape[0], dtype=jnp.int32)
    visible = positions[None, :] <= positions[:, None]
    scores = jnp.dot(queries, keys_in.T, preferred_element_type=jnp.float32) * factor
    scores = jnp.where(visible, scores, -jnp.inf)
    row_max = lax.optimization_barrier(jnp.max(scores, axis=1, keepdims=True))
    log_total = row_max + jnp.log(lax.optimization_barrier(jnp.sum(jnp.exp(scores - row_max), axis=1, keepdims=True)))
    weights = jnp.exp(scores - log_total)
    weights_low = weights.astype(jnp.bfloat16)
    attended = jnp.dot(weights_low, values_in, preferred_element_type=jnp.float32).astype(jnp.bfloat16)
    row_delta = lax.optimization_barrier(jnp.sum(grad_att.astype(jnp.float32) * attended.astype(jnp.float32), axis=1, keepdims=True))
    grad_weights = jnp.dot(grad_att, values_in.T, preferred_element_type=jnp.float32)
    grad_scores = (weights * (grad_weights - row_delta) * factor).astype(jnp.bfloat16)
    grad_queries = jnp.dot(grad_scores, keys_in, preferred_element_type=jnp.float32)
    grad_keys = jnp.dot(grad_scores.T, queries, preferred_element_type=jnp.float32)
    grad_values = jnp.dot(weights_low.T, grad_att, preferred_element_type=jnp.float32)
    return (attended, grad_queries, grad_keys, grad_values)

def reference(qkv, grad_out, attn_out):
    seq_total = qkv.shape[0]
    queries = qkv[:, :, 0].transpose(1, 0, 2)
    keys_in = qkv[:, :, 1].transpose(1, 0, 2)
    values_in = qkv[:, :, 2].transpose(1, 0, 2)
    grad_full = jnp.dot(grad_out, attn_out.T, preferred_element_type=jnp.float32).astype(jnp.bfloat16)
    grad_att = grad_full.reshape(seq_total, HEADS, HD).transpose(1, 0, 2)
    attended, grad_queries, grad_keys, grad_values = lax.map(head_pass, (queries, keys_in, values_in, grad_att))
    attended_flat = attended.transpose(1, 0, 2).reshape(seq_total, HEADS * HD)
    mixed_out = jnp.dot(attended_flat, attn_out, preferred_element_type=jnp.float32)
    grad_qkv = jnp.stack([grad_queries, grad_keys, grad_values], axis=2).transpose(1, 0, 2, 3)
    return (mixed_out, grad_qkv)
```

```python
import functools
import math

import jax
import jax.numpy as jnp
from jax import lax
from jax.experimental import pallas as pl
from jax.experimental.pallas import tpu as pltpu
from jax.sharding import PartitionSpec as P

HD = 128
LOG2E = math.log2(math.e)
VMEM_LIMIT = 48 * 1024 * 1024


def dot_nt(a, b):
    return lax.dot_general(a, b, (((1,), (1,)), ((), ())), preferred_element_type=jnp.float32)


def dot_nn(a, b):
    return lax.dot_general(a, b, (((1,), (0,)), ((), ())), preferred_element_type=jnp.float32)


def rows_of(ref, start, count, *which):
    part = ref[(pl.ds(start, count), *which)]
    return part.reshape(count * part.shape[1], part.shape[2])


def forward_kernel(step, qkv_ref, att_ref, lse_ref, v_t, s_buf):
    chunks, _, unit, _ = qkv_ref.shape
    per = step // unit
    blocks = chunks // per
    scale = LOG2E / math.sqrt(HD)
    for b in range(blocks):
        v_t[b] = rows_of(qkv_ref, b * per, per, 2).T

    def query_block(i, _):
        q = rows_of(qkv_ref, i * per, per, 0)

        def scores(j, top):
            s = dot_nt(rows_of(qkv_ref, j * per, per, 1), q)
            s_buf[j] = s
            return jnp.maximum(top, jnp.max(s, axis=0, keepdims=True))

        top = lax.fori_loop(0, i, scores, jnp.full((1, step), -jnp.inf, jnp.float32))
        s = dot_nt(rows_of(qkv_ref, i * per, per, 1), q)
        key = lax.broadcasted_iota(jnp.int32, s.shape, 0)
        query = lax.broadcasted_iota(jnp.int32, s.shape, 1)
        s = jnp.where(key <= query, s, -jnp.inf)
        s_buf[i] = s
        top = jnp.maximum(top, jnp.max(s, axis=0, keepdims=True))

        def exps(j, total):
            p = jnp.exp2((s_buf[j] - top) * scale)
            s_buf[j] = p
            return total + jnp.sum(p, axis=0, keepdims=True)

        total = lax.fori_loop(0, i + 1, exps, jnp.zeros((1, step), jnp.float32))
        inverse = 1.0 / total

        def mix(j, acc):
            return acc + dot_nn(v_t[j], (s_buf[j] * inverse).astype(jnp.bfloat16))

        acc = lax.fori_loop(0, i + 1, mix, jnp.zeros((HD, step), jnp.float32))
        att_ref[pl.ds(i * per, per)] = acc.T.astype(jnp.bfloat16).reshape(per, unit, HD)
        lse_ref[i] = top * scale + jnp.log2(total)
        return 0

    lax.fori_loop(0, blocks, query_block, 0)


def backward_kernel(step, qkv_ref, g_ref, att_ref, lse_ref, out_ref, k_t, dq_t, delta):
    chunks, _, unit, _ = qkv_ref.shape
    per = step // unit
    blocks = chunks // per
    factor = 1.0 / math.sqrt(HD)
    for b in range(blocks):
        k_t[b] = rows_of(qkv_ref, b * per, per, 1).T
        prod = rows_of(g_ref, b * per, per).astype(jnp.float32)
        prod = prod * rows_of(att_ref, b * per, per).astype(jnp.float32)
        delta[b] = jnp.sum(prod.T, axis=0, keepdims=True)

    def key_block(j, _):
        k = rows_of(qkv_ref, j * per, per, 1)
        v = rows_of(qkv_ref, j * per, per, 2)
        kt = k_t[j]

        def pair(i, diagonal):
            q = rows_of(qkv_ref, i * per, per, 0)
            g = rows_of(g_ref, i * per, per)
            w = jnp.exp2(dot_nt(k, q) * (factor * LOG2E) - lse_ref[i])
            if diagonal:
                key = lax.broadcasted_iota(jnp.int32, w.shape, 0)
                query = lax.broadcasted_iota(jnp.int32, w.shape, 1)
                w = jnp.where(key <= query, w, 0.0)
            ds = (w * (dot_nt(v, g) - delta[i]) * factor).astype(jnp.bfloat16)
            dv = dot_nn(w.astype(jnp.bfloat16), g)
            dk = dot_nn(ds, q)
            return dk, dv, dot_nn(kt, ds)

        dk, dv, part = pair(j, True)

        @pl.when(j == 0)
        def _():
            dq_t[j] = part

        @pl.when(j > 0)
        def _():
            dq_t[j] = dq_t[j] + part

        def later(i, carry):
            dk, dv, part = pair(i, False)

            @pl.when(j == 0)
            def _():
                dq_t[i] = part

            @pl.when(j > 0)
            def _():
                dq_t[i] = dq_t[i] + part

            return carry[0] + dk, carry[1] + dv

        dk, dv = lax.fori_loop(j + 1, blocks, later, (dk, dv))
        spot = pl.ds(j * per, per)
        out_ref[spot, 1] = dk.astype(jnp.bfloat16).reshape(per, unit, HD)
        out_ref[spot, 2] = dv.astype(jnp.bfloat16).reshape(per, unit, HD)
        return 0

    lax.fori_loop(0, blocks, key_block, 0)
    for b in range(blocks):
        out_ref[pl.ds(b * per, per), 0] = dq_t[b].T.astype(jnp.bfloat16).reshape(per, unit, HD)


def in_vmem(count):
    return [pl.BlockSpec(memory_space=pltpu.VMEM)] * count


def attend(qkv, step):
    chunks, _, unit, _ = qkv.shape
    length = chunks * unit
    blocks = length // step
    area = length * length // 2
    return pl.pallas_call(
        functools.partial(forward_kernel, step),
        out_shape=(
            jax.ShapeDtypeStruct((chunks, unit, HD), jnp.bfloat16),
            jax.ShapeDtypeStruct((blocks, 1, step), jnp.float32),
        ),
        in_specs=in_vmem(1),
        out_specs=tuple(in_vmem(2)),
        scratch_shapes=[
            pltpu.VMEM((blocks, HD, step), jnp.bfloat16),
            pltpu.VMEM((blocks, step, step), jnp.float32),
        ],
        compiler_params=pltpu.CompilerParams(vmem_limit_bytes=VMEM_LIMIT),
        cost_estimate=pl.CostEstimate(
            flops=4 * area * HD, transcendentals=area, bytes_accessed=8 * length * HD
        ),
        name="attend",
    )(qkv)


def attend_grad(qkv, g, att, lse, step):
    chunks, _, unit, _ = qkv.shape
    length = chunks * unit
    blocks = length // step
    area = length * length // 2
    return pl.pallas_call(
        functools.partial(backward_kernel, step),
        out_shape=jax.ShapeDtypeStruct((chunks, 3, unit, HD), jnp.bfloat16),
        in_specs=in_vmem(4),
        out_specs=in_vmem(1)[0],
        scratch_shapes=[
            pltpu.VMEM((blocks, HD, step), jnp.bfloat16),
            pltpu.VMEM((blocks, HD, step), jnp.float32),
            pltpu.VMEM((blocks, 1, step), jnp.float32),
        ],
        compiler_params=pltpu.CompilerParams(vmem_limit_bytes=VMEM_LIMIT),
        cost_estimate=pl.CostEstimate(
            flops=10 * area * HD, transcendentals=area, bytes_accessed=16 * length * HD
        ),
        name="attend_grad",
    )(qkv, g, att, lse)


def by_head(qkv, grad_out, attn_out):
    rows, heads = qkv.shape[:2]
    half = grad_out.shape[0]
    width = attn_out.shape[1]
    step = 512 if (rows * heads) % 512 == 0 else rows
    swap = [(0, 1), (1, 0)]
    turn = lax.axis_index("tp")
    weights = attn_out.reshape(heads, HD, width)

    def spread(x):
        return lax.all_to_all(x, "ctx", 0, 0, tiled=True)

    other_out = lax.ppermute(grad_out, "tp", swap)
    mine = spread(jnp.transpose(qkv, (1, 2, 0, 3)))

    def back(x):
        y = jnp.einsum("nm,hdm->hnd", x, weights, preferred_element_type=jnp.float32)
        return y.astype(jnp.bfloat16)

    g_own, g_other = back(grad_out), back(other_out)
    first = jnp.where(turn == 0, g_own, g_other)
    second = jnp.where(turn == 0, g_other, g_own)
    g = spread(jnp.concatenate([first, second], axis=1))

    att, lse = attend(mine, step)
    local = spread(att)
    mixed = jnp.einsum("hrd,hdm->rm", local, weights, preferred_element_type=jnp.float32)
    sent = lax.dynamic_slice_in_dim(mixed, (1 - turn) * half, half, 0).astype(jnp.bfloat16)
    kept = lax.dynamic_slice_in_dim(mixed, turn * half, half, 0)
    mixed_out = kept + lax.ppermute(sent, "tp", swap).astype(jnp.float32)

    grads = spread(attend_grad(mine, g, att, lse, step))
    return mixed_out, jnp.transpose(grads, (2, 0, 1, 3)).astype(jnp.float32)


def by_rows(qkv, grad_out, attn_out):
    row_count, heads_local = (qkv.shape[0], qkv.shape[1])
    factor = 1.0 / math.sqrt(HD)
    queries = qkv[:, :, 0]
    keys_local = qkv[:, :, 1]
    values_local = qkv[:, :, 2]
    all_keys, all_values = (
        lax.all_gather(keys_local, "ctx", axis=0, tiled=True),
        lax.all_gather(values_local, "ctx", axis=0, tiled=True),
    )
    seq_len = all_keys.shape[0]
    offset = lax.axis_index("ctx") * row_count
    query_pos = offset + jnp.arange(row_count, dtype=jnp.int32)
    key_pos = jnp.arange(seq_len, dtype=jnp.int32)
    visible = key_pos[None, :] <= query_pos[:, None]
    scores = (
        jnp.einsum("rhd,shd->hrs", queries, all_keys, preferred_element_type=jnp.float32) * factor
    )
    scores = jnp.where(visible[None], scores, -jnp.inf)
    row_max = jnp.max(scores, axis=2, keepdims=True)
    log_total = row_max + jnp.log(jnp.sum(jnp.exp(scores - row_max), axis=2, keepdims=True))
    weights = jnp.exp(scores - log_total)
    weights_low = weights.astype(jnp.bfloat16)
    attended = jnp.einsum(
        "hrs,shd->rhd", weights_low, all_values, preferred_element_type=jnp.float32
    ).astype(jnp.bfloat16)
    attended_flat = attended.reshape(row_count, heads_local * HD)
    mixed_out = lax.psum_scatter(
        jnp.dot(attended_flat, attn_out, preferred_element_type=jnp.float32),
        "tp",
        scatter_dimension=0,
        tiled=True,
    )
    grad_full = jnp.einsum(
        "nm,km->nk",
        lax.all_gather(grad_out, "tp", axis=0, tiled=True),
        attn_out,
        preferred_element_type=jnp.float32,
    )
    grad_att = grad_full.astype(jnp.bfloat16).reshape(row_count, heads_local, HD)
    row_delta = jnp.einsum("rhd,rhd->rh", grad_att, attended, preferred_element_type=jnp.float32)
    grad_weights = jnp.einsum(
        "rhd,shd->hrs", grad_att, all_values, preferred_element_type=jnp.float32
    )
    grad_scores = (weights * (grad_weights - row_delta.T[:, :, None]) * factor).astype(jnp.bfloat16)
    grad_queries = jnp.einsum(
        "hrs,shd->rhd", grad_scores, all_keys, preferred_element_type=jnp.float32
    )
    lse_rows = log_total[:, :, 0].T
    row_stats = (
        lax.all_gather(lse_rows, "ctx", axis=0, tiled=True),
        lax.all_gather(row_delta, "ctx", axis=0, tiled=True),
    )
    piece_q = lax.all_gather(queries, "ctx", axis=0, tiled=True)
    piece_g = lax.all_gather(grad_att, "ctx", axis=0, tiled=True)
    piece_len = piece_q.shape[0]
    piece_lse = row_stats[0]
    piece_delta = row_stats[1]
    piece_pos = jnp.arange(piece_len, dtype=jnp.int32)
    visible_part = query_pos[None, :] <= piece_pos[:, None]
    part_scores = (
        jnp.einsum("nhd,rhd->hnr", piece_q, keys_local, preferred_element_type=jnp.float32) * factor
    )
    part_weights = jnp.where(
        visible_part[None], jnp.exp(part_scores - piece_lse.T[:, :, None]), 0.0
    )
    part_grad = jnp.einsum(
        "nhd,rhd->hnr", piece_g, values_local, preferred_element_type=jnp.float32
    )
    part_ds = (part_weights * (part_grad - piece_delta.T[:, :, None]) * factor).astype(jnp.bfloat16)
    grad_k = jnp.einsum("hnr,nhd->rhd", part_ds, piece_q, preferred_element_type=jnp.float32)
    grad_v = jnp.einsum(
        "hnr,nhd->rhd",
        part_weights.astype(jnp.bfloat16),
        piece_g,
        preferred_element_type=jnp.float32,
    )
    grad_qkv = jnp.stack([grad_queries, grad_k, grad_v], axis=2)
    return (mixed_out, grad_qkv)


def solution(mesh):
    ctx, tp = mesh.shape["ctx"], mesh.shape["tp"]

    def per_device(qkv, grad_out, attn_out):
        path = by_head if qkv.shape[1] == ctx and tp == 2 else by_rows
        return path(qkv, grad_out, attn_out)

    in_specs = (P("ctx", "tp", None, None), P(("ctx", "tp"), None), P("tp", None))
    out_specs = (P(("ctx", "tp"), None), P("ctx", "tp", None, None))
    return jax.shard_map(
        per_device, mesh=mesh, in_specs=in_specs, out_specs=out_specs, check_vma=False
    )
```

```python
import functools
import math

import jax
import jax.numpy as jnp
from jax import lax
from jax.experimental import pallas as pl
from jax.experimental.pallas import tpu as pltpu
from jax.sharding import PartitionSpec as P


HD = 128
LOG2E = math.log2(math.e)
MIX_PARTS = 2
VMEM_LIMIT = 48 * 1024 * 1024


def dot_nt(a, b):
    return lax.dot_general(a, b, (((1,), (1,)), ((), ())), preferred_element_type=jnp.float32)


def dot_nn(a, b):
    return lax.dot_general(a, b, (((1,), (0,)), ((), ())), preferred_element_type=jnp.float32)


def rows_of(ref, start, count, *which):
    part = ref[(pl.ds(start, count), *which)]
    return part.reshape(count * part.shape[1], part.shape[2])


def forward_kernel(step, qkv_ref, att_ref, lse_ref, v_t, s_buf):
    chunks, _, unit, _ = qkv_ref.shape
    per = step // unit
    blocks = chunks // per
    scale = LOG2E / math.sqrt(HD)
    for b in range(blocks):
        v_t[b] = rows_of(qkv_ref, b * per, per, 2).T

    def query_block(i, _):
        q = rows_of(qkv_ref, i * per, per, 0)

        def scores(j, top):
            s = dot_nt(rows_of(qkv_ref, j * per, per, 1), q)
            s_buf[j] = s
            return jnp.maximum(top, jnp.max(s, axis=0, keepdims=True))

        top = lax.fori_loop(0, i, scores, jnp.full((1, step), -jnp.inf, jnp.float32))
        s = dot_nt(rows_of(qkv_ref, i * per, per, 1), q)
        key = lax.broadcasted_iota(jnp.int32, s.shape, 0)
        query = lax.broadcasted_iota(jnp.int32, s.shape, 1)
        s = jnp.where(key <= query, s, -jnp.inf)
        s_buf[i] = s
        top = jnp.maximum(top, jnp.max(s, axis=0, keepdims=True))

        def exps(j, total):
            p = jnp.exp2((s_buf[j] - top) * scale)
            s_buf[j] = p
            return total + jnp.sum(p, axis=0, keepdims=True)

        total = lax.fori_loop(0, i + 1, exps, jnp.zeros((1, step), jnp.float32))
        inverse = 1.0 / total

        def mix(j, acc):
            return acc + dot_nn(v_t[j], (s_buf[j] * inverse).astype(jnp.bfloat16))

        acc = lax.fori_loop(0, i + 1, mix, jnp.zeros((HD, step), jnp.float32))
        att_ref[pl.ds(i * per, per)] = acc.T.astype(jnp.bfloat16).reshape(per, unit, HD)
        lse_ref[i] = top * scale + jnp.log2(total)
        return 0

    lax.fori_loop(0, blocks, query_block, 0)


def backward_kernel(step, qkv_ref, g_ref, att_ref, lse_ref, out_ref, k_t, dq_t, delta):
    chunks, _, unit, _ = qkv_ref.shape
    per = step // unit
    blocks = chunks // per
    factor = 1.0 / math.sqrt(HD)
    for b in range(blocks):
        k_t[b] = rows_of(qkv_ref, b * per, per, 1).T
        prod = rows_of(g_ref, b * per, per).astype(jnp.float32)
        prod = prod * rows_of(att_ref, b * per, per).astype(jnp.float32)
        delta[b] = jnp.sum(prod.T, axis=0, keepdims=True)

    def key_block(j, _):
        k = rows_of(qkv_ref, j * per, per, 1)
        v = rows_of(qkv_ref, j * per, per, 2)
        kt = k_t[j]

        def pair(i, diagonal):
            q = rows_of(qkv_ref, i * per, per, 0)
            g = rows_of(g_ref, i * per, per)
            w = jnp.exp2(dot_nt(k, q) * (factor * LOG2E) - lse_ref[i])
            if diagonal:
                key = lax.broadcasted_iota(jnp.int32, w.shape, 0)
                query = lax.broadcasted_iota(jnp.int32, w.shape, 1)
                w = jnp.where(key <= query, w, 0.0)
            ds = (w * (dot_nt(v, g) - delta[i]) * factor).astype(jnp.bfloat16)
            dv = dot_nn(w.astype(jnp.bfloat16), g)
            dk = dot_nn(ds, q)
            return dk, dv, dot_nn(kt, ds)

        dk, dv, part = pair(j, True)

        @pl.when(j == 0)
        def _():
            dq_t[j] = part

        @pl.when(j > 0)
        def _():
            dq_t[j] = dq_t[j] + part

        def later(i, carry):
            dk, dv, part = pair(i, False)

            @pl.when(j == 0)
            def _():
                dq_t[i] = part

            @pl.when(j > 0)
            def _():
                dq_t[i] = dq_t[i] + part

            return carry[0] + dk, carry[1] + dv

        dk, dv = lax.fori_loop(j + 1, blocks, later, (dk, dv))
        spot = pl.ds(j * per, per)
        out_ref[spot, 1] = dk.astype(jnp.bfloat16).reshape(per, unit, HD)
        out_ref[spot, 2] = dv.astype(jnp.bfloat16).reshape(per, unit, HD)
        return 0

    lax.fori_loop(0, blocks, key_block, 0)
    for b in range(blocks):
        out_ref[pl.ds(b * per, per), 0] = dq_t[b].T.astype(jnp.bfloat16).reshape(per, unit, HD)


def in_vmem(count):
    return [pl.BlockSpec(memory_space=pltpu.VMEM)] * count


def attend(qkv, step):
    chunks, _, unit, _ = qkv.shape
    length = chunks * unit
    blocks = length // step
    area = length * length // 2
    return pl.pallas_call(
        functools.partial(forward_kernel, step),
        out_shape=(
            jax.ShapeDtypeStruct((chunks, unit, HD), jnp.bfloat16),
            jax.ShapeDtypeStruct((blocks, 1, step), jnp.float32),
        ),
        in_specs=in_vmem(1),
        out_specs=tuple(in_vmem(2)),
        scratch_shapes=[
            pltpu.VMEM((blocks, HD, step), jnp.bfloat16),
            pltpu.VMEM((blocks, step, step), jnp.float32),
        ],
        compiler_params=pltpu.CompilerParams(vmem_limit_bytes=VMEM_LIMIT),
        cost_estimate=pl.CostEstimate(
            flops=4 * area * HD, transcendentals=area, bytes_accessed=8 * length * HD
        ),
        name="attend",
    )(qkv)


def attend_grad(qkv, g, att, lse, step):
    chunks, _, unit, _ = qkv.shape
    length = chunks * unit
    blocks = length // step
    area = length * length // 2
    return pl.pallas_call(
        functools.partial(backward_kernel, step),
        out_shape=jax.ShapeDtypeStruct((chunks, 3, unit, HD), jnp.bfloat16),
        in_specs=in_vmem(4),
        out_specs=in_vmem(1)[0],
        scratch_shapes=[
            pltpu.VMEM((blocks, HD, step), jnp.bfloat16),
            pltpu.VMEM((blocks, HD, step), jnp.float32),
            pltpu.VMEM((blocks, 1, step), jnp.float32),
        ],
        compiler_params=pltpu.CompilerParams(vmem_limit_bytes=VMEM_LIMIT),
        cost_estimate=pl.CostEstimate(
            flops=10 * area * HD, transcendentals=area, bytes_accessed=16 * length * HD
        ),
        name="attend_grad",
    )(qkv, g, att, lse)


def by_head(qkv, grad_out, attn_out):
    rows, heads = qkv.shape[:2]
    half = grad_out.shape[0]
    width = attn_out.shape[1]
    step = 512 if (rows * heads) % 512 == 0 else rows
    swap = [(0, 1), (1, 0)]
    turn = lax.axis_index("tp")
    weights = attn_out.reshape(heads, HD, width)

    def spread(x):
        return lax.all_to_all(x, "ctx", 0, 0, tiled=True)

    def back(x):
        y = jnp.einsum("nm,hdm->hnd", x, weights, preferred_element_type=jnp.float32)
        return y.astype(jnp.bfloat16)

    other_out = lax.ppermute(grad_out, "tp", swap)
    mine = spread(jnp.transpose(qkv, (1, 2, 0, 3)))
    g_own, g_other = back(grad_out), back(other_out)
    first = jnp.where(turn == 0, g_own, g_other)
    second = jnp.where(turn == 0, g_other, g_own)
    g_all = jnp.concatenate([first, second], axis=1)
    g = spread(g_all)
    att, lse = attend(mine, step)
    local = spread(att)
    grads = attend_grad(mine, g, att, lse, step)
    grads = spread(grads)
    pieces = []
    part = width // MIX_PARTS
    for c in range(MIX_PARTS):
        mixed = jnp.einsum(
            "hrd,hdm->rm",
            local,
            weights[:, :, c * part : (c + 1) * part],
            preferred_element_type=jnp.float32,
        )
        sent = lax.dynamic_slice_in_dim(mixed, (1 - turn) * half, half, 0)
        kept = lax.dynamic_slice_in_dim(mixed, turn * half, half, 0)
        got = lax.ppermute(sent.astype(jnp.bfloat16), "tp", swap)
        pieces.append(kept + got.astype(jnp.float32))
    mixed_out = jnp.concatenate(pieces, axis=1)
    return mixed_out, jnp.transpose(grads, (2, 0, 1, 3)).astype(jnp.float32)


def by_rows(qkv, grad_out, attn_out):
    row_count, heads_local = (qkv.shape[0], qkv.shape[1])
    factor = 1.0 / math.sqrt(HD)
    queries = qkv[:, :, 0]
    keys_local = qkv[:, :, 1]
    values_local = qkv[:, :, 2]
    all_keys, all_values = (
        lax.all_gather(keys_local, "ctx", axis=0, tiled=True),
        lax.all_gather(values_local, "ctx", axis=0, tiled=True),
    )
    seq_len = all_keys.shape[0]
    offset = lax.axis_index("ctx") * row_count
    query_pos = offset + jnp.arange(row_count, dtype=jnp.int32)
    key_pos = jnp.arange(seq_len, dtype=jnp.int32)
    visible = key_pos[None, :] <= query_pos[:, None]
    scores = (
        jnp.einsum("rhd,shd->hrs", queries, all_keys, preferred_element_type=jnp.float32) * factor
    )
    scores = jnp.where(visible[None], scores, -jnp.inf)
    row_max = jnp.max(scores, axis=2, keepdims=True)
    log_total = row_max + jnp.log(jnp.sum(jnp.exp(scores - row_max), axis=2, keepdims=True))
    weights = jnp.exp(scores - log_total)
    weights_low = weights.astype(jnp.bfloat16)
    attended = jnp.einsum(
        "hrs,shd->rhd", weights_low, all_values, preferred_element_type=jnp.float32
    ).astype(jnp.bfloat16)
    attended_flat = attended.reshape(row_count, heads_local * HD)
    mixed_out = lax.psum_scatter(
        jnp.dot(attended_flat, attn_out, preferred_element_type=jnp.float32),
        "tp",
        scatter_dimension=0,
        tiled=True,
    )
    grad_full = jnp.einsum(
        "nm,km->nk",
        lax.all_gather(grad_out, "tp", axis=0, tiled=True),
        attn_out,
        preferred_element_type=jnp.float32,
    )
    grad_att = grad_full.astype(jnp.bfloat16).reshape(row_count, heads_local, HD)
    row_delta = jnp.einsum("rhd,rhd->rh", grad_att, attended, preferred_element_type=jnp.float32)
    grad_weights = jnp.einsum(
        "rhd,shd->hrs", grad_att, all_values, preferred_element_type=jnp.float32
    )
    grad_scores = (weights * (grad_weights - row_delta.T[:, :, None]) * factor).astype(jnp.bfloat16)
    grad_queries = jnp.einsum(
        "hrs,shd->rhd", grad_scores, all_keys, preferred_element_type=jnp.float32
    )
    lse_rows = log_total[:, :, 0].T
    row_stats = (
        lax.all_gather(lse_rows, "ctx", axis=0, tiled=True),
        lax.all_gather(row_delta, "ctx", axis=0, tiled=True),
    )
    piece_q = lax.all_gather(queries, "ctx", axis=0, tiled=True)
    piece_g = lax.all_gather(grad_att, "ctx", axis=0, tiled=True)
    piece_len = piece_q.shape[0]
    piece_lse = row_stats[0]
    piece_delta = row_stats[1]
    piece_pos = jnp.arange(piece_len, dtype=jnp.int32)
    visible_part = query_pos[None, :] <= piece_pos[:, None]
    part_scores = (
        jnp.einsum("nhd,rhd->hnr", piece_q, keys_local, preferred_element_type=jnp.float32) * factor
    )
    part_weights = jnp.where(
        visible_part[None], jnp.exp(part_scores - piece_lse.T[:, :, None]), 0.0
    )
    part_grad = jnp.einsum(
        "nhd,rhd->hnr", piece_g, values_local, preferred_element_type=jnp.float32
    )
    part_ds = (part_weights * (part_grad - piece_delta.T[:, :, None]) * factor).astype(jnp.bfloat16)
    grad_k = jnp.einsum("hnr,nhd->rhd", part_ds, piece_q, preferred_element_type=jnp.float32)
    grad_v = jnp.einsum(
        "hnr,nhd->rhd",
        part_weights.astype(jnp.bfloat16),
        piece_g,
        preferred_element_type=jnp.float32,
    )
    grad_qkv = jnp.stack([grad_queries, grad_k, grad_v], axis=2)
    return (mixed_out, grad_qkv)


def solution(mesh):
    ctx, tp = mesh.shape["ctx"], mesh.shape["tp"]
    in_specs = (P("ctx", "tp", None, None), P(("ctx", "tp"), None), P("tp", None))
    out_specs = (P(("ctx", "tp"), None), P("ctx", "tp", None, None))

    def whole(qkv, grad_out, attn_out):
        split = qkv.shape[1] == ctx * tp and tp == 2
        step = jax.shard_map(
            by_head if split else by_rows,
            mesh=mesh,
            in_specs=in_specs,
            out_specs=out_specs,
            check_vma=False,
        )
        return step(qkv, grad_out, attn_out)

    return whole
```

```python
import functools
import math

import jax
import jax.numpy as jnp
from jax import lax
from jax.experimental import pallas as pl
from jax.experimental.pallas import tpu as pltpu
from jax.sharding import PartitionSpec as P


HD = 128
LOG2E = math.log2(math.e)
MIX_PARTS = 4
BACK_PARTS = (4, 2, 2)
VMEM_LIMIT = 48 * 1024 * 1024


def dot_nt(a, b):
    return lax.dot_general(a, b, (((1,), (1,)), ((), ())), preferred_element_type=jnp.float32)


def dot_nn(a, b):
    return lax.dot_general(a, b, (((1,), (0,)), ((), ())), preferred_element_type=jnp.float32)


def rows_of(ref, start, count, *which):
    part = ref[(pl.ds(start, count), *which)]
    return part.reshape(count * part.shape[1], part.shape[2])


def forward_kernel(step, qkv_ref, att_ref, lse_ref, v_t, s_buf):
    chunks, _, unit, _ = qkv_ref.shape
    per = step // unit
    blocks = chunks // per
    scale = LOG2E / math.sqrt(HD)
    for b in range(blocks):
        v_t[b] = rows_of(qkv_ref, b * per, per, 2).T

    def query_block(i, _):
        q = rows_of(qkv_ref, i * per, per, 0)

        def scores(j, top):
            s = dot_nt(rows_of(qkv_ref, j * per, per, 1), q)
            s_buf[j] = s
            return jnp.maximum(top, jnp.max(s, axis=0, keepdims=True))

        top = lax.fori_loop(0, i, scores, jnp.full((1, step), -jnp.inf, jnp.float32))
        s = dot_nt(rows_of(qkv_ref, i * per, per, 1), q)
        key = lax.broadcasted_iota(jnp.int32, s.shape, 0)
        query = lax.broadcasted_iota(jnp.int32, s.shape, 1)
        s = jnp.where(key <= query, s, -jnp.inf)
        s_buf[i] = s
        top = jnp.maximum(top, jnp.max(s, axis=0, keepdims=True))

        def exps(j, total):
            p = jnp.exp2((s_buf[j] - top) * scale)
            s_buf[j] = p
            return total + jnp.sum(p, axis=0, keepdims=True)

        total = lax.fori_loop(0, i + 1, exps, jnp.zeros((1, step), jnp.float32))
        inverse = 1.0 / total

        def mix(j, acc):
            return acc + dot_nn(v_t[j], (s_buf[j] * inverse).astype(jnp.bfloat16))

        acc = lax.fori_loop(0, i + 1, mix, jnp.zeros((HD, step), jnp.float32))
        att_ref[pl.ds(i * per, per)] = acc.T.astype(jnp.bfloat16).reshape(per, unit, HD)
        lse_ref[i] = top * scale + jnp.log2(total)
        return 0

    lax.fori_loop(0, blocks, query_block, 0)


def backward_kernel(step, qkv_ref, g_ref, att_ref, lse_ref, out_ref, k_t, dq_t, delta):
    chunks, _, unit, _ = qkv_ref.shape
    per = step // unit
    blocks = chunks // per
    factor = 1.0 / math.sqrt(HD)
    for b in range(blocks):
        k_t[b] = rows_of(qkv_ref, b * per, per, 1).T
        prod = rows_of(g_ref, b * per, per).astype(jnp.float32)
        prod = prod * rows_of(att_ref, b * per, per).astype(jnp.float32)
        delta[b] = jnp.sum(prod.T, axis=0, keepdims=True)

    def key_block(j, _):
        k = rows_of(qkv_ref, j * per, per, 1)
        v = rows_of(qkv_ref, j * per, per, 2)
        kt = k_t[j]

        def pair(i, diagonal):
            q = rows_of(qkv_ref, i * per, per, 0)
            g = rows_of(g_ref, i * per, per)
            w = jnp.exp2(dot_nt(k, q) * (factor * LOG2E) - lse_ref[i])
            if diagonal:
                key = lax.broadcasted_iota(jnp.int32, w.shape, 0)
                query = lax.broadcasted_iota(jnp.int32, w.shape, 1)
                w = jnp.where(key <= query, w, 0.0)
            ds = (w * (dot_nt(v, g) - delta[i]) * factor).astype(jnp.bfloat16)
            dv = dot_nn(w.astype(jnp.bfloat16), g)
            dk = dot_nn(ds, q)
            return dk, dv, dot_nn(kt, ds)

        dk, dv, part = pair(j, True)

        @pl.when(j == 0)
        def _():
            dq_t[j] = part

        @pl.when(j > 0)
        def _():
            dq_t[j] = dq_t[j] + part

        def later(i, carry):
            dk, dv, part = pair(i, False)

            @pl.when(j == 0)
            def _():
                dq_t[i] = part

            @pl.when(j > 0)
            def _():
                dq_t[i] = dq_t[i] + part

            return carry[0] + dk, carry[1] + dv

        dk, dv = lax.fori_loop(j + 1, blocks, later, (dk, dv))
        spot = pl.ds(j * per, per)
        out_ref[spot, 1] = dk.astype(jnp.bfloat16).reshape(per, unit, HD)
        out_ref[spot, 2] = dv.astype(jnp.bfloat16).reshape(per, unit, HD)
        return 0

    lax.fori_loop(0, blocks, key_block, 0)
    for b in range(blocks):
        out_ref[pl.ds(b * per, per), 0] = dq_t[b].T.astype(jnp.bfloat16).reshape(per, unit, HD)


def in_vmem(count):
    return [pl.BlockSpec(memory_space=pltpu.VMEM)] * count


def attend(qkv, step):
    chunks, _, unit, _ = qkv.shape
    length = chunks * unit
    blocks = length // step
    area = length * length // 2
    return pl.pallas_call(
        functools.partial(forward_kernel, step),
        out_shape=(
            jax.ShapeDtypeStruct((chunks, unit, HD), jnp.bfloat16),
            jax.ShapeDtypeStruct((blocks, 1, step), jnp.float32),
        ),
        in_specs=in_vmem(1),
        out_specs=tuple(in_vmem(2)),
        scratch_shapes=[
            pltpu.VMEM((blocks, HD, step), jnp.bfloat16),
            pltpu.VMEM((blocks, step, step), jnp.float32),
        ],
        compiler_params=pltpu.CompilerParams(vmem_limit_bytes=VMEM_LIMIT),
        cost_estimate=pl.CostEstimate(
            flops=4 * area * HD, transcendentals=area, bytes_accessed=8 * length * HD
        ),
        name="attend",
    )(qkv)


def attend_grad(qkv, g, att, lse, step):
    chunks, _, unit, _ = qkv.shape
    length = chunks * unit
    blocks = length // step
    area = length * length // 2
    return pl.pallas_call(
        functools.partial(backward_kernel, step),
        out_shape=jax.ShapeDtypeStruct((chunks, 3, unit, HD), jnp.bfloat16),
        in_specs=in_vmem(4),
        out_specs=in_vmem(1)[0],
        scratch_shapes=[
            pltpu.VMEM((blocks, HD, step), jnp.bfloat16),
            pltpu.VMEM((blocks, HD, step), jnp.float32),
            pltpu.VMEM((blocks, 1, step), jnp.float32),
        ],
        compiler_params=pltpu.CompilerParams(vmem_limit_bytes=VMEM_LIMIT),
        cost_estimate=pl.CostEstimate(
            flops=10 * area * HD, transcendentals=area, bytes_accessed=16 * length * HD
        ),
        name="attend_grad",
    )(qkv, g, att, lse)


def staged(x):
    count = x.shape[0]
    me = lax.axis_index("ctx")
    outer = count // 4
    x = x.reshape(outer, 2, 2, *x.shape[1:])

    def pair(x, axis, bit):
        place = (me // bit) % 2
        kept = lax.dynamic_index_in_dim(x, place, axis, keepdims=False)
        sent = lax.dynamic_index_in_dim(x, 1 - place, axis, keepdims=False)
        got = lax.ppermute(sent, "ctx", [(i, i ^ bit) for i in range(count)])
        first = jnp.where(place == 0, kept, got)
        second = jnp.where(place == 0, got, kept)
        return jnp.stack([first, second], axis=axis)

    x = pair(x, 2, 1)
    x = pair(x, 1, 2)
    place = me // 4
    pieces = [lax.dynamic_index_in_dim(x, place, 0, keepdims=False)]
    for d in range(1, outer):
        sent = lax.dynamic_index_in_dim(x, place ^ d, 0, keepdims=False)
        pieces.append(lax.ppermute(sent, "ctx", [(i, i ^ (4 * d)) for i in range(count)]))
    x = jnp.stack(pieces)
    x = jnp.concatenate(
        [lax.dynamic_slice_in_dim(x, place ^ d, 1, axis=0) for d in range(outer)], axis=0
    )
    return x.reshape(count, *x.shape[3:])


def by_head(qkv, grad_out, attn_out):
    rows, heads = qkv.shape[:2]
    half = grad_out.shape[0]
    width = attn_out.shape[1]
    step = 512 if (rows * heads) % 512 == 0 else rows
    swap = [(0, 1), (1, 0)]
    turn = lax.axis_index("tp")
    weights = attn_out.reshape(heads, HD, width)

    def spread(x):
        return lax.all_to_all(x, "ctx", 0, 0, tiled=True)

    y = None
    start = 0
    for eighths in BACK_PARTS:
        stop = start + eighths * (width // 8)
        part = grad_out[:, start:stop]
        other = lax.ppermute(part, "tp", swap)
        term = jnp.einsum(
            "nm,hdm->hnd",
            jnp.concatenate([part, other], axis=0),
            weights[:, :, start:stop],
            preferred_element_type=jnp.float32,
        )
        y = term if y is None else term + lax.optimization_barrier(y)
        start = stop
    mine = spread(jnp.transpose(qkv, (1, 2, 0, 3)))
    y = y.astype(jnp.bfloat16)
    g_own, g_other = y[:, :half], y[:, half:]
    first = jnp.where(turn == 0, g_own, g_other)
    second = jnp.where(turn == 0, g_other, g_own)
    g_all = jnp.concatenate([first, second], axis=1)
    g = staged(g_all)
    att, lse = attend(mine, step)
    att, g = lax.optimization_barrier((att, g))
    local = staged(att)
    grads = attend_grad(mine, g, att, lse, step)
    grads = spread(grads)
    pieces = []
    part = width // MIX_PARTS
    for c in range(MIX_PARTS):
        mixed = jnp.einsum(
            "hrd,hdm->rm",
            local,
            weights[:, :, c * part : (c + 1) * part],
            preferred_element_type=jnp.float32,
        )
        sent = lax.dynamic_slice_in_dim(mixed, (1 - turn) * half, half, 0)
        kept = lax.dynamic_slice_in_dim(mixed, turn * half, half, 0)
        got = lax.ppermute(sent.astype(jnp.bfloat16), "tp", swap)
        pieces.append(kept + got.astype(jnp.float32))
    mixed_out = jnp.concatenate(pieces, axis=1)
    return mixed_out, jnp.transpose(grads, (2, 0, 1, 3)).astype(jnp.float32)


def by_rows(qkv, grad_out, attn_out):
    row_count, heads_local = (qkv.shape[0], qkv.shape[1])
    factor = 1.0 / math.sqrt(HD)
    queries = qkv[:, :, 0]
    keys_local = qkv[:, :, 1]
    values_local = qkv[:, :, 2]
    all_keys, all_values = (
        lax.all_gather(keys_local, "ctx", axis=0, tiled=True),
        lax.all_gather(values_local, "ctx", axis=0, tiled=True),
    )
    seq_len = all_keys.shape[0]
    offset = lax.axis_index("ctx") * row_count
    query_pos = offset + jnp.arange(row_count, dtype=jnp.int32)
    key_pos = jnp.arange(seq_len, dtype=jnp.int32)
    visible = key_pos[None, :] <= query_pos[:, None]
    scores = (
        jnp.einsum("rhd,shd->hrs", queries, all_keys, preferred_element_type=jnp.float32) * factor
    )
    scores = jnp.where(visible[None], scores, -jnp.inf)
    row_max = jnp.max(scores, axis=2, keepdims=True)
    log_total = row_max + jnp.log(jnp.sum(jnp.exp(scores - row_max), axis=2, keepdims=True))
    weights = jnp.exp(scores - log_total)
    weights_low = weights.astype(jnp.bfloat16)
    attended = jnp.einsum(
        "hrs,shd->rhd", weights_low, all_values, preferred_element_type=jnp.float32
    ).astype(jnp.bfloat16)
    attended_flat = attended.reshape(row_count, heads_local * HD)
    mixed_out = lax.psum_scatter(
        jnp.dot(attended_flat, attn_out, preferred_element_type=jnp.float32),
        "tp",
        scatter_dimension=0,
        tiled=True,
    )
    grad_full = jnp.einsum(
        "nm,km->nk",
        lax.all_gather(grad_out, "tp", axis=0, tiled=True),
        attn_out,
        preferred_element_type=jnp.float32,
    )
    grad_att = grad_full.astype(jnp.bfloat16).reshape(row_count, heads_local, HD)
    row_delta = jnp.einsum("rhd,rhd->rh", grad_att, attended, preferred_element_type=jnp.float32)
    grad_weights = jnp.einsum(
        "rhd,shd->hrs", grad_att, all_values, preferred_element_type=jnp.float32
    )
    grad_scores = (weights * (grad_weights - row_delta.T[:, :, None]) * factor).astype(jnp.bfloat16)
    grad_queries = jnp.einsum(
        "hrs,shd->rhd", grad_scores, all_keys, preferred_element_type=jnp.float32
    )
    lse_rows = log_total[:, :, 0].T
    row_stats = (
        lax.all_gather(lse_rows, "ctx", axis=0, tiled=True),
        lax.all_gather(row_delta, "ctx", axis=0, tiled=True),
    )
    piece_q = lax.all_gather(queries, "ctx", axis=0, tiled=True)
    piece_g = lax.all_gather(grad_att, "ctx", axis=0, tiled=True)
    piece_len = piece_q.shape[0]
    piece_lse = row_stats[0]
    piece_delta = row_stats[1]
    piece_pos = jnp.arange(piece_len, dtype=jnp.int32)
    visible_part = query_pos[None, :] <= piece_pos[:, None]
    part_scores = (
        jnp.einsum("nhd,rhd->hnr", piece_q, keys_local, preferred_element_type=jnp.float32) * factor
    )
    part_weights = jnp.where(
        visible_part[None], jnp.exp(part_scores - piece_lse.T[:, :, None]), 0.0
    )
    part_grad = jnp.einsum(
        "nhd,rhd->hnr", piece_g, values_local, preferred_element_type=jnp.float32
    )
    part_ds = (part_weights * (part_grad - piece_delta.T[:, :, None]) * factor).astype(jnp.bfloat16)
    grad_k = jnp.einsum("hnr,nhd->rhd", part_ds, piece_q, preferred_element_type=jnp.float32)
    grad_v = jnp.einsum(
        "hnr,nhd->rhd",
        part_weights.astype(jnp.bfloat16),
        piece_g,
        preferred_element_type=jnp.float32,
    )
    grad_qkv = jnp.stack([grad_queries, grad_k, grad_v], axis=2)
    return (mixed_out, grad_qkv)


def solution(mesh):
    ctx, tp = mesh.shape["ctx"], mesh.shape["tp"]
    in_specs = (P("ctx", "tp", None, None), P(("ctx", "tp"), None), P("tp", None))
    out_specs = (P(("ctx", "tp"), None), P("ctx", "tp", None, None))

    def whole(qkv, grad_out, attn_out):
        split = qkv.shape[1] == ctx * tp and tp == 2 and ctx % 4 == 0
        step = jax.shard_map(
            by_head if split else by_rows,
            mesh=mesh,
            in_specs=in_specs,
            out_specs=out_specs,
            check_vma=False,
        )
        return step(qkv, grad_out, attn_out)

    return whole
```

```python
import functools
import math

import jax
import jax.numpy as jnp
from jax import lax
from jax.experimental import pallas as pl
from jax.experimental.pallas import tpu as pltpu
from jax.sharding import PartitionSpec as P


HD = 128
LOG2E = math.log2(math.e)
MIX_PARTS = 2
VMEM_LIMIT = 20 * 1024 * 1024


def dot_nt(a, b):
    return lax.dot_general(a, b, (((1,), (1,)), ((), ())), preferred_element_type=jnp.float32)


def dot_nn(a, b):
    return lax.dot_general(a, b, (((1,), (0,)), ((), ())), preferred_element_type=jnp.float32)


def rows_of(ref, start, count, *which):
    part = ref[(pl.ds(start, count), *which)]
    return part.reshape(count * part.shape[1], part.shape[2])


def swap_matrix(heads, chunk, me):
    size = heads * chunk
    row = lax.broadcasted_iota(jnp.int32, (size, size), 0)
    col = lax.broadcasted_iota(jnp.int32, (size, size), 1)
    want = (row % chunk) * heads + ((row // chunk) ^ me)
    return jnp.where(col == want, 1.0, 0.0).astype(jnp.bfloat16)


def split_kernel(me_ref, x_ref, *out_refs):
    rows, three, heads, _ = x_ref.shape
    chunk = 16
    order = swap_matrix(heads, chunk, me_ref[0])
    for b in range(rows // chunk):
        span = slice(b * chunk, (b + 1) * chunk)
        for c in range(three):
            y = dot_nn(order, x_ref[span, c].reshape(chunk * heads, HD)).astype(jnp.bfloat16)
            y = y.reshape(heads, chunk, HD)
            for k in range(heads):
                out_refs[k][c, span] = y[k]


def join_kernel(x_ref, out_ref):
    heads, three, _, _ = x_ref.shape
    chunk = out_ref.shape[0]
    order = swap_matrix(chunk, heads, 0)
    span = pl.ds(pl.program_id(0) * chunk, chunk)
    for c in range(three):
        x = x_ref[:, c, span].reshape(chunk * heads, HD)
        out_ref[:, c] = dot_nn(order, x).reshape(chunk, heads, HD)


def back_kernel(turn_ref, own_ref, other_ref, w_ref, out_ref):
    half = own_ref.shape[0]
    turn = turn_ref[0]
    for x_ref, place in ((own_ref, turn), (other_ref, 1 - turn)):
        y = dot_nt(x_ref[...], w_ref[...]).astype(jnp.bfloat16)
        for h in range(out_ref.shape[0]):
            out_ref[h, pl.ds(pl.multiple_of(place * half, half), half)] = y[:, h * HD : (h + 1) * HD]


def forward_kernel(step, me_ref, *refs):
    *parts, qkv_ref, att_ref, lse_ref, v_t, s_buf = refs
    me = me_ref[0]
    for k, part in enumerate(parts):
        qkv_ref[me ^ k] = part[...]
    chunks, _, unit, _ = qkv_ref.shape
    per = step // unit
    blocks = chunks // per
    scale = LOG2E / math.sqrt(HD)
    for b in range(blocks):
        v_t[b] = rows_of(qkv_ref, b * per, per, 2).T

    def query_block(i, _):
        q = rows_of(qkv_ref, i * per, per, 0)

        def scores(j, top):
            s = dot_nt(rows_of(qkv_ref, j * per, per, 1), q)
            s_buf[j] = s
            return jnp.maximum(top, jnp.max(s, axis=0, keepdims=True))

        top = lax.fori_loop(0, i, scores, jnp.full((1, step), -jnp.inf, jnp.float32))
        s = dot_nt(rows_of(qkv_ref, i * per, per, 1), q)
        key = lax.broadcasted_iota(jnp.int32, s.shape, 0)
        query = lax.broadcasted_iota(jnp.int32, s.shape, 1)
        s = jnp.where(key <= query, s, -jnp.inf)
        s_buf[i] = s
        top = jnp.maximum(top, jnp.max(s, axis=0, keepdims=True))

        def exps(j, total):
            p = jnp.exp2((s_buf[j] - top) * scale)
            s_buf[j] = p
            return total + jnp.sum(p, axis=0, keepdims=True)

        total = lax.fori_loop(0, i + 1, exps, jnp.zeros((1, step), jnp.float32))
        inverse = 1.0 / total

        def mix(j, acc):
            return acc + dot_nn(v_t[j], (s_buf[j] * inverse).astype(jnp.bfloat16))

        acc = lax.fori_loop(0, i + 1, mix, jnp.zeros((HD, step), jnp.float32))
        att_ref[pl.ds(i * per, per)] = acc.T.astype(jnp.bfloat16).reshape(per, unit, HD)
        lse_ref[i] = top * scale + jnp.log2(total)
        return 0

    lax.fori_loop(0, blocks, query_block, 0)


def backward_kernel(step, qkv_ref, g_ref, att_ref, lse_ref, out_ref, k_t, dq_t, delta):
    chunks, _, unit, _ = qkv_ref.shape
    per = step // unit
    blocks = chunks // per
    factor = 1.0 / math.sqrt(HD)
    for b in range(blocks):
        k_t[b] = rows_of(qkv_ref, b * per, per, 1).T
        prod = rows_of(g_ref, b * per, per).astype(jnp.float32)
        prod = prod * rows_of(att_ref, b * per, per).astype(jnp.float32)
        delta[b] = jnp.sum(prod.T, axis=0, keepdims=True)

    def key_block(j, _):
        k = rows_of(qkv_ref, j * per, per, 1)
        v = rows_of(qkv_ref, j * per, per, 2)
        kt = k_t[j]

        def pair(i, diagonal):
            q = rows_of(qkv_ref, i * per, per, 0)
            g = rows_of(g_ref, i * per, per)
            w = jnp.exp2(dot_nt(k, q) * (factor * LOG2E) - lse_ref[i])
            if diagonal:
                key = lax.broadcasted_iota(jnp.int32, w.shape, 0)
                query = lax.broadcasted_iota(jnp.int32, w.shape, 1)
                w = jnp.where(key <= query, w, 0.0)
            ds = (w * (dot_nt(v, g) - delta[i]) * factor).astype(jnp.bfloat16)
            dv = dot_nn(w.astype(jnp.bfloat16), g)
            dk = dot_nn(ds, q)
            return dk, dv, dot_nn(kt, ds)

        dk, dv, part = pair(j, True)

        @pl.when(j == 0)
        def _():
            dq_t[j] = part

        @pl.when(j > 0)
        def _():
            dq_t[j] = dq_t[j] + part

        def later(i, carry):
            dk, dv, part = pair(i, False)

            @pl.when(j == 0)
            def _():
                dq_t[i] = part

            @pl.when(j > 0)
            def _():
                dq_t[i] = dq_t[i] + part

            return carry[0] + dk, carry[1] + dv

        dk, dv = lax.fori_loop(j + 1, blocks, later, (dk, dv))
        spot = pl.ds(j * per, per)
        out_ref[spot, 1] = dk.astype(jnp.bfloat16).reshape(per, unit, HD)
        out_ref[spot, 2] = dv.astype(jnp.bfloat16).reshape(per, unit, HD)
        return 0

    lax.fori_loop(0, blocks, key_block, 0)
    for b in range(blocks):
        out_ref[pl.ds(b * per, per), 0] = dq_t[b].T.astype(jnp.bfloat16).reshape(per, unit, HD)


def in_vmem(count):
    return [pl.BlockSpec(memory_space=pltpu.VMEM)] * count


def in_smem():
    return pl.BlockSpec(memory_space=pltpu.SMEM)


def split_heads(me, qkv):
    rows, heads = qkv.shape[:2]
    return pl.pallas_call(
        split_kernel,
        out_shape=[jax.ShapeDtypeStruct((3, rows, HD), jnp.bfloat16)] * heads,
        in_specs=[in_smem(), *in_vmem(1)],
        out_specs=in_vmem(heads),
        compiler_params=pltpu.CompilerParams(vmem_limit_bytes=VMEM_LIMIT),
        name="split_heads",
    )(me, jnp.transpose(qkv, (0, 2, 1, 3)))


def join_heads(grads):
    heads, three, rows, _ = grads.shape
    chunk = 16
    out = pl.pallas_call(
        join_kernel,
        grid=(rows // chunk,),
        out_shape=jax.ShapeDtypeStruct((rows, three, heads, HD), jnp.float32),
        in_specs=in_vmem(1),
        out_specs=pl.BlockSpec((chunk, three, heads, HD), lambda b: (b, 0, 0, 0)),
        compiler_params=pltpu.CompilerParams(vmem_limit_bytes=VMEM_LIMIT),
        name="join_heads",
    )(grads)
    return jnp.transpose(out, (0, 2, 1, 3))


def project_back(turn, own, other, weights):
    half, width = own.shape
    heads = weights.shape[0] // HD
    group = 2
    return pl.pallas_call(
        back_kernel,
        grid=(heads // group,),
        out_shape=jax.ShapeDtypeStruct((heads, 2 * half, HD), jnp.bfloat16),
        in_specs=[
            in_smem(),
            *in_vmem(2),
            pl.BlockSpec((group * HD, width), lambda b: (b, 0)),
        ],
        out_specs=pl.BlockSpec((group, 2 * half, HD), lambda b: (b, 0, 0)),
        compiler_params=pltpu.CompilerParams(vmem_limit_bytes=VMEM_LIMIT),
        cost_estimate=pl.CostEstimate(
            flops=4 * half * width * heads * HD,
            transcendentals=0,
            bytes_accessed=2 * width * heads * HD,
        ),
        name="project_back",
    )(turn, own, other, weights)


def attend(me, parts, step):
    chunks = len(parts)
    unit = parts[0].shape[1]
    length = chunks * unit
    blocks = length // step
    area = length * length // 2
    return pl.pallas_call(
        functools.partial(forward_kernel, step),
        out_shape=(
            jax.ShapeDtypeStruct((chunks, 3, unit, HD), jnp.bfloat16),
            jax.ShapeDtypeStruct((chunks, unit, HD), jnp.bfloat16),
            jax.ShapeDtypeStruct((blocks, 1, step), jnp.float32),
        ),
        in_specs=[in_smem(), *in_vmem(chunks)],
        out_specs=tuple(in_vmem(3)),
        scratch_shapes=[
            pltpu.VMEM((blocks, HD, step), jnp.bfloat16),
            pltpu.VMEM((blocks, step, step), jnp.float32),
        ],
        compiler_params=pltpu.CompilerParams(vmem_limit_bytes=VMEM_LIMIT),
        cost_estimate=pl.CostEstimate(
            flops=4 * area * HD, transcendentals=area, bytes_accessed=8 * length * HD
        ),
        name="attend",
    )(me, *parts)


def attend_grad(qkv, g, att, lse, step):
    chunks, _, unit, _ = qkv.shape
    length = chunks * unit
    blocks = length // step
    area = length * length // 2
    return pl.pallas_call(
        functools.partial(backward_kernel, step),
        out_shape=jax.ShapeDtypeStruct((chunks, 3, unit, HD), jnp.bfloat16),
        in_specs=in_vmem(4),
        out_specs=in_vmem(1)[0],
        scratch_shapes=[
            pltpu.VMEM((blocks, HD, step), jnp.bfloat16),
            pltpu.VMEM((blocks, HD, step), jnp.float32),
            pltpu.VMEM((blocks, 1, step), jnp.float32),
        ],
        compiler_params=pltpu.CompilerParams(vmem_limit_bytes=VMEM_LIMIT),
        cost_estimate=pl.CostEstimate(
            flops=10 * area * HD, transcendentals=area, bytes_accessed=16 * length * HD
        ),
        name="attend_grad",
    )(qkv, g, att, lse)


def by_head(qkv, grad_out, attn_out):
    rows, heads = qkv.shape[:2]
    half = grad_out.shape[0]
    width = attn_out.shape[1]
    step = 512 if (rows * heads) % 512 == 0 else rows
    swap = [(0, 1), (1, 0)]
    turn = lax.axis_index("tp")
    me = lax.axis_index("ctx").reshape(1)
    weights = attn_out.reshape(heads, HD, width)

    def spread(x):
        return lax.all_to_all(x, "ctx", 0, 0, tiled=True)

    other_out = lax.ppermute(grad_out, "tp", swap)
    parts = list(split_heads(me, qkv))
    for k in range(1, heads):
        parts[k] = lax.ppermute(parts[k], "ctx", [(i, i ^ k) for i in range(heads)])
    g = project_back(turn.reshape(1), grad_out, other_out, attn_out)
    g = spread(g)
    mine, att, lse = attend(me, parts, step)
    local = spread(att)
    grads = attend_grad(mine, g, att, lse, step)
    grads = spread(grads)
    pieces = []
    part = width // MIX_PARTS
    for c in range(MIX_PARTS):
        mixed = jnp.einsum(
            "hrd,hdm->rm",
            local,
            weights[:, :, c * part : (c + 1) * part],
            preferred_element_type=jnp.float32,
        )
        sent = lax.dynamic_slice_in_dim(mixed, (1 - turn) * half, half, 0)
        kept = lax.dynamic_slice_in_dim(mixed, turn * half, half, 0)
        got = lax.ppermute(sent.astype(jnp.bfloat16), "tp", swap)
        pieces.append(kept + got.astype(jnp.float32))
    mixed_out = jnp.concatenate(pieces, axis=1)
    return mixed_out, join_heads(grads)


def by_rows(qkv, grad_out, attn_out):
    row_count, heads_local = (qkv.shape[0], qkv.shape[1])
    factor = 1.0 / math.sqrt(HD)
    queries = qkv[:, :, 0]
    keys_local = qkv[:, :, 1]
    values_local = qkv[:, :, 2]
    all_keys, all_values = (
        lax.all_gather(keys_local, "ctx", axis=0, tiled=True),
        lax.all_gather(values_local, "ctx", axis=0, tiled=True),
    )
    seq_len = all_keys.shape[0]
    offset = lax.axis_index("ctx") * row_count
    query_pos = offset + jnp.arange(row_count, dtype=jnp.int32)
    key_pos = jnp.arange(seq_len, dtype=jnp.int32)
    visible = key_pos[None, :] <= query_pos[:, None]
    scores = (
        jnp.einsum("rhd,shd->hrs", queries, all_keys, preferred_element_type=jnp.float32) * factor
    )
    scores = jnp.where(visible[None], scores, -jnp.inf)
    row_max = jnp.max(scores, axis=2, keepdims=True)
    log_total = row_max + jnp.log(jnp.sum(jnp.exp(scores - row_max), axis=2, keepdims=True))
    weights = jnp.exp(scores - log_total)
    weights_low = weights.astype(jnp.bfloat16)
    attended = jnp.einsum(
        "hrs,shd->rhd", weights_low, all_values, preferred_element_type=jnp.float32
    ).astype(jnp.bfloat16)
    attended_flat = attended.reshape(row_count, heads_local * HD)
    mixed_out = lax.psum_scatter(
        jnp.dot(attended_flat, attn_out, preferred_element_type=jnp.float32),
        "tp",
        scatter_dimension=0,
        tiled=True,
    )
    grad_full = jnp.einsum(
        "nm,km->nk",
        lax.all_gather(grad_out, "tp", axis=0, tiled=True),
        attn_out,
        preferred_element_type=jnp.float32,
    )
    grad_att = grad_full.astype(jnp.bfloat16).reshape(row_count, heads_local, HD)
    row_delta = jnp.einsum("rhd,rhd->rh", grad_att, attended, preferred_element_type=jnp.float32)
    grad_weights = jnp.einsum(
        "rhd,shd->hrs", grad_att, all_values, preferred_element_type=jnp.float32
    )
    grad_scores = (weights * (grad_weights - row_delta.T[:, :, None]) * factor).astype(jnp.bfloat16)
    grad_queries = jnp.einsum(
        "hrs,shd->rhd", grad_scores, all_keys, preferred_element_type=jnp.float32
    )
    lse_rows = log_total[:, :, 0].T
    row_stats = (
        lax.all_gather(lse_rows, "ctx", axis=0, tiled=True),
        lax.all_gather(row_delta, "ctx", axis=0, tiled=True),
    )
    piece_q = lax.all_gather(queries, "ctx", axis=0, tiled=True)
    piece_g = lax.all_gather(grad_att, "ctx", axis=0, tiled=True)
    piece_len = piece_q.shape[0]
    piece_lse = row_stats[0]
    piece_delta = row_stats[1]
    piece_pos = jnp.arange(piece_len, dtype=jnp.int32)
    visible_part = query_pos[None, :] <= piece_pos[:, None]
    part_scores = (
        jnp.einsum("nhd,rhd->hnr", piece_q, keys_local, preferred_element_type=jnp.float32) * factor
    )
    part_weights = jnp.where(
        visible_part[None], jnp.exp(part_scores - piece_lse.T[:, :, None]), 0.0
    )
    part_grad = jnp.einsum(
        "nhd,rhd->hnr", piece_g, values_local, preferred_element_type=jnp.float32
    )
    part_ds = (part_weights * (part_grad - piece_delta.T[:, :, None]) * factor).astype(jnp.bfloat16)
    grad_k = jnp.einsum("hnr,nhd->rhd", part_ds, piece_q, preferred_element_type=jnp.float32)
    grad_v = jnp.einsum(
        "hnr,nhd->rhd",
        part_weights.astype(jnp.bfloat16),
        piece_g,
        preferred_element_type=jnp.float32,
    )
    grad_qkv = jnp.stack([grad_queries, grad_k, grad_v], axis=2)
    return (mixed_out, grad_qkv)


def solution(mesh):
    ctx, tp = mesh.shape["ctx"], mesh.shape["tp"]
    in_specs = (P("ctx", "tp", None, None), P(("ctx", "tp"), None), P("tp", None))
    out_specs = (P(("ctx", "tp"), None), P("ctx", "tp", None, None))

    def whole(qkv, grad_out, attn_out):
        split = qkv.shape[1] == ctx * tp and tp == 2 and ctx & (ctx - 1) == 0
        step = jax.shard_map(
            by_head if split else by_rows,
            mesh=mesh,
            in_specs=in_specs,
            out_specs=out_specs,
            check_vma=False,
        )
        return step(qkv, grad_out, attn_out)

    return whole
```

```python
import functools
import math

import jax
import jax.numpy as jnp
from jax import lax
from jax.experimental import pallas as pl
from jax.experimental.pallas import tpu as pltpu
from jax.sharding import PartitionSpec as P


HD = 128
LOG2E = math.log2(math.e)
MIX_PARTS = 2
VMEM_LIMIT = 20 * 1024 * 1024


def dot_nt(a, b):
    return lax.dot_general(a, b, (((1,), (1,)), ((), ())), preferred_element_type=jnp.float32)


def dot_nn(a, b):
    return lax.dot_general(a, b, (((1,), (0,)), ((), ())), preferred_element_type=jnp.float32)


def rows_of(ref, start, count, *which):
    part = ref[(pl.ds(start, count), *which)]
    return part.reshape(count * part.shape[1], part.shape[2])


CHUNK = 16


def py_loop(lo, hi, body, carry):
    for i in range(lo, hi):
        carry = body(i, carry)
    return carry


def swap_matrix(heads, chunk, me):
    size = heads * chunk
    row = lax.broadcasted_iota(jnp.int32, (size, size), 0)
    col = lax.broadcasted_iota(jnp.int32, (size, size), 1)
    want = lax.rem(row, chunk) * heads + (lax.div(row, chunk) ^ me)
    return jnp.where(col == want, 1.0, 0.0).astype(jnp.bfloat16)


def split_kernel(me_ref, x_ref, *refs):
    *out_refs, order = refs
    rows, three, heads, _ = x_ref.shape
    step = pl.program_id(0)

    @pl.when(step == 0)
    def _():
        order[...] = swap_matrix(heads, CHUNK, me_ref[0])

    for b in range(rows // CHUNK):
        span = pl.ds(pl.multiple_of(step * rows + b * CHUNK, CHUNK), CHUNK)
        for c in range(three):
            x = x_ref[b * CHUNK : (b + 1) * CHUNK, c].reshape(CHUNK * heads, HD)
            y = dot_nn(order[...], x).astype(jnp.bfloat16).reshape(heads, CHUNK, HD)
            for k in range(heads):
                out_refs[k][c, span] = y[k]


def join_kernel(x_ref, out_ref, order):
    heads, three, _, _ = x_ref.shape
    rows = out_ref.shape[0]
    step = pl.program_id(0)

    @pl.when(step == 0)
    def _():
        order[...] = swap_matrix(CHUNK, heads, 0)

    for b in range(rows // CHUNK):
        span = pl.ds(pl.multiple_of(step * rows + b * CHUNK, CHUNK), CHUNK)
        for c in range(three):
            x = x_ref[:, c, span].reshape(CHUNK * heads, HD)
            out_ref[b * CHUNK : (b + 1) * CHUNK, c] = dot_nn(order[...], x).reshape(CHUNK, heads, HD)


def back_kernel(turn_ref, own_ref, other_ref, w_ref, out_ref, x_buf):
    half = own_ref.shape[0]

    @pl.when(pl.program_id(0) == 0)
    def _():
        for x_ref, place in ((own_ref, turn_ref[0]), (other_ref, 1 - turn_ref[0])):
            x_buf[pl.ds(pl.multiple_of(place * half, half), half)] = x_ref[...]

    y = dot_nt(x_buf[...], w_ref[...]).astype(jnp.bfloat16)
    for h in range(out_ref.shape[0]):
        out_ref[h] = y[:, h * HD : (h + 1) * HD]


def forward_kernel(step, me_ref, *refs):
    *parts, qkv_ref, att_ref, lse_ref, v_t, s_buf = refs
    me = me_ref[0]
    for k, part in enumerate(parts):
        qkv_ref[me ^ k] = part[...]
    chunks, _, unit, _ = qkv_ref.shape
    per = step // unit
    blocks = chunks // per
    scale = LOG2E / math.sqrt(HD)
    for b in range(blocks):
        v_t[b] = rows_of(qkv_ref, b * per, per, 2).T
    for i in range(blocks):
        q = rows_of(qkv_ref, i * per, per, 0)
        top = None
        for j in range(i + 1):
            s = dot_nt(rows_of(qkv_ref, j * per, per, 1), q)
            if j == i:
                key = lax.broadcasted_iota(jnp.int32, s.shape, 0)
                query = lax.broadcasted_iota(jnp.int32, s.shape, 1)
                s = jnp.where(key <= query, s, -jnp.inf)
            s_buf[i % 2, j] = s
            peak = jnp.max(s, axis=0, keepdims=True)
            top = peak if top is None else jnp.maximum(top, peak)
        total = jnp.zeros((1, step), jnp.float32)
        for j in range(i + 1):
            p = jnp.exp2((s_buf[i % 2, j] - top) * scale)
            s_buf[i % 2, j] = p
            total = total + jnp.sum(p, axis=0, keepdims=True)
        inverse = 1.0 / total
        acc = jnp.zeros((HD, step), jnp.float32)
        for j in range(i + 1):
            acc = acc + dot_nn(v_t[j], (s_buf[i % 2, j] * inverse).astype(jnp.bfloat16))
        att_ref[i * per : (i + 1) * per] = acc.T.astype(jnp.bfloat16).reshape(per, unit, HD)
        lse_ref[i] = top * scale + jnp.log2(total)


def backward_kernel(step, qkv_ref, g_ref, att_ref, lse_ref, out_ref, k_t, dq_t, delta):
    chunks, _, unit, _ = qkv_ref.shape
    per = step // unit
    blocks = chunks // per
    half = step // 2
    factor = 1.0 / math.sqrt(HD)
    for b in range(blocks):
        k_t[b] = rows_of(qkv_ref, b * per, per, 1).T
        prod = rows_of(g_ref, b * per, per).astype(jnp.float32)
        prod = prod * rows_of(att_ref, b * per, per).astype(jnp.float32)
        delta[b] = jnp.sum(prod.T, axis=0, keepdims=True)
        dq_t[b] = jnp.zeros((HD, step), jnp.float32)

    def pair(k, v, kt, q, g, lse, dlt, masked):
        w = jnp.exp2(dot_nt(k, q) * (factor * LOG2E) - lse)
        if masked:
            key = lax.broadcasted_iota(jnp.int32, w.shape, 0)
            query = lax.broadcasted_iota(jnp.int32, w.shape, 1)
            w = jnp.where(key <= query, w, 0.0)
        ds = (w * (dot_nt(v, g) - dlt) * factor).astype(jnp.bfloat16)
        dv = dot_nn(w.astype(jnp.bfloat16), g)
        return dot_nn(ds, q), dv, dot_nn(kt, ds)

    def key_block(j, _):
        k = rows_of(qkv_ref, j * per, per, 1)
        v = rows_of(qkv_ref, j * per, per, 2)
        kt = k_t[j]
        q = rows_of(qkv_ref, j * per, per, 0)
        g = rows_of(g_ref, j * per, per)
        lse, dlt = lse_ref[j], delta[j]
        dk0, dv0, part0 = pair(k[:half], v[:half], kt[:, :half], q, g, lse, dlt, True)
        dk1, dv1, part1 = pair(
            k[half:], v[half:], kt[:, half:], q[half:], g[half:], lse[:, half:], dlt[:, half:], True
        )
        dq_t[j, :, :half] += part0[:, :half]
        dq_t[j, :, half:] += part0[:, half:] + part1

        def later(i, carry):
            dk, dv, part = pair(
                k, v, kt, rows_of(qkv_ref, i * per, per, 0), rows_of(g_ref, i * per, per),
                lse_ref[i], delta[i], False,
            )
            dq_t[i] += part
            return carry[0] + dk, carry[1] + dv

        start = jnp.concatenate([dk0, dk1]), jnp.concatenate([dv0, dv1])
        dk, dv = py_loop(j + 1, blocks, later, start)
        spot = pl.ds(j * per, per)
        out_ref[spot, 1] = dk.astype(jnp.bfloat16).reshape(per, unit, HD)
        out_ref[spot, 2] = dv.astype(jnp.bfloat16).reshape(per, unit, HD)
        return 0

    py_loop(0, blocks, key_block, 0)
    for b in range(blocks):
        out_ref[pl.ds(b * per, per), 0] = dq_t[b].T.astype(jnp.bfloat16).reshape(per, unit, HD)


def in_vmem(count):
    return [pl.BlockSpec(memory_space=pltpu.VMEM)] * count


def in_smem():
    return pl.BlockSpec(memory_space=pltpu.SMEM)


def split_heads(me, qkv):
    rows, heads = qkv.shape[:2]
    part = 4 * CHUNK
    return pl.pallas_call(
        split_kernel,
        grid=(rows // part,),
        out_shape=[jax.ShapeDtypeStruct((3, rows, HD), jnp.bfloat16)] * heads,
        in_specs=[in_smem(), pl.BlockSpec((part, 3, heads, HD), lambda b: (b, 0, 0, 0))],
        out_specs=in_vmem(heads),
        scratch_shapes=[pltpu.VMEM((CHUNK * heads, CHUNK * heads), jnp.bfloat16)],
        compiler_params=pltpu.CompilerParams(vmem_limit_bytes=VMEM_LIMIT),
        name="split_heads",
    )(me, jnp.transpose(qkv, (0, 2, 1, 3)))


def join_heads(grads):
    heads, three, rows, _ = grads.shape
    part = 2 * CHUNK
    out = pl.pallas_call(
        join_kernel,
        grid=(rows // part,),
        out_shape=jax.ShapeDtypeStruct((rows, three, heads, HD), jnp.float32),
        in_specs=in_vmem(1),
        out_specs=pl.BlockSpec((part, three, heads, HD), lambda b: (b, 0, 0, 0)),
        scratch_shapes=[pltpu.VMEM((CHUNK * heads, CHUNK * heads), jnp.bfloat16)],
        compiler_params=pltpu.CompilerParams(vmem_limit_bytes=VMEM_LIMIT),
        name="join_heads",
    )(grads)
    return jnp.transpose(out, (0, 2, 1, 3))


def project_back(turn, own, other, weights):
    half, width = own.shape
    heads = weights.shape[0] // HD
    group = 2
    return pl.pallas_call(
        back_kernel,
        grid=(heads // group,),
        out_shape=jax.ShapeDtypeStruct((heads, 2 * half, HD), jnp.bfloat16),
        in_specs=[
            in_smem(),
            *in_vmem(2),
            pl.BlockSpec((group * HD, width), lambda b: (b, 0)),
        ],
        out_specs=pl.BlockSpec((group, 2 * half, HD), lambda b: (b, 0, 0)),
        scratch_shapes=[pltpu.VMEM((2 * half, width), jnp.bfloat16)],
        compiler_params=pltpu.CompilerParams(vmem_limit_bytes=VMEM_LIMIT),
        cost_estimate=pl.CostEstimate(
            flops=4 * half * width * heads * HD,
            transcendentals=0,
            bytes_accessed=2 * width * heads * HD,
        ),
        name="project_back",
    )(turn, own, other, weights)


def attend(me, parts, step):
    chunks = len(parts)
    unit = parts[0].shape[1]
    length = chunks * unit
    blocks = length // step
    area = length * length // 2
    return pl.pallas_call(
        functools.partial(forward_kernel, step),
        out_shape=(
            jax.ShapeDtypeStruct((chunks, 3, unit, HD), jnp.bfloat16),
            jax.ShapeDtypeStruct((chunks, unit, HD), jnp.bfloat16),
            jax.ShapeDtypeStruct((blocks, 1, step), jnp.float32),
        ),
        in_specs=[in_smem(), *in_vmem(chunks)],
        out_specs=tuple(in_vmem(3)),
        scratch_shapes=[
            pltpu.VMEM((blocks, HD, step), jnp.bfloat16),
            pltpu.VMEM((2, blocks, step, step), jnp.float32),
        ],
        compiler_params=pltpu.CompilerParams(vmem_limit_bytes=VMEM_LIMIT),
        cost_estimate=pl.CostEstimate(
            flops=4 * area * HD, transcendentals=area, bytes_accessed=8 * length * HD
        ),
        name="attend",
    )(me, *parts)


def attend_grad(qkv, g, att, lse, step):
    chunks, _, unit, _ = qkv.shape
    length = chunks * unit
    blocks = length // step
    area = length * length // 2
    return pl.pallas_call(
        functools.partial(backward_kernel, step),
        out_shape=jax.ShapeDtypeStruct((chunks, 3, unit, HD), jnp.bfloat16),
        in_specs=in_vmem(4),
        out_specs=in_vmem(1)[0],
        scratch_shapes=[
            pltpu.VMEM((blocks, HD, step), jnp.bfloat16),
            pltpu.VMEM((blocks, HD, step), jnp.float32),
            pltpu.VMEM((blocks, 1, step), jnp.float32),
        ],
        compiler_params=pltpu.CompilerParams(vmem_limit_bytes=VMEM_LIMIT),
        cost_estimate=pl.CostEstimate(
            flops=10 * area * HD, transcendentals=area, bytes_accessed=16 * length * HD
        ),
        name="attend_grad",
    )(qkv, g, att, lse)


def by_head(qkv, grad_out, attn_out):
    rows, heads = qkv.shape[:2]
    half = grad_out.shape[0]
    width = attn_out.shape[1]
    step = 512 if (rows * heads) % 512 == 0 else rows
    swap = [(0, 1), (1, 0)]
    turn = lax.axis_index("tp")
    me = lax.axis_index("ctx").reshape(1)
    weights = attn_out.reshape(heads, HD, width)

    def spread(x):
        return lax.all_to_all(x, "ctx", 0, 0, tiled=True)

    other_out = lax.ppermute(grad_out, "tp", swap)
    parts = list(split_heads(me, qkv))
    for k in range(1, heads):
        parts[k] = lax.ppermute(parts[k], "ctx", [(i, i ^ k) for i in range(heads)])
    g = project_back(turn.reshape(1), grad_out, other_out, attn_out)
    g = spread(g)
    mine, att, lse = attend(me, parts, step)
    local = spread(att)
    grads = attend_grad(mine, g, att, lse, step)
    grads = spread(grads)
    pieces = []
    part = width // MIX_PARTS
    for c in range(MIX_PARTS):
        mixed = jnp.einsum(
            "hrd,hdm->rm",
            local,
            weights[:, :, c * part : (c + 1) * part],
            preferred_element_type=jnp.float32,
        )
        sent = lax.dynamic_slice_in_dim(mixed, (1 - turn) * half, half, 0)
        kept = lax.dynamic_slice_in_dim(mixed, turn * half, half, 0)
        got = lax.ppermute(sent.astype(jnp.bfloat16), "tp", swap)
        pieces.append(kept + got.astype(jnp.float32))
    mixed_out = jnp.concatenate(pieces, axis=1)
    return mixed_out, join_heads(grads)


def by_rows(qkv, grad_out, attn_out):
    row_count, heads_local = (qkv.shape[0], qkv.shape[1])
    factor = 1.0 / math.sqrt(HD)
    queries = qkv[:, :, 0]
    keys_local = qkv[:, :, 1]
    values_local = qkv[:, :, 2]
    all_keys, all_values = (
        lax.all_gather(keys_local, "ctx", axis=0, tiled=True),
        lax.all_gather(values_local, "ctx", axis=0, tiled=True),
    )
    seq_len = all_keys.shape[0]
    offset = lax.axis_index("ctx") * row_count
    query_pos = offset + jnp.arange(row_count, dtype=jnp.int32)
    key_pos = jnp.arange(seq_len, dtype=jnp.int32)
    visible = key_pos[None, :] <= query_pos[:, None]
    scores = (
        jnp.einsum("rhd,shd->hrs", queries, all_keys, preferred_element_type=jnp.float32) * factor
    )
    scores = jnp.where(visible[None], scores, -jnp.inf)
    row_max = jnp.max(scores, axis=2, keepdims=True)
    log_total = row_max + jnp.log(jnp.sum(jnp.exp(scores - row_max), axis=2, keepdims=True))
    weights = jnp.exp(scores - log_total)
    weights_low = weights.astype(jnp.bfloat16)
    attended = jnp.einsum(
        "hrs,shd->rhd", weights_low, all_values, preferred_element_type=jnp.float32
    ).astype(jnp.bfloat16)
    attended_flat = attended.reshape(row_count, heads_local * HD)
    mixed_out = lax.psum_scatter(
        jnp.dot(attended_flat, attn_out, preferred_element_type=jnp.float32),
        "tp",
        scatter_dimension=0,
        tiled=True,
    )
    grad_full = jnp.einsum(
        "nm,km->nk",
        lax.all_gather(grad_out, "tp", axis=0, tiled=True),
        attn_out,
        preferred_element_type=jnp.float32,
    )
    grad_att = grad_full.astype(jnp.bfloat16).reshape(row_count, heads_local, HD)
    row_delta = jnp.einsum("rhd,rhd->rh", grad_att, attended, preferred_element_type=jnp.float32)
    grad_weights = jnp.einsum(
        "rhd,shd->hrs", grad_att, all_values, preferred_element_type=jnp.float32
    )
    grad_scores = (weights * (grad_weights - row_delta.T[:, :, None]) * factor).astype(jnp.bfloat16)
    grad_queries = jnp.einsum(
        "hrs,shd->rhd", grad_scores, all_keys, preferred_element_type=jnp.float32
    )
    lse_rows = log_total[:, :, 0].T
    row_stats = (
        lax.all_gather(lse_rows, "ctx", axis=0, tiled=True),
        lax.all_gather(row_delta, "ctx", axis=0, tiled=True),
    )
    piece_q = lax.all_gather(queries, "ctx", axis=0, tiled=True)
    piece_g = lax.all_gather(grad_att, "ctx", axis=0, tiled=True)
    piece_len = piece_q.shape[0]
    piece_lse = row_stats[0]
    piece_delta = row_stats[1]
    piece_pos = jnp.arange(piece_len, dtype=jnp.int32)
    visible_part = query_pos[None, :] <= piece_pos[:, None]
    part_scores = (
        jnp.einsum("nhd,rhd->hnr", piece_q, keys_local, preferred_element_type=jnp.float32) * factor
    )
    part_weights = jnp.where(
        visible_part[None], jnp.exp(part_scores - piece_lse.T[:, :, None]), 0.0
    )
    part_grad = jnp.einsum(
        "nhd,rhd->hnr", piece_g, values_local, preferred_element_type=jnp.float32
    )
    part_ds = (part_weights * (part_grad - piece_delta.T[:, :, None]) * factor).astype(jnp.bfloat16)
    grad_k = jnp.einsum("hnr,nhd->rhd", part_ds, piece_q, preferred_element_type=jnp.float32)
    grad_v = jnp.einsum(
        "hnr,nhd->rhd",
        part_weights.astype(jnp.bfloat16),
        piece_g,
        preferred_element_type=jnp.float32,
    )
    grad_qkv = jnp.stack([grad_queries, grad_k, grad_v], axis=2)
    return (mixed_out, grad_qkv)


def solution(mesh):
    ctx, tp = mesh.shape["ctx"], mesh.shape["tp"]
    in_specs = (P("ctx", "tp", None, None), P(("ctx", "tp"), None), P("tp", None))
    out_specs = (P(("ctx", "tp"), None), P("ctx", "tp", None, None))

    def whole(qkv, grad_out, attn_out):
        split = qkv.shape[1] == ctx * tp and tp == 2 and ctx & (ctx - 1) == 0
        step = jax.shard_map(
            by_head if split else by_rows,
            mesh=mesh,
            in_specs=in_specs,
            out_specs=out_specs,
            check_vma=False,
        )
        return step(qkv, grad_out, attn_out)

    return whole
```

```python
import functools
import math

import jax
import jax.numpy as jnp
from jax import lax
from jax.experimental import pallas as pl
from jax.experimental.pallas import tpu as pltpu
from jax.sharding import PartitionSpec as P


HD = 128
LOG2E = math.log2(math.e)
MIX_PARTS = 4
VMEM_LIMIT = 20 * 1024 * 1024


def dot_nt(a, b):
    return lax.dot_general(a, b, (((1,), (1,)), ((), ())), preferred_element_type=jnp.float32)


def dot_nn(a, b):
    return lax.dot_general(a, b, (((1,), (0,)), ((), ())), preferred_element_type=jnp.float32)


def rows_of(ref, start, count, *which):
    part = ref[(pl.ds(start, count), *which)]
    return part.reshape(count * part.shape[1], part.shape[2])


CHUNK = 16
PLANE = 4


def py_loop(lo, hi, body, carry):
    for i in range(lo, hi):
        carry = body(i, carry)
    return carry


def swap_matrix(heads, chunk, me):
    size = heads * chunk
    row = lax.broadcasted_iota(jnp.int32, (size, size), 0)
    col = lax.broadcasted_iota(jnp.int32, (size, size), 1)
    want = lax.rem(row, chunk) * heads + (lax.div(row, chunk) ^ me)
    return jnp.where(col == want, 1.0, 0.0).astype(jnp.bfloat16)


def split_kernel(me_ref, x_ref, *refs):
    *out_refs, order = refs
    rows, three, heads, _ = x_ref.shape
    step = pl.program_id(0)

    @pl.when(step == 0)
    def _():
        order[...] = swap_matrix(heads, CHUNK, me_ref[0])

    for b in range(rows // CHUNK):
        span = pl.ds(pl.multiple_of(step * rows + b * CHUNK, CHUNK), CHUNK)
        for c in range(three):
            x = x_ref[b * CHUNK : (b + 1) * CHUNK, c].reshape(CHUNK * heads, HD)
            y = dot_nn(order[...], x).astype(jnp.bfloat16).reshape(heads, CHUNK, HD)
            for k in range(heads):
                out_refs[k][c, span] = y[k]


def join_kernel(x_ref, out_ref, order):
    heads, three, _, _ = x_ref.shape
    rows = out_ref.shape[0]
    step = pl.program_id(0)

    @pl.when(step == 0)
    def _():
        order[...] = swap_matrix(CHUNK, heads, 0)

    for b in range(rows // CHUNK):
        span = pl.ds(pl.multiple_of(step * rows + b * CHUNK, CHUNK), CHUNK)
        for c in range(three):
            x = x_ref[:, c, span].reshape(CHUNK * heads, HD)
            out_ref[b * CHUNK : (b + 1) * CHUNK, c] = dot_nn(order[...], x).reshape(CHUNK, heads, HD)


def back_kernel(turn_ref, own_ref, other_ref, w_ref, out_ref, x_buf):
    half = own_ref.shape[0]

    @pl.when(pl.program_id(0) == 0)
    def _():
        for x_ref, place in ((own_ref, turn_ref[0]), (other_ref, 1 - turn_ref[0])):
            x_buf[pl.ds(pl.multiple_of(place * half, half), half)] = x_ref[...]

    y = dot_nt(w_ref[...], x_buf[...])
    for h in range(out_ref.shape[0]):
        out_ref[h] = y[h * HD : (h + 1) * HD].T.astype(jnp.bfloat16)


def forward_kernel(step, outer, me_ref, *refs):
    parts, rest = refs[:-5 - outer], refs[-5 - outer :]
    qkv_ref, att_ref, lse_ref, *sent, v_t, s_buf = rest
    me = me_ref[0]
    for k, part in enumerate(parts):
        qkv_ref[me ^ k] = part[...]
    chunks, _, unit, _ = qkv_ref.shape
    per = step // unit
    blocks = chunks // per
    scale = LOG2E / math.sqrt(HD)
    for b in range(blocks):
        v_t[b] = rows_of(qkv_ref, b * per, per, 2).T
    for i in range(blocks):
        q = rows_of(qkv_ref, i * per, per, 0)
        top = None
        for j in range(i + 1):
            s = dot_nt(rows_of(qkv_ref, j * per, per, 1), q)
            if j == i:
                key = lax.broadcasted_iota(jnp.int32, s.shape, 0)
                query = lax.broadcasted_iota(jnp.int32, s.shape, 1)
                s = jnp.where(key <= query, s, -jnp.inf)
            s_buf[i % 2, j] = s
            peak = jnp.max(s, axis=0, keepdims=True)
            top = peak if top is None else jnp.maximum(top, peak)
        total = jnp.zeros((1, step), jnp.float32)
        for j in range(i + 1):
            p = jnp.exp2((s_buf[i % 2, j] - top) * scale)
            s_buf[i % 2, j] = p
            total = total + jnp.sum(p, axis=0, keepdims=True)
        inverse = 1.0 / total
        acc = jnp.zeros((HD, step), jnp.float32)
        for j in range(i + 1):
            acc = acc + dot_nn(v_t[j], (s_buf[i % 2, j] * inverse).astype(jnp.bfloat16))
        att_ref[i * per : (i + 1) * per] = acc.T.astype(jnp.bfloat16).reshape(per, unit, HD)
        lse_ref[i] = top * scale + jnp.log2(total)
    for d, ref in enumerate(sent):
        for e in range(PLANE):
            ref[e] = att_ref[me ^ (PLANE * d + e)]


def gather_kernel(me_ref, *refs):
    *parts, out_ref = refs
    own, others = parts[: len(parts) - PLANE + 1], parts[len(parts) - PLANE + 1 :]
    for d, ref in enumerate(own):
        out_ref[me_ref[0] ^ (PLANE * d)] = ref[0]
        for e in range(1, PLANE):
            out_ref[me_ref[0] ^ (PLANE * d + e)] = others[e - 1][d]


def backward_kernel(step, qkv_ref, g_ref, att_ref, lse_ref, out_ref, k_t, dq_t, delta):
    chunks, _, unit, _ = qkv_ref.shape
    per = step // unit
    blocks = chunks // per
    half = step // 2
    factor = 1.0 / math.sqrt(HD)
    for b in range(blocks):
        k_t[b] = rows_of(qkv_ref, b * per, per, 1).T
        prod = rows_of(g_ref, b * per, per).astype(jnp.float32)
        prod = prod * rows_of(att_ref, b * per, per).astype(jnp.float32)
        delta[b] = jnp.sum(prod.T, axis=0, keepdims=True)
        dq_t[b] = jnp.zeros((HD, step), jnp.float32)

    def pair(k, v, kt, q, g, lse, dlt, masked):
        w = jnp.exp2(dot_nt(k, q) * (factor * LOG2E) - lse)
        if masked:
            key = lax.broadcasted_iota(jnp.int32, w.shape, 0)
            query = lax.broadcasted_iota(jnp.int32, w.shape, 1)
            w = jnp.where(key <= query, w, 0.0)
        ds = (w * (dot_nt(v, g) - dlt) * factor).astype(jnp.bfloat16)
        dv = dot_nn(w.astype(jnp.bfloat16), g)
        return dot_nn(ds, q), dv, dot_nn(kt, ds)

    def key_block(j, _):
        k = rows_of(qkv_ref, j * per, per, 1)
        v = rows_of(qkv_ref, j * per, per, 2)
        kt = k_t[j]
        q = rows_of(qkv_ref, j * per, per, 0)
        g = rows_of(g_ref, j * per, per)
        lse, dlt = lse_ref[j], delta[j]
        dk0, dv0, part0 = pair(k[:half], v[:half], kt[:, :half], q, g, lse, dlt, True)
        dk1, dv1, part1 = pair(
            k[half:], v[half:], kt[:, half:], q[half:], g[half:], lse[:, half:], dlt[:, half:], True
        )
        dq_t[j, :, :half] += part0[:, :half]
        dq_t[j, :, half:] += part0[:, half:] + part1

        def later(i, carry):
            dk, dv, part = pair(
                k, v, kt, rows_of(qkv_ref, i * per, per, 0), rows_of(g_ref, i * per, per),
                lse_ref[i], delta[i], False,
            )
            dq_t[i] += part
            return carry[0] + dk, carry[1] + dv

        start = jnp.concatenate([dk0, dk1]), jnp.concatenate([dv0, dv1])
        dk, dv = py_loop(j + 1, blocks, later, start)
        spot = pl.ds(j * per, per)
        out_ref[spot, 1] = dk.astype(jnp.bfloat16).reshape(per, unit, HD)
        out_ref[spot, 2] = dv.astype(jnp.bfloat16).reshape(per, unit, HD)
        return 0

    py_loop(0, blocks, key_block, 0)
    for b in range(blocks):
        out_ref[pl.ds(b * per, per), 0] = dq_t[b].T.astype(jnp.bfloat16).reshape(per, unit, HD)


def in_vmem(count):
    return [pl.BlockSpec(memory_space=pltpu.VMEM)] * count


def in_smem():
    return pl.BlockSpec(memory_space=pltpu.SMEM)


def split_heads(me, qkv):
    rows, heads = qkv.shape[:2]
    part = 4 * CHUNK
    return pl.pallas_call(
        split_kernel,
        grid=(rows // part,),
        out_shape=[jax.ShapeDtypeStruct((3, rows, HD), jnp.bfloat16)] * heads,
        in_specs=[in_smem(), pl.BlockSpec((part, 3, heads, HD), lambda b: (b, 0, 0, 0))],
        out_specs=in_vmem(heads),
        scratch_shapes=[pltpu.VMEM((CHUNK * heads, CHUNK * heads), jnp.bfloat16)],
        compiler_params=pltpu.CompilerParams(vmem_limit_bytes=VMEM_LIMIT),
        name="split_heads",
    )(me, pltpu.with_memory_space_constraint(jnp.transpose(qkv, (0, 2, 1, 3)), pltpu.HBM))


def join_heads(grads):
    heads, three, rows, _ = grads.shape
    part = 2 * CHUNK
    out = pl.pallas_call(
        join_kernel,
        grid=(rows // part,),
        out_shape=jax.ShapeDtypeStruct((rows, three, heads, HD), jnp.float32),
        in_specs=in_vmem(1),
        out_specs=pl.BlockSpec((part, three, heads, HD), lambda b: (b, 0, 0, 0)),
        scratch_shapes=[pltpu.VMEM((CHUNK * heads, CHUNK * heads), jnp.bfloat16)],
        compiler_params=pltpu.CompilerParams(vmem_limit_bytes=VMEM_LIMIT),
        name="join_heads",
    )(grads)
    return jnp.transpose(out, (0, 2, 1, 3))


def project_back(turn, own, other, weights):
    half, width = own.shape
    heads = weights.shape[0] // HD
    group = 4
    return pl.pallas_call(
        back_kernel,
        grid=(heads // group,),
        out_shape=jax.ShapeDtypeStruct((heads, 2 * half, HD), jnp.bfloat16),
        in_specs=[
            in_smem(),
            *in_vmem(2),
            pl.BlockSpec((group * HD, width), lambda b: (b, 0)),
        ],
        out_specs=pl.BlockSpec((group, 2 * half, HD), lambda b: (b, 0, 0)),
        scratch_shapes=[pltpu.VMEM((2 * half, width), jnp.bfloat16)],
        compiler_params=pltpu.CompilerParams(vmem_limit_bytes=32 * 1024 * 1024),
        cost_estimate=pl.CostEstimate(
            flops=4 * half * width * heads * HD,
            transcendentals=0,
            bytes_accessed=2 * width * heads * HD,
        ),
        name="project_back",
    )(turn, own, other, weights)


def attend(me, parts, step):
    chunks = len(parts)
    outer = chunks // PLANE
    unit = parts[0].shape[1]
    length = chunks * unit
    blocks = length // step
    area = length * length // 2
    return pl.pallas_call(
        functools.partial(forward_kernel, step, outer),
        out_shape=(
            jax.ShapeDtypeStruct((chunks, 3, unit, HD), jnp.bfloat16),
            jax.ShapeDtypeStruct((chunks, unit, HD), jnp.bfloat16),
            jax.ShapeDtypeStruct((blocks, 1, step), jnp.float32),
            *[jax.ShapeDtypeStruct((PLANE, unit, HD), jnp.bfloat16)] * outer,
        ),
        in_specs=[in_smem(), *in_vmem(chunks)],
        out_specs=tuple(in_vmem(3 + outer)),
        scratch_shapes=[
            pltpu.VMEM((blocks, HD, step), jnp.bfloat16),
            pltpu.VMEM((2, blocks, step, step), jnp.float32),
        ],
        compiler_params=pltpu.CompilerParams(vmem_limit_bytes=VMEM_LIMIT),
        cost_estimate=pl.CostEstimate(
            flops=4 * area * HD, transcendentals=area, bytes_accessed=8 * length * HD
        ),
        name="attend",
    )(me, *parts)


def gather_heads(me, own, others):
    chunks = PLANE * len(own)
    shape = (chunks, *own[0].shape[1:])
    return pl.pallas_call(
        gather_kernel,
        out_shape=jax.ShapeDtypeStruct(shape, jnp.bfloat16),
        in_specs=[in_smem(), *in_vmem(len(own) + PLANE - 1)],
        out_specs=in_vmem(1)[0],
        compiler_params=pltpu.CompilerParams(vmem_limit_bytes=VMEM_LIMIT),
        name="gather_heads",
    )(me, *own, *others)


def attend_grad(qkv, g, att, lse, step):
    chunks, _, unit, _ = qkv.shape
    length = chunks * unit
    blocks = length // step
    area = length * length // 2
    return pl.pallas_call(
        functools.partial(backward_kernel, step),
        out_shape=jax.ShapeDtypeStruct((chunks, 3, unit, HD), jnp.bfloat16),
        in_specs=in_vmem(4),
        out_specs=in_vmem(1)[0],
        scratch_shapes=[
            pltpu.VMEM((blocks, HD, step), jnp.bfloat16),
            pltpu.VMEM((blocks, HD, step), jnp.float32),
            pltpu.VMEM((blocks, 1, step), jnp.float32),
        ],
        compiler_params=pltpu.CompilerParams(vmem_limit_bytes=VMEM_LIMIT),
        cost_estimate=pl.CostEstimate(
            flops=10 * area * HD, transcendentals=area, bytes_accessed=16 * length * HD
        ),
        name="attend_grad",
    )(qkv, g, att, lse)


def by_head(qkv, grad_out, attn_out):
    rows, heads = qkv.shape[:2]
    half = grad_out.shape[0]
    width = attn_out.shape[1]
    step = 512 if (rows * heads) % 512 == 0 else rows
    swap = [(0, 1), (1, 0)]
    turn = lax.axis_index("tp")
    me = lax.axis_index("ctx").reshape(1)
    weights = attn_out.reshape(heads, HD, width)

    def spread(x):
        return lax.all_to_all(x, "ctx", 0, 0, tiled=True)

    other_out = lax.ppermute(grad_out, "tp", swap)
    parts = list(split_heads(me, qkv))
    for k in range(1, heads):
        parts[k] = lax.ppermute(parts[k], "ctx", [(i, i ^ k) for i in range(heads)])
    g = project_back(turn.reshape(1), grad_out, other_out, attn_out)
    g = spread(g)
    mine, att, lse, *own = attend(me, parts, step)
    for d in range(1, len(own)):
        own[d] = lax.ppermute(own[d], "ctx", [(i, i ^ (PLANE * d)) for i in range(heads)])
    grads = attend_grad(mine, g, att, lse, step)
    others = []
    for e in range(1, PLANE):
        sent = jnp.stack([x[e] for x in own])
        others.append(lax.ppermute(sent, "ctx", [(i, i ^ e) for i in range(heads)]))
    grads = spread(grads)
    local = gather_heads(me, own, others)
    pieces = []
    part = width // MIX_PARTS
    for c in range(MIX_PARTS):
        mixed = jnp.einsum(
            "hrd,hdm->rm",
            local,
            weights[:, :, c * part : (c + 1) * part],
            preferred_element_type=jnp.float32,
        )
        sent = lax.dynamic_slice_in_dim(mixed, (1 - turn) * half, half, 0)
        kept = lax.dynamic_slice_in_dim(mixed, turn * half, half, 0)
        got = lax.ppermute(sent.astype(jnp.bfloat16), "tp", swap)
        pieces.append(kept + got.astype(jnp.float32))
    mixed_out = jnp.concatenate(pieces, axis=1)
    return mixed_out, join_heads(grads)


def by_rows(qkv, grad_out, attn_out):
    row_count, heads_local = (qkv.shape[0], qkv.shape[1])
    factor = 1.0 / math.sqrt(HD)
    queries = qkv[:, :, 0]
    keys_local = qkv[:, :, 1]
    values_local = qkv[:, :, 2]
    all_keys, all_values = (
        lax.all_gather(keys_local, "ctx", axis=0, tiled=True),
        lax.all_gather(values_local, "ctx", axis=0, tiled=True),
    )
    seq_len = all_keys.shape[0]
    offset = lax.axis_index("ctx") * row_count
    query_pos = offset + jnp.arange(row_count, dtype=jnp.int32)
    key_pos = jnp.arange(seq_len, dtype=jnp.int32)
    visible = key_pos[None, :] <= query_pos[:, None]
    scores = (
        jnp.einsum("rhd,shd->hrs", queries, all_keys, preferred_element_type=jnp.float32) * factor
    )
    scores = jnp.where(visible[None], scores, -jnp.inf)
    row_max = jnp.max(scores, axis=2, keepdims=True)
    log_total = row_max + jnp.log(jnp.sum(jnp.exp(scores - row_max), axis=2, keepdims=True))
    weights = jnp.exp(scores - log_total)
    weights_low = weights.astype(jnp.bfloat16)
    attended = jnp.einsum(
        "hrs,shd->rhd", weights_low, all_values, preferred_element_type=jnp.float32
    ).astype(jnp.bfloat16)
    attended_flat = attended.reshape(row_count, heads_local * HD)
    mixed_out = lax.psum_scatter(
        jnp.dot(attended_flat, attn_out, preferred_element_type=jnp.float32),
        "tp",
        scatter_dimension=0,
        tiled=True,
    )
    grad_full = jnp.einsum(
        "nm,km->nk",
        lax.all_gather(grad_out, "tp", axis=0, tiled=True),
        attn_out,
        preferred_element_type=jnp.float32,
    )
    grad_att = grad_full.astype(jnp.bfloat16).reshape(row_count, heads_local, HD)
    row_delta = jnp.einsum("rhd,rhd->rh", grad_att, attended, preferred_element_type=jnp.float32)
    grad_weights = jnp.einsum(
        "rhd,shd->hrs", grad_att, all_values, preferred_element_type=jnp.float32
    )
    grad_scores = (weights * (grad_weights - row_delta.T[:, :, None]) * factor).astype(jnp.bfloat16)
    grad_queries = jnp.einsum(
        "hrs,shd->rhd", grad_scores, all_keys, preferred_element_type=jnp.float32
    )
    lse_rows = log_total[:, :, 0].T
    row_stats = (
        lax.all_gather(lse_rows, "ctx", axis=0, tiled=True),
        lax.all_gather(row_delta, "ctx", axis=0, tiled=True),
    )
    piece_q = lax.all_gather(queries, "ctx", axis=0, tiled=True)
    piece_g = lax.all_gather(grad_att, "ctx", axis=0, tiled=True)
    piece_len = piece_q.shape[0]
    piece_lse = row_stats[0]
    piece_delta = row_stats[1]
    piece_pos = jnp.arange(piece_len, dtype=jnp.int32)
    visible_part = query_pos[None, :] <= piece_pos[:, None]
    part_scores = (
        jnp.einsum("nhd,rhd->hnr", piece_q, keys_local, preferred_element_type=jnp.float32) * factor
    )
    part_weights = jnp.where(
        visible_part[None], jnp.exp(part_scores - piece_lse.T[:, :, None]), 0.0
    )
    part_grad = jnp.einsum(
        "nhd,rhd->hnr", piece_g, values_local, preferred_element_type=jnp.float32
    )
    part_ds = (part_weights * (part_grad - piece_delta.T[:, :, None]) * factor).astype(jnp.bfloat16)
    grad_k = jnp.einsum("hnr,nhd->rhd", part_ds, piece_q, preferred_element_type=jnp.float32)
    grad_v = jnp.einsum(
        "hnr,nhd->rhd",
        part_weights.astype(jnp.bfloat16),
        piece_g,
        preferred_element_type=jnp.float32,
    )
    grad_qkv = jnp.stack([grad_queries, grad_k, grad_v], axis=2)
    return (mixed_out, grad_qkv)


def solution(mesh):
    ctx, tp = mesh.shape["ctx"], mesh.shape["tp"]
    in_specs = (P("ctx", "tp", None, None), P(("ctx", "tp"), None), P("tp", None))
    out_specs = (P(("ctx", "tp"), None), P("ctx", "tp", None, None))

    def whole(qkv, grad_out, attn_out):
        split = qkv.shape[1] == ctx * tp and tp == 2 and ctx >= 2 * PLANE and ctx & (ctx - 1) == 0
        step = jax.shard_map(
            by_head if split else by_rows,
            mesh=mesh,
            in_specs=in_specs,
            out_specs=out_specs,
            check_vma=False,
        )
        return step(qkv, grad_out, attn_out)

    return whole
```

```python
import functools
import math

import jax
import jax.numpy as jnp
from jax import lax
from jax.experimental import pallas as pl
from jax.experimental.pallas import tpu as pltpu
from jax.sharding import PartitionSpec as P


HD = 128
LOG2E = math.log2(math.e)
MIX_PARTS = (1, 1, 2, 2, 2)
MIB = 1024 * 1024


def dot_nt(a, b):
    return lax.dot_general(a, b, (((1,), (1,)), ((), ())), preferred_element_type=jnp.float32)


def dot_nn(a, b):
    return lax.dot_general(a, b, (((1,), (0,)), ((), ())), preferred_element_type=jnp.float32)


def rows_of(ref, start, count, *which):
    part = ref[(pl.ds(start, count), *which)]
    return part.reshape(count * part.shape[1], part.shape[2])


CHUNK = 16
PLANE = 4


def py_loop(lo, hi, body, carry):
    for i in range(lo, hi):
        carry = body(i, carry)
    return carry


def swap_matrix(heads, chunk, me):
    size = heads * chunk
    row = lax.broadcasted_iota(jnp.int32, (size, size), 0)
    col = lax.broadcasted_iota(jnp.int32, (size, size), 1)
    want = lax.rem(row, chunk) * heads + (lax.div(row, chunk) ^ me)
    return jnp.where(col == want, 1.0, 0.0).astype(jnp.bfloat16)


def split_kernel(me_ref, x_ref, *refs):
    *out_refs, order = refs
    rows, three, heads, _ = x_ref.shape
    step = pl.program_id(0)

    @pl.when(step == 0)
    def _():
        order[...] = swap_matrix(heads, CHUNK, me_ref[0])

    for b in range(rows // CHUNK):
        span = pl.ds(pl.multiple_of(step * rows + b * CHUNK, CHUNK), CHUNK)
        for c in range(three):
            x = x_ref[b * CHUNK : (b + 1) * CHUNK, c].reshape(CHUNK * heads, HD)
            y = dot_nn(order[...], x).astype(jnp.bfloat16).reshape(heads, CHUNK, HD)
            for k in range(heads):
                out_refs[k][c, span] = y[k]


def join_kernel(x_ref, out_ref, order):
    heads, three, _, _ = x_ref.shape
    rows = out_ref.shape[0]
    step = pl.program_id(0)

    @pl.when(step == 0)
    def _():
        order[...] = swap_matrix(CHUNK, heads, 0)

    for b in range(rows // CHUNK):
        span = pl.ds(pl.multiple_of(step * rows + b * CHUNK, CHUNK), CHUNK)
        for c in range(three):
            x = x_ref[:, c, span].reshape(CHUNK * heads, HD)
            out_ref[b * CHUNK : (b + 1) * CHUNK, c] = dot_nn(order[...], x).reshape(CHUNK, heads, HD)


def back_kernel(turn_ref, own_ref, other_ref, w_ref, out_ref, x_buf):
    half = own_ref.shape[0]

    @pl.when(pl.program_id(0) == 0)
    def _():
        for x_ref, place in ((own_ref, turn_ref[0]), (other_ref, 1 - turn_ref[0])):
            x_buf[pl.ds(pl.multiple_of(place * half, half), half)] = x_ref[...]

    y = dot_nt(w_ref[...], x_buf[...])
    for h in range(out_ref.shape[0]):
        out_ref[h] = y[h * HD : (h + 1) * HD].T.astype(jnp.bfloat16)


def forward_kernel(step, outer, me_ref, *refs):
    parts, rest = refs[: -5 - outer], refs[-5 - outer :]
    lse_ref, *sent, qkv_ref, att_ref, v_t, s_buf = rest
    me = me_ref[0]
    for k, part in enumerate(parts):
        qkv_ref[me ^ k] = part[...]
    chunks, _, unit, _ = qkv_ref.shape
    per = step // unit
    blocks = chunks // per
    scale = LOG2E / math.sqrt(HD)
    for b in range(blocks):
        v_t[b] = rows_of(qkv_ref, b * per, per, 2).T
    for i in range(blocks):
        q = rows_of(qkv_ref, i * per, per, 0)
        top = None
        for j in range(i + 1):
            s = dot_nt(rows_of(qkv_ref, j * per, per, 1), q)
            if j == i:
                key = lax.broadcasted_iota(jnp.int32, s.shape, 0)
                query = lax.broadcasted_iota(jnp.int32, s.shape, 1)
                s = jnp.where(key <= query, s, -jnp.inf)
            s_buf[i % 2, j] = s
            peak = jnp.max(s, axis=0, keepdims=True)
            top = peak if top is None else jnp.maximum(top, peak)
        total = jnp.zeros((1, step), jnp.float32)
        for j in range(i + 1):
            p = jnp.exp2((s_buf[i % 2, j] - top) * scale)
            s_buf[i % 2, j] = p
            total = total + jnp.sum(p, axis=0, keepdims=True)
        inverse = 1.0 / total
        acc = jnp.zeros((HD, step), jnp.float32)
        for j in range(i + 1):
            acc = acc + dot_nn(v_t[j], (s_buf[i % 2, j] * inverse).astype(jnp.bfloat16))
        att_ref[i * per : (i + 1) * per] = acc.T.astype(jnp.bfloat16).reshape(per, unit, HD)
        lse_ref[i] = top * scale + jnp.log2(total)
    for d, ref in enumerate(sent):
        for e in range(PLANE):
            ref[e] = att_ref[me ^ (PLANE * d + e)]


def gather_kernel(me_ref, *refs):
    *parts, out_ref = refs
    own, others = parts[: len(parts) - PLANE + 1], parts[len(parts) - PLANE + 1 :]
    for d, ref in enumerate(own):
        out_ref[me_ref[0] ^ (PLANE * d)] = ref[0]
        for e in range(1, PLANE):
            out_ref[me_ref[0] ^ (PLANE * d + e)] = others[e - 1][d]


def finish_kernel(turn_ref, *refs):
    *parts, out_ref = refs
    half = out_ref.shape[0]
    start = 0
    for mixed_ref, got_ref in zip(parts[::2], parts[1::2]):
        stop = start + mixed_ref.shape[1]
        kept = mixed_ref[pl.ds(pl.multiple_of(turn_ref[0] * half, half), half)]
        out_ref[:, start:stop] = kept + got_ref[...].astype(jnp.float32)
        start = stop


def backward_kernel(step, chunks, me_ref, g_ref, lse_ref, *refs):
    parts, own, rest = refs[:chunks], refs[chunks:-6], refs[-6:]
    out_ref, qkv_ref, att_ref, k_t, dq_t, delta = rest
    me = me_ref[0]
    for k, part in enumerate(parts):
        qkv_ref[me ^ k] = part[...]
        att_ref[me ^ k] = own[k // PLANE][k % PLANE]
    chunks, _, unit, _ = qkv_ref.shape
    per = step // unit
    blocks = chunks // per
    half = step // 2
    factor = 1.0 / math.sqrt(HD)
    for b in range(blocks):
        k_t[b] = rows_of(qkv_ref, b * per, per, 1).T
        prod = rows_of(g_ref, b * per, per).astype(jnp.float32)
        prod = prod * rows_of(att_ref, b * per, per).astype(jnp.float32)
        delta[b] = jnp.sum(prod.T, axis=0, keepdims=True)
        dq_t[b] = jnp.zeros((HD, step), jnp.float32)

    def pair(k, v, kt, q, g, lse, dlt, masked):
        w = jnp.exp2(dot_nt(k, q) * (factor * LOG2E) - lse)
        if masked:
            key = lax.broadcasted_iota(jnp.int32, w.shape, 0)
            query = lax.broadcasted_iota(jnp.int32, w.shape, 1)
            w = jnp.where(key <= query, w, 0.0)
        ds = (w * (dot_nt(v, g) - dlt) * factor).astype(jnp.bfloat16)
        dv = dot_nn(w.astype(jnp.bfloat16), g)
        return dot_nn(ds, q), dv, dot_nn(kt, ds)

    def key_block(j, _):
        k = rows_of(qkv_ref, j * per, per, 1)
        v = rows_of(qkv_ref, j * per, per, 2)
        kt = k_t[j]
        q = rows_of(qkv_ref, j * per, per, 0)
        g = rows_of(g_ref, j * per, per)
        lse, dlt = lse_ref[j], delta[j]
        dk0, dv0, part0 = pair(k[:half], v[:half], kt[:, :half], q, g, lse, dlt, True)
        dk1, dv1, part1 = pair(
            k[half:], v[half:], kt[:, half:], q[half:], g[half:], lse[:, half:], dlt[:, half:], True
        )
        dq_t[j, :, :half] += part0[:, :half]
        dq_t[j, :, half:] += part0[:, half:] + part1

        def later(i, carry):
            dk, dv, part = pair(
                k, v, kt, rows_of(qkv_ref, i * per, per, 0), rows_of(g_ref, i * per, per),
                lse_ref[i], delta[i], False,
            )
            dq_t[i] += part
            return carry[0] + dk, carry[1] + dv

        start = jnp.concatenate([dk0, dk1]), jnp.concatenate([dv0, dv1])
        dk, dv = py_loop(j + 1, blocks, later, start)
        spot = pl.ds(j * per, per)
        out_ref[spot, 1] = dk.astype(jnp.bfloat16).reshape(per, unit, HD)
        out_ref[spot, 2] = dv.astype(jnp.bfloat16).reshape(per, unit, HD)
        return 0

    py_loop(0, blocks, key_block, 0)
    for b in range(blocks):
        out_ref[pl.ds(b * per, per), 0] = dq_t[b].T.astype(jnp.bfloat16).reshape(per, unit, HD)


def in_vmem(count):
    return [pl.BlockSpec(memory_space=pltpu.VMEM)] * count


def in_smem():
    return pl.BlockSpec(memory_space=pltpu.SMEM)


def split_heads(me, qkv):
    rows, heads = qkv.shape[:2]
    part = 4 * CHUNK
    return pl.pallas_call(
        split_kernel,
        grid=(rows // part,),
        out_shape=[jax.ShapeDtypeStruct((3, rows, HD), jnp.bfloat16)] * heads,
        in_specs=[in_smem(), pl.BlockSpec((part, 3, heads, HD), lambda b: (b, 0, 0, 0))],
        out_specs=in_vmem(heads),
        scratch_shapes=[pltpu.VMEM((CHUNK * heads, CHUNK * heads), jnp.bfloat16)],
        compiler_params=pltpu.CompilerParams(vmem_limit_bytes=6 * MIB),
        name="split_heads",
    )(me, pltpu.with_memory_space_constraint(jnp.transpose(qkv, (0, 2, 1, 3)), pltpu.HBM))


def join_heads(grads):
    heads, three, rows, _ = grads.shape
    part = 2 * CHUNK
    out = pl.pallas_call(
        join_kernel,
        grid=(rows // part,),
        out_shape=jax.ShapeDtypeStruct((rows, three, heads, HD), jnp.float32),
        in_specs=in_vmem(1),
        out_specs=pl.BlockSpec((part, three, heads, HD), lambda b: (b, 0, 0, 0)),
        scratch_shapes=[pltpu.VMEM((CHUNK * heads, CHUNK * heads), jnp.bfloat16)],
        compiler_params=pltpu.CompilerParams(vmem_limit_bytes=8 * MIB),
        name="join_heads",
    )(grads)
    return jnp.transpose(out, (0, 2, 1, 3))


def project_back(turn, own, other, weights):
    half, width = own.shape
    heads = weights.shape[0] // HD
    group = 4
    return pl.pallas_call(
        back_kernel,
        grid=(heads // group,),
        out_shape=jax.ShapeDtypeStruct((heads, 2 * half, HD), jnp.bfloat16),
        in_specs=[
            in_smem(),
            pl.BlockSpec((half, width), lambda b: (0, 0)),
            *in_vmem(1),
            pl.BlockSpec((group * HD, width), lambda b: (b, 0)),
        ],
        out_specs=pl.BlockSpec((group, 2 * half, HD), lambda b: (b, 0, 0)),
        scratch_shapes=[pltpu.VMEM((2 * half, width), jnp.bfloat16)],
        compiler_params=pltpu.CompilerParams(vmem_limit_bytes=26 * MIB),
        cost_estimate=pl.CostEstimate(
            flops=4 * half * width * heads * HD,
            transcendentals=0,
            bytes_accessed=2 * width * heads * HD,
        ),
        name="project_back",
    )(turn, own, other, weights)


def attend(me, parts, step):
    chunks = len(parts)
    outer = chunks // PLANE
    unit = parts[0].shape[1]
    length = chunks * unit
    blocks = length // step
    area = length * length // 2
    return pl.pallas_call(
        functools.partial(forward_kernel, step, outer),
        out_shape=(
            jax.ShapeDtypeStruct((blocks, 1, step), jnp.float32),
            *[jax.ShapeDtypeStruct((PLANE, unit, HD), jnp.bfloat16)] * outer,
        ),
        in_specs=[in_smem(), *in_vmem(chunks)],
        out_specs=tuple(in_vmem(1 + outer)),
        scratch_shapes=[
            pltpu.VMEM((chunks, 3, unit, HD), jnp.bfloat16),
            pltpu.VMEM((chunks, unit, HD), jnp.bfloat16),
            pltpu.VMEM((blocks, HD, step), jnp.bfloat16),
            pltpu.VMEM((2, blocks, step, step), jnp.float32),
        ],
        compiler_params=pltpu.CompilerParams(vmem_limit_bytes=16 * MIB),
        cost_estimate=pl.CostEstimate(
            flops=4 * area * HD, transcendentals=area, bytes_accessed=8 * length * HD
        ),
        name="attend",
    )(me, *parts)


def gather_heads(me, own, others):
    chunks = PLANE * len(own)
    shape = (chunks, *own[0].shape[1:])
    return pl.pallas_call(
        gather_kernel,
        out_shape=jax.ShapeDtypeStruct(shape, jnp.bfloat16),
        in_specs=[in_smem(), *in_vmem(len(own) + PLANE - 1)],
        out_specs=in_vmem(1)[0],
        compiler_params=pltpu.CompilerParams(vmem_limit_bytes=2 * MIB),
        name="gather_heads",
    )(me, *own, *others)


def finish(turn, parts):
    half = parts[0][1].shape[0]
    width = sum(mixed.shape[1] for mixed, _ in parts)
    flat = [x for pair in parts for x in pair]
    return pl.pallas_call(
        finish_kernel,
        out_shape=jax.ShapeDtypeStruct((half, width), jnp.float32),
        in_specs=[in_smem(), *in_vmem(len(flat))],
        out_specs=in_vmem(1)[0],
        compiler_params=pltpu.CompilerParams(vmem_limit_bytes=4 * MIB),
        name="finish",
    )(turn, *flat)


def attend_grad(me, g, lse, parts, own, step):
    chunks = len(parts)
    unit = parts[0].shape[1]
    length = chunks * unit
    blocks = length // step
    area = length * length // 2
    return pl.pallas_call(
        functools.partial(backward_kernel, step, chunks),
        out_shape=jax.ShapeDtypeStruct((chunks, 3, unit, HD), jnp.bfloat16),
        in_specs=[in_smem(), *in_vmem(2 + chunks + len(own))],
        out_specs=in_vmem(1)[0],
        scratch_shapes=[
            pltpu.VMEM((chunks, 3, unit, HD), jnp.bfloat16),
            pltpu.VMEM((chunks, unit, HD), jnp.bfloat16),
            pltpu.VMEM((blocks, HD, step), jnp.bfloat16),
            pltpu.VMEM((blocks, HD, step), jnp.float32),
            pltpu.VMEM((blocks, 1, step), jnp.float32),
        ],
        compiler_params=pltpu.CompilerParams(vmem_limit_bytes=16 * MIB),
        cost_estimate=pl.CostEstimate(
            flops=10 * area * HD, transcendentals=area, bytes_accessed=16 * length * HD
        ),
        name="attend_grad",
    )(me, g, lse, *parts, *own)


def by_head(qkv, grad_out, attn_out):
    rows, heads = qkv.shape[:2]
    half = grad_out.shape[0]
    width = attn_out.shape[1]
    step = 512 if (rows * heads) % 512 == 0 else rows
    swap = [(0, 1), (1, 0)]
    turn = lax.axis_index("tp")
    me = lax.axis_index("ctx").reshape(1)
    weights = attn_out.reshape(heads, HD, width)

    def spread(x):
        return lax.all_to_all(x, "ctx", 0, 0, tiled=True)

    other_out = lax.ppermute(grad_out, "tp", swap)
    parts = list(split_heads(me, qkv))
    for k in range(1, heads):
        parts[k] = lax.ppermute(parts[k], "ctx", [(i, i ^ k) for i in range(heads)])
    g = project_back(turn.reshape(1), grad_out, other_out, attn_out)
    g = spread(g)
    lse, *own = attend(me, parts, step)
    mixed_own = list(own)
    for d in range(1, len(own)):
        mixed_own[d] = lax.ppermute(own[d], "ctx", [(i, i ^ (PLANE * d)) for i in range(heads)])
    grads = attend_grad(me, g, lse, parts, own, step)
    others = []
    for e in range(1, PLANE):
        sent = jnp.stack([x[e] for x in mixed_own])
        others.append(lax.ppermute(sent, "ctx", [(i, i ^ e) for i in range(heads)]))
    grads = spread(grads)
    local = gather_heads(me, mixed_own, others)
    pieces = []
    start = 0
    for eighths in MIX_PARTS:
        stop = start + eighths * (width // 8)
        mixed = jnp.einsum(
            "hrd,hdm->rm",
            local,
            weights[:, :, start:stop],
            preferred_element_type=jnp.float32,
        )
        sent = lax.dynamic_slice_in_dim(mixed, (1 - turn) * half, half, 0)
        pieces.append((mixed, lax.ppermute(sent.astype(jnp.bfloat16), "tp", swap)))
        start = stop
    mixed_out = finish(turn.reshape(1), pieces)
    return mixed_out, join_heads(grads)


def by_rows(qkv, grad_out, attn_out):
    row_count, heads_local = (qkv.shape[0], qkv.shape[1])
    factor = 1.0 / math.sqrt(HD)
    queries = qkv[:, :, 0]
    keys_local = qkv[:, :, 1]
    values_local = qkv[:, :, 2]
    all_keys, all_values = (
        lax.all_gather(keys_local, "ctx", axis=0, tiled=True),
        lax.all_gather(values_local, "ctx", axis=0, tiled=True),
    )
    seq_len = all_keys.shape[0]
    offset = lax.axis_index("ctx") * row_count
    query_pos = offset + jnp.arange(row_count, dtype=jnp.int32)
    key_pos = jnp.arange(seq_len, dtype=jnp.int32)
    visible = key_pos[None, :] <= query_pos[:, None]
    scores = (
        jnp.einsum("rhd,shd->hrs", queries, all_keys, preferred_element_type=jnp.float32) * factor
    )
    scores = jnp.where(visible[None], scores, -jnp.inf)
    row_max = jnp.max(scores, axis=2, keepdims=True)
    log_total = row_max + jnp.log(jnp.sum(jnp.exp(scores - row_max), axis=2, keepdims=True))
    weights = jnp.exp(scores - log_total)
    weights_low = weights.astype(jnp.bfloat16)
    attended = jnp.einsum(
        "hrs,shd->rhd", weights_low, all_values, preferred_element_type=jnp.float32
    ).astype(jnp.bfloat16)
    attended_flat = attended.reshape(row_count, heads_local * HD)
    mixed_out = lax.psum_scatter(
        jnp.dot(attended_flat, attn_out, preferred_element_type=jnp.float32),
        "tp",
        scatter_dimension=0,
        tiled=True,
    )
    grad_full = jnp.einsum(
        "nm,km->nk",
        lax.all_gather(grad_out, "tp", axis=0, tiled=True),
        attn_out,
        preferred_element_type=jnp.float32,
    )
    grad_att = grad_full.astype(jnp.bfloat16).reshape(row_count, heads_local, HD)
    row_delta = jnp.einsum("rhd,rhd->rh", grad_att, attended, preferred_element_type=jnp.float32)
    grad_weights = jnp.einsum(
        "rhd,shd->hrs", grad_att, all_values, preferred_element_type=jnp.float32
    )
    grad_scores = (weights * (grad_weights - row_delta.T[:, :, None]) * factor).astype(jnp.bfloat16)
    grad_queries = jnp.einsum(
        "hrs,shd->rhd", grad_scores, all_keys, preferred_element_type=jnp.float32
    )
    lse_rows = log_total[:, :, 0].T
    row_stats = (
        lax.all_gather(lse_rows, "ctx", axis=0, tiled=True),
        lax.all_gather(row_delta, "ctx", axis=0, tiled=True),
    )
    piece_q = lax.all_gather(queries, "ctx", axis=0, tiled=True)
    piece_g = lax.all_gather(grad_att, "ctx", axis=0, tiled=True)
    piece_len = piece_q.shape[0]
    piece_lse = row_stats[0]
    piece_delta = row_stats[1]
    piece_pos = jnp.arange(piece_len, dtype=jnp.int32)
    visible_part = query_pos[None, :] <= piece_pos[:, None]
    part_scores = (
        jnp.einsum("nhd,rhd->hnr", piece_q, keys_local, preferred_element_type=jnp.float32) * factor
    )
    part_weights = jnp.where(
        visible_part[None], jnp.exp(part_scores - piece_lse.T[:, :, None]), 0.0
    )
    part_grad = jnp.einsum(
        "nhd,rhd->hnr", piece_g, values_local, preferred_element_type=jnp.float32
    )
    part_ds = (part_weights * (part_grad - piece_delta.T[:, :, None]) * factor).astype(jnp.bfloat16)
    grad_k = jnp.einsum("hnr,nhd->rhd", part_ds, piece_q, preferred_element_type=jnp.float32)
    grad_v = jnp.einsum(
        "hnr,nhd->rhd",
        part_weights.astype(jnp.bfloat16),
        piece_g,
        preferred_element_type=jnp.float32,
    )
    grad_qkv = jnp.stack([grad_queries, grad_k, grad_v], axis=2)
    return (mixed_out, grad_qkv)


def solution(mesh):
    ctx, tp = mesh.shape["ctx"], mesh.shape["tp"]
    in_specs = (P("ctx", "tp", None, None), P(("ctx", "tp"), None), P("tp", None))
    out_specs = (P(("ctx", "tp"), None), P("ctx", "tp", None, None))

    def whole(qkv, grad_out, attn_out):
        split = qkv.shape[1] == ctx * tp and tp == 2 and ctx >= 2 * PLANE and ctx & (ctx - 1) == 0
        step = jax.shard_map(
            by_head if split else by_rows,
            mesh=mesh,
            in_specs=in_specs,
            out_specs=out_specs,
            check_vma=False,
        )
        return step(qkv, grad_out, attn_out)

    return whole
```

```python
import functools
import math

import jax
import jax.numpy as jnp
from jax import lax
from jax.experimental import pallas as pl
from jax.experimental.pallas import tpu as pltpu
from jax.sharding import PartitionSpec as P


HD = 128
LOG2E = math.log2(math.e)
MIX_PARTS = (1, 1, 2, 2, 2)
MIB = 1024 * 1024


def dot_nt(a, b):
    return lax.dot_general(a, b, (((1,), (1,)), ((), ())), preferred_element_type=jnp.float32)


def dot_nn(a, b):
    return lax.dot_general(a, b, (((1,), (0,)), ((), ())), preferred_element_type=jnp.float32)


def rows_of(ref, start, count, *which):
    part = ref[(pl.ds(start, count), *which)]
    return part.reshape(count * part.shape[1], part.shape[2])


CHUNK = 16
PLANE = 4


def py_loop(lo, hi, body, carry):
    for i in range(lo, hi):
        carry = body(i, carry)
    return carry


def swap_matrix(heads, chunk, me):
    size = heads * chunk
    row = lax.broadcasted_iota(jnp.int32, (size, size), 0)
    col = lax.broadcasted_iota(jnp.int32, (size, size), 1)
    want = lax.rem(row, chunk) * heads + (lax.div(row, chunk) ^ me)
    return jnp.where(col == want, 1.0, 0.0).astype(jnp.bfloat16)


def split_kernel(me_ref, x_ref, *refs):
    *out_refs, order = refs
    rows, three, heads, _ = x_ref.shape
    step = pl.program_id(0)

    @pl.when(step == 0)
    def _():
        order[...] = swap_matrix(heads, CHUNK, me_ref[0])

    for b in range(rows // CHUNK):
        span = pl.ds(pl.multiple_of(step * rows + b * CHUNK, CHUNK), CHUNK)
        for c in range(three):
            x = x_ref[b * CHUNK : (b + 1) * CHUNK, c].reshape(CHUNK * heads, HD)
            y = dot_nn(order[...], x).astype(jnp.bfloat16).reshape(heads, CHUNK, HD)
            for k in range(heads):
                out_refs[k][c, span] = y[k]


def join_kernel(x_ref, out_ref, order):
    heads, three, _, _ = x_ref.shape
    rows = out_ref.shape[0]
    step = pl.program_id(0)

    @pl.when(step == 0)
    def _():
        order[...] = swap_matrix(CHUNK, heads, 0)

    for b in range(rows // CHUNK):
        span = pl.ds(pl.multiple_of(step * rows + b * CHUNK, CHUNK), CHUNK)
        for c in range(three):
            x = x_ref[:, c, span].reshape(CHUNK * heads, HD)
            out_ref[b * CHUNK : (b + 1) * CHUNK, c] = dot_nn(order[...], x).reshape(CHUNK, heads, HD)


def back_kernel(turn_ref, own_ref, other_ref, w_ref, out_ref, x_buf):
    half = own_ref.shape[0]

    @pl.when(pl.program_id(0) == 0)
    def _():
        for x_ref, place in ((own_ref, turn_ref[0]), (other_ref, 1 - turn_ref[0])):
            x_buf[pl.ds(pl.multiple_of(place * half, half), half)] = x_ref[...]

    y = dot_nt(w_ref[...], x_buf[...])
    for h in range(out_ref.shape[0]):
        out_ref[h] = y[h * HD : (h + 1) * HD].T.astype(jnp.bfloat16)


def forward_kernel(step, me_ref, *refs):
    parts, rest = refs[: -5 - PLANE], refs[-5 - PLANE :]
    lse_ref, *sent, qkv_ref, att_ref, v_t, s_buf = rest
    me = me_ref[0]
    for k, part in enumerate(parts):
        qkv_ref[me ^ k] = part[...]
    chunks, _, unit, _ = qkv_ref.shape
    per = step // unit
    blocks = chunks // per
    scale = LOG2E / math.sqrt(HD)
    for b in range(blocks):
        v_t[b] = rows_of(qkv_ref, b * per, per, 2).T
    for i in range(blocks):
        q = rows_of(qkv_ref, i * per, per, 0)
        top = None
        for j in range(i + 1):
            s = dot_nt(rows_of(qkv_ref, j * per, per, 1), q)
            if j == i:
                key = lax.broadcasted_iota(jnp.int32, s.shape, 0)
                query = lax.broadcasted_iota(jnp.int32, s.shape, 1)
                s = jnp.where(key <= query, s, -jnp.inf)
            s_buf[i % 2, j] = s
            peak = jnp.max(s, axis=0, keepdims=True)
            top = peak if top is None else jnp.maximum(top, peak)
        total = jnp.zeros((1, step), jnp.float32)
        for j in range(i + 1):
            p = jnp.exp2((s_buf[i % 2, j] - top) * scale)
            s_buf[i % 2, j] = p
            total = total + jnp.sum(p, axis=0, keepdims=True)
        inverse = 1.0 / total
        acc = jnp.zeros((HD, step), jnp.float32)
        for j in range(i + 1):
            acc = acc + dot_nn(v_t[j], (s_buf[i % 2, j] * inverse).astype(jnp.bfloat16))
        att_ref[i * per : (i + 1) * per] = acc.T.astype(jnp.bfloat16).reshape(per, unit, HD)
        lse_ref[i] = top * scale + jnp.log2(total)
    for e, ref in enumerate(sent):
        for d in range(chunks // PLANE):
            ref[d] = att_ref[me ^ (PLANE * d + e)]


def gather_kernel(me_ref, *refs):
    *parts, out_ref = refs
    plane, others = parts[:PLANE], parts[PLANE:]
    for e, ref in enumerate(plane):
        out_ref[me_ref[0] ^ e] = ref[0]
        for d, other in enumerate(others, 1):
            out_ref[me_ref[0] ^ (PLANE * d + e)] = other[e]


def finish_kernel(turn_ref, *refs):
    *parts, out_ref = refs
    half = out_ref.shape[0]
    start = 0
    for mixed_ref, got_ref in zip(parts[::2], parts[1::2]):
        stop = start + mixed_ref.shape[1]
        kept = mixed_ref[pl.ds(pl.multiple_of(turn_ref[0] * half, half), half)]
        out_ref[:, start:stop] = kept + got_ref[...].astype(jnp.float32)
        start = stop


def backward_kernel(step, chunks, me_ref, g_ref, lse_ref, *refs):
    parts, own, rest = refs[:chunks], refs[chunks:-6], refs[-6:]
    out_ref, qkv_ref, att_ref, k_t, dq_t, delta = rest
    me = me_ref[0]
    for k, part in enumerate(parts):
        qkv_ref[me ^ k] = part[...]
        att_ref[me ^ k] = own[k % PLANE][k // PLANE]
    chunks, _, unit, _ = qkv_ref.shape
    per = step // unit
    blocks = chunks // per
    half = step // 2
    factor = 1.0 / math.sqrt(HD)
    for b in range(blocks):
        k_t[b] = rows_of(qkv_ref, b * per, per, 1).T
        prod = rows_of(g_ref, b * per, per).astype(jnp.float32)
        prod = prod * rows_of(att_ref, b * per, per).astype(jnp.float32)
        delta[b] = jnp.sum(prod.T, axis=0, keepdims=True)
        dq_t[b] = jnp.zeros((HD, step), jnp.float32)

    def pair(k, v, kt, q, g, lse, dlt, masked):
        w = jnp.exp2(dot_nt(k, q) * (factor * LOG2E) - lse)
        if masked:
            key = lax.broadcasted_iota(jnp.int32, w.shape, 0)
            query = lax.broadcasted_iota(jnp.int32, w.shape, 1)
            w = jnp.where(key <= query, w, 0.0)
        ds = (w * (dot_nt(v, g) - dlt) * factor).astype(jnp.bfloat16)
        dv = dot_nn(w.astype(jnp.bfloat16), g)
        return dot_nn(ds, q), dv, dot_nn(kt, ds)

    def key_block(j, _):
        k = rows_of(qkv_ref, j * per, per, 1)
        v = rows_of(qkv_ref, j * per, per, 2)
        kt = k_t[j]
        q = rows_of(qkv_ref, j * per, per, 0)
        g = rows_of(g_ref, j * per, per)
        lse, dlt = lse_ref[j], delta[j]
        dk0, dv0, part0 = pair(k[:half], v[:half], kt[:, :half], q, g, lse, dlt, True)
        dk1, dv1, part1 = pair(
            k[half:], v[half:], kt[:, half:], q[half:], g[half:], lse[:, half:], dlt[:, half:], True
        )
        dq_t[j, :, :half] += part0[:, :half]
        dq_t[j, :, half:] += part0[:, half:] + part1

        def later(i, carry):
            dk, dv, part = pair(
                k, v, kt, rows_of(qkv_ref, i * per, per, 0), rows_of(g_ref, i * per, per),
                lse_ref[i], delta[i], False,
            )
            dq_t[i] += part
            return carry[0] + dk, carry[1] + dv

        start = jnp.concatenate([dk0, dk1]), jnp.concatenate([dv0, dv1])
        dk, dv = py_loop(j + 1, blocks, later, start)
        spot = pl.ds(j * per, per)
        out_ref[spot, 1] = dk.astype(jnp.bfloat16).reshape(per, unit, HD)
        out_ref[spot, 2] = dv.astype(jnp.bfloat16).reshape(per, unit, HD)
        return 0

    py_loop(0, blocks, key_block, 0)
    for b in range(blocks):
        out_ref[pl.ds(b * per, per), 0] = dq_t[b].T.astype(jnp.bfloat16).reshape(per, unit, HD)


def in_vmem(count):
    return [pl.BlockSpec(memory_space=pltpu.VMEM)] * count


def in_smem():
    return pl.BlockSpec(memory_space=pltpu.SMEM)


def split_heads(me, qkv):
    rows, heads = qkv.shape[:2]
    part = 4 * CHUNK
    return pl.pallas_call(
        split_kernel,
        grid=(rows // part,),
        out_shape=[jax.ShapeDtypeStruct((3, rows, HD), jnp.bfloat16)] * heads,
        in_specs=[in_smem(), pl.BlockSpec((part, 3, heads, HD), lambda b: (b, 0, 0, 0))],
        out_specs=in_vmem(heads),
        scratch_shapes=[pltpu.VMEM((CHUNK * heads, CHUNK * heads), jnp.bfloat16)],
        compiler_params=pltpu.CompilerParams(vmem_limit_bytes=6 * MIB),
        name="split_heads",
    )(me, pltpu.with_memory_space_constraint(jnp.transpose(qkv, (0, 2, 1, 3)), pltpu.HBM))


def join_heads(grads):
    heads, three, rows, _ = grads.shape
    part = 2 * CHUNK
    out = pl.pallas_call(
        join_kernel,
        grid=(rows // part,),
        out_shape=jax.ShapeDtypeStruct((rows, three, heads, HD), jnp.float32),
        in_specs=in_vmem(1),
        out_specs=pl.BlockSpec((part, three, heads, HD), lambda b: (b, 0, 0, 0)),
        scratch_shapes=[pltpu.VMEM((CHUNK * heads, CHUNK * heads), jnp.bfloat16)],
        compiler_params=pltpu.CompilerParams(vmem_limit_bytes=8 * MIB),
        name="join_heads",
    )(grads)
    return jnp.transpose(out, (0, 2, 1, 3))


def project_back(turn, own, other, weights):
    half, width = own.shape
    heads = weights.shape[0] // HD
    group = 4
    return pl.pallas_call(
        back_kernel,
        grid=(heads // group,),
        out_shape=jax.ShapeDtypeStruct((heads, 2 * half, HD), jnp.bfloat16),
        in_specs=[
            in_smem(),
            pl.BlockSpec((half, width), lambda b: (0, 0)),
            *in_vmem(1),
            pl.BlockSpec((group * HD, width), lambda b: (b, 0)),
        ],
        out_specs=pl.BlockSpec((group, 2 * half, HD), lambda b: (b, 0, 0)),
        scratch_shapes=[pltpu.VMEM((2 * half, width), jnp.bfloat16)],
        compiler_params=pltpu.CompilerParams(vmem_limit_bytes=26 * MIB),
        cost_estimate=pl.CostEstimate(
            flops=4 * half * width * heads * HD,
            transcendentals=0,
            bytes_accessed=2 * width * heads * HD,
        ),
        name="project_back",
    )(turn, own, other, weights)


def attend(me, parts, step):
    chunks = len(parts)
    outer = chunks // PLANE
    unit = parts[0].shape[1]
    length = chunks * unit
    blocks = length // step
    area = length * length // 2
    return pl.pallas_call(
        functools.partial(forward_kernel, step),
        out_shape=(
            jax.ShapeDtypeStruct((blocks, 1, step), jnp.float32),
            *[jax.ShapeDtypeStruct((outer, unit, HD), jnp.bfloat16)] * PLANE,
        ),
        in_specs=[in_smem(), *in_vmem(chunks)],
        out_specs=tuple(in_vmem(1 + PLANE)),
        scratch_shapes=[
            pltpu.VMEM((chunks, 3, unit, HD), jnp.bfloat16),
            pltpu.VMEM((chunks, unit, HD), jnp.bfloat16),
            pltpu.VMEM((blocks, HD, step), jnp.bfloat16),
            pltpu.VMEM((2, blocks, step, step), jnp.float32),
        ],
        compiler_params=pltpu.CompilerParams(vmem_limit_bytes=16 * MIB),
        cost_estimate=pl.CostEstimate(
            flops=4 * area * HD, transcendentals=area, bytes_accessed=8 * length * HD
        ),
        name="attend",
    )(me, *parts)


def gather_heads(me, plane, others):
    shape = (PLANE * (len(others) + 1), *plane[0].shape[1:])
    return pl.pallas_call(
        gather_kernel,
        out_shape=jax.ShapeDtypeStruct(shape, jnp.bfloat16),
        in_specs=[in_smem(), *in_vmem(PLANE + len(others))],
        out_specs=in_vmem(1)[0],
        compiler_params=pltpu.CompilerParams(vmem_limit_bytes=2 * MIB),
        name="gather_heads",
    )(me, *plane, *others)


def finish(turn, parts):
    half = parts[0][1].shape[0]
    width = sum(mixed.shape[1] for mixed, _ in parts)
    flat = [x for pair in parts for x in pair]
    return pl.pallas_call(
        finish_kernel,
        out_shape=jax.ShapeDtypeStruct((half, width), jnp.float32),
        in_specs=[in_smem(), *in_vmem(len(flat))],
        out_specs=in_vmem(1)[0],
        compiler_params=pltpu.CompilerParams(vmem_limit_bytes=4 * MIB),
        name="finish",
    )(turn, *flat)


def attend_grad(me, g, lse, parts, own, step):
    chunks = len(parts)
    unit = parts[0].shape[1]
    length = chunks * unit
    blocks = length // step
    area = length * length // 2
    return pl.pallas_call(
        functools.partial(backward_kernel, step, chunks),
        out_shape=jax.ShapeDtypeStruct((chunks, 3, unit, HD), jnp.bfloat16),
        in_specs=[in_smem(), *in_vmem(2 + chunks + len(own))],
        out_specs=in_vmem(1)[0],
        scratch_shapes=[
            pltpu.VMEM((chunks, 3, unit, HD), jnp.bfloat16),
            pltpu.VMEM((chunks, unit, HD), jnp.bfloat16),
            pltpu.VMEM((blocks, HD, step), jnp.bfloat16),
            pltpu.VMEM((blocks, HD, step), jnp.float32),
            pltpu.VMEM((blocks, 1, step), jnp.float32),
        ],
        compiler_params=pltpu.CompilerParams(vmem_limit_bytes=16 * MIB),
        cost_estimate=pl.CostEstimate(
            flops=10 * area * HD, transcendentals=area, bytes_accessed=16 * length * HD
        ),
        name="attend_grad",
    )(me, g, lse, *parts, *own)


def by_head(qkv, grad_out, attn_out):
    rows, heads = qkv.shape[:2]
    half = grad_out.shape[0]
    width = attn_out.shape[1]
    step = 512 if (rows * heads) % 512 == 0 else rows
    swap = [(0, 1), (1, 0)]
    turn = lax.axis_index("tp")
    me = lax.axis_index("ctx").reshape(1)
    weights = attn_out.reshape(heads, HD, width)

    def spread(x):
        return lax.all_to_all(x, "ctx", 0, 0, tiled=True)

    other_out = lax.ppermute(grad_out, "tp", swap)
    parts = list(split_heads(me, qkv))
    for k in range(1, heads):
        parts[k] = lax.ppermute(parts[k], "ctx", [(i, i ^ k) for i in range(heads)])
    g = project_back(turn.reshape(1), grad_out, other_out, attn_out)
    g = spread(g)
    lse, *own = attend(me, parts, step)
    plane = list(own)
    for e in range(1, PLANE):
        plane[e] = lax.ppermute(own[e], "ctx", [(i, i ^ e) for i in range(heads)])
    others = []
    for d in range(1, heads // PLANE):
        sent = jnp.stack([x[d] for x in plane])
        pairs = [(i, i ^ (PLANE * d)) for i in range(heads)]
        others.append(lax.ppermute(sent, "ctx", pairs))
    grads = attend_grad(me, g, lse, parts, own, step)
    grads = spread(grads)
    local = gather_heads(me, plane, others)
    pieces = []
    start = 0
    for eighths in MIX_PARTS:
        stop = start + eighths * (width // 8)
        mixed = jnp.einsum(
            "hrd,hdm->rm",
            local,
            weights[:, :, start:stop],
            preferred_element_type=jnp.float32,
        )
        sent = lax.dynamic_slice_in_dim(mixed, (1 - turn) * half, half, 0)
        pieces.append((mixed, lax.ppermute(sent.astype(jnp.bfloat16), "tp", swap)))
        start = stop
    mixed_out = finish(turn.reshape(1), pieces)
    return mixed_out, join_heads(grads)


def by_rows(qkv, grad_out, attn_out):
    row_count, heads_local = (qkv.shape[0], qkv.shape[1])
    factor = 1.0 / math.sqrt(HD)
    queries = qkv[:, :, 0]
    keys_local = qkv[:, :, 1]
    values_local = qkv[:, :, 2]
    all_keys, all_values = (
        lax.all_gather(keys_local, "ctx", axis=0, tiled=True),
        lax.all_gather(values_local, "ctx", axis=0, tiled=True),
    )
    seq_len = all_keys.shape[0]
    offset = lax.axis_index("ctx") * row_count
    query_pos = offset + jnp.arange(row_count, dtype=jnp.int32)
    key_pos = jnp.arange(seq_len, dtype=jnp.int32)
    visible = key_pos[None, :] <= query_pos[:, None]
    scores = (
        jnp.einsum("rhd,shd->hrs", queries, all_keys, preferred_element_type=jnp.float32) * factor
    )
    scores = jnp.where(visible[None], scores, -jnp.inf)
    row_max = jnp.max(scores, axis=2, keepdims=True)
    log_total = row_max + jnp.log(jnp.sum(jnp.exp(scores - row_max), axis=2, keepdims=True))
    weights = jnp.exp(scores - log_total)
    weights_low = weights.astype(jnp.bfloat16)
    attended = jnp.einsum(
        "hrs,shd->rhd", weights_low, all_values, preferred_element_type=jnp.float32
    ).astype(jnp.bfloat16)
    attended_flat = attended.reshape(row_count, heads_local * HD)
    mixed_out = lax.psum_scatter(
        jnp.dot(attended_flat, attn_out, preferred_element_type=jnp.float32),
        "tp",
        scatter_dimension=0,
        tiled=True,
    )
    grad_full = jnp.einsum(
        "nm,km->nk",
        lax.all_gather(grad_out, "tp", axis=0, tiled=True),
        attn_out,
        preferred_element_type=jnp.float32,
    )
    grad_att = grad_full.astype(jnp.bfloat16).reshape(row_count, heads_local, HD)
    row_delta = jnp.einsum("rhd,rhd->rh", grad_att, attended, preferred_element_type=jnp.float32)
    grad_weights = jnp.einsum(
        "rhd,shd->hrs", grad_att, all_values, preferred_element_type=jnp.float32
    )
    grad_scores = (weights * (grad_weights - row_delta.T[:, :, None]) * factor).astype(jnp.bfloat16)
    grad_queries = jnp.einsum(
        "hrs,shd->rhd", grad_scores, all_keys, preferred_element_type=jnp.float32
    )
    lse_rows = log_total[:, :, 0].T
    row_stats = (
        lax.all_gather(lse_rows, "ctx", axis=0, tiled=True),
        lax.all_gather(row_delta, "ctx", axis=0, tiled=True),
    )
    piece_q = lax.all_gather(queries, "ctx", axis=0, tiled=True)
    piece_g = lax.all_gather(grad_att, "ctx", axis=0, tiled=True)
    piece_len = piece_q.shape[0]
    piece_lse = row_stats[0]
    piece_delta = row_stats[1]
    piece_pos = jnp.arange(piece_len, dtype=jnp.int32)
    visible_part = query_pos[None, :] <= piece_pos[:, None]
    part_scores = (
        jnp.einsum("nhd,rhd->hnr", piece_q, keys_local, preferred_element_type=jnp.float32) * factor
    )
    part_weights = jnp.where(
        visible_part[None], jnp.exp(part_scores - piece_lse.T[:, :, None]), 0.0
    )
    part_grad = jnp.einsum(
        "nhd,rhd->hnr", piece_g, values_local, preferred_element_type=jnp.float32
    )
    part_ds = (part_weights * (part_grad - piece_delta.T[:, :, None]) * factor).astype(jnp.bfloat16)
    grad_k = jnp.einsum("hnr,nhd->rhd", part_ds, piece_q, preferred_element_type=jnp.float32)
    grad_v = jnp.einsum(
        "hnr,nhd->rhd",
        part_weights.astype(jnp.bfloat16),
        piece_g,
        preferred_element_type=jnp.float32,
    )
    grad_qkv = jnp.stack([grad_queries, grad_k, grad_v], axis=2)
    return (mixed_out, grad_qkv)


def solution(mesh):
    ctx, tp = mesh.shape["ctx"], mesh.shape["tp"]
    in_specs = (P("ctx", "tp", None, None), P(("ctx", "tp"), None), P("tp", None))
    out_specs = (P(("ctx", "tp"), None), P("ctx", "tp", None, None))

    def whole(qkv, grad_out, attn_out):
        split = qkv.shape[1] == ctx * tp and tp == 2 and ctx >= 2 * PLANE and ctx & (ctx - 1) == 0
        step = jax.shard_map(
            by_head if split else by_rows,
            mesh=mesh,
            in_specs=in_specs,
            out_specs=out_specs,
            check_vma=False,
        )
        return step(qkv, grad_out, attn_out)

    return whole
```

```python
import functools
import math

import jax
import jax.numpy as jnp
from jax import lax
from jax.experimental import pallas as pl
from jax.experimental.pallas import tpu as pltpu
from jax.sharding import PartitionSpec as P


HD = 128
LOG2E = math.log2(math.e)
MIX_PARTS = (1, 1, 2, 2, 2)
MIB = 1024 * 1024


def dot_nt(a, b):
    return lax.dot_general(a, b, (((1,), (1,)), ((), ())), preferred_element_type=jnp.float32)


def dot_nn(a, b):
    return lax.dot_general(a, b, (((1,), (0,)), ((), ())), preferred_element_type=jnp.float32)


def rows_of(ref, start, count, *which):
    part = ref[(pl.ds(start, count), *which)]
    return part.reshape(count * part.shape[1], part.shape[2])


CHUNK = 16
PLANE = 4


def py_loop(lo, hi, body, carry):
    for i in range(lo, hi):
        carry = body(i, carry)
    return carry


def swap_matrix(heads, chunk, me):
    size = heads * chunk
    row = lax.broadcasted_iota(jnp.int32, (size, size), 0)
    col = lax.broadcasted_iota(jnp.int32, (size, size), 1)
    want = lax.rem(row, chunk) * heads + (lax.div(row, chunk) ^ me)
    return jnp.where(col == want, 1.0, 0.0).astype(jnp.bfloat16)


def join_kernel(x_ref, out_ref, order):
    heads, three, _, _ = x_ref.shape
    rows = out_ref.shape[0]
    step = pl.program_id(0)

    @pl.when(step == 0)
    def _():
        order[...] = swap_matrix(CHUNK, heads, 0)

    for b in range(rows // CHUNK):
        span = pl.ds(pl.multiple_of(step * rows + b * CHUNK, CHUNK), CHUNK)
        for c in range(three):
            x = x_ref[:, c, span].reshape(CHUNK * heads, HD)
            out_ref[b * CHUNK : (b + 1) * CHUNK, c] = dot_nn(order[...], x).reshape(CHUNK, heads, HD)


def stack_rows(turn_ref, own_ref, other_ref, x_buf):
    half = own_ref.shape[0]
    for x_ref, place in ((own_ref, turn_ref[0]), (other_ref, 1 - turn_ref[0])):
        x_buf[pl.ds(pl.multiple_of(place * half, half), half)] = x_ref[...]


def back_first_kernel(turn_ref, own_ref, other_ref, w_ref, out_ref, x_buf):
    @pl.when(pl.program_id(0) == 0)
    def _():
        stack_rows(turn_ref, own_ref, other_ref, x_buf)

    out_ref[...] = dot_nt(w_ref[...], x_buf[...])


def back_last_kernel(turn_ref, me_ref, own_ref, other_ref, w_ref, y_ref, *refs):
    *out_refs, x_buf, chunks = refs
    step = pl.program_id(0)
    group = w_ref.shape[0] // HD

    @pl.when(step == 0)
    def _():
        stack_rows(turn_ref, own_ref, other_ref, x_buf)

    y = y_ref[...] + dot_nt(w_ref[...], x_buf[...])
    for h in range(group):
        head = (step * group + h) ^ me_ref[0]
        chunks[head] = y[h * HD : (h + 1) * HD].T.astype(jnp.bfloat16)

    @pl.when(step == pl.num_programs(0) - 1)
    def _():
        for e, ref in enumerate(out_refs):
            for d in range(ref.shape[0]):
                ref[d] = chunks[PLANE * d + e]


def forward_kernel(step, qkv_ref, att_ref, lse_ref, v_t, s_buf):
    chunks, _, unit, _ = qkv_ref.shape
    per = step // unit
    blocks = chunks // per
    scale = LOG2E / math.sqrt(HD)
    for b in range(blocks):
        v_t[b] = rows_of(qkv_ref, b * per, per, 2).T
    for i in range(blocks):
        q = rows_of(qkv_ref, i * per, per, 0)
        top = None
        for j in range(i + 1):
            s = dot_nt(rows_of(qkv_ref, j * per, per, 1), q)
            if j == i:
                key = lax.broadcasted_iota(jnp.int32, s.shape, 0)
                query = lax.broadcasted_iota(jnp.int32, s.shape, 1)
                s = jnp.where(key <= query, s, -jnp.inf)
            s_buf[i % 2, j] = s
            peak = jnp.max(s, axis=0, keepdims=True)
            top = peak if top is None else jnp.maximum(top, peak)
        total = jnp.zeros((1, step), jnp.float32)
        for j in range(i + 1):
            p = jnp.exp2((s_buf[i % 2, j] - top) * scale)
            s_buf[i % 2, j] = p
            total = total + jnp.sum(p, axis=0, keepdims=True)
        inverse = 1.0 / total
        acc = jnp.zeros((HD, step), jnp.float32)
        for j in range(i + 1):
            acc = acc + dot_nn(v_t[j], (s_buf[i % 2, j] * inverse).astype(jnp.bfloat16))
        att_ref[i * per : (i + 1) * per] = acc.T.astype(jnp.bfloat16).reshape(per, unit, HD)
        lse_ref[i] = top * scale + jnp.log2(total)


def finish_kernel(turn_ref, *refs):
    *parts, out_ref = refs
    half = out_ref.shape[0]
    start = 0
    for mixed_ref, got_ref in zip(parts[::2], parts[1::2]):
        stop = start + mixed_ref.shape[1]
        kept = mixed_ref[pl.ds(pl.multiple_of(turn_ref[0] * half, half), half)]
        out_ref[:, start:stop] = kept + got_ref[...].astype(jnp.float32)
        start = stop


def backward_kernel(step, me_ref, qkv_ref, att_ref, lse_ref, *refs):
    parts, rest = refs[:-5], refs[-5:]
    out_ref, g_ref, k_t, dq_t, delta = rest
    plane, others = parts[:PLANE], parts[PLANE:]
    for e, ref in enumerate(plane):
        g_ref[me_ref[0] ^ e] = ref[0]
        for d, other in enumerate(others, 1):
            g_ref[me_ref[0] ^ (PLANE * d + e)] = other[e]
    chunks, _, unit, _ = qkv_ref.shape
    per = step // unit
    blocks = chunks // per
    half = step // 2
    factor = 1.0 / math.sqrt(HD)
    for b in range(blocks):
        k_t[b] = rows_of(qkv_ref, b * per, per, 1).T
        prod = rows_of(g_ref, b * per, per).astype(jnp.float32)
        prod = prod * rows_of(att_ref, b * per, per).astype(jnp.float32)
        delta[b] = jnp.sum(prod.T, axis=0, keepdims=True)
        dq_t[b] = jnp.zeros((HD, step), jnp.float32)

    def pair(k, v, kt, q, g, lse, dlt, masked):
        w = jnp.exp2(dot_nt(k, q) * (factor * LOG2E) - lse)
        if masked:
            key = lax.broadcasted_iota(jnp.int32, w.shape, 0)
            query = lax.broadcasted_iota(jnp.int32, w.shape, 1)
            w = jnp.where(key <= query, w, 0.0)
        ds = (w * (dot_nt(v, g) - dlt) * factor).astype(jnp.bfloat16)
        dv = dot_nn(w.astype(jnp.bfloat16), g)
        return dot_nn(ds, q), dv, dot_nn(kt, ds)

    def key_block(j, _):
        k = rows_of(qkv_ref, j * per, per, 1)
        v = rows_of(qkv_ref, j * per, per, 2)
        kt = k_t[j]
        q = rows_of(qkv_ref, j * per, per, 0)
        g = rows_of(g_ref, j * per, per)
        lse, dlt = lse_ref[j], delta[j]
        dk0, dv0, part0 = pair(k[:half], v[:half], kt[:, :half], q, g, lse, dlt, True)
        dk1, dv1, part1 = pair(
            k[half:], v[half:], kt[:, half:], q[half:], g[half:], lse[:, half:], dlt[:, half:], True
        )
        dq_t[j, :, :half] += part0[:, :half]
        dq_t[j, :, half:] += part0[:, half:] + part1

        def later(i, carry):
            dk, dv, part = pair(
                k, v, kt, rows_of(qkv_ref, i * per, per, 0), rows_of(g_ref, i * per, per),
                lse_ref[i], delta[i], False,
            )
            dq_t[i] += part
            return carry[0] + dk, carry[1] + dv

        start = jnp.concatenate([dk0, dk1]), jnp.concatenate([dv0, dv1])
        dk, dv = py_loop(j + 1, blocks, later, start)
        spot = pl.ds(j * per, per)
        out_ref[spot, 1] = dk.astype(jnp.bfloat16).reshape(per, unit, HD)
        out_ref[spot, 2] = dv.astype(jnp.bfloat16).reshape(per, unit, HD)
        return 0

    py_loop(0, blocks, key_block, 0)
    for b in range(blocks):
        out_ref[pl.ds(b * per, per), 0] = dq_t[b].T.astype(jnp.bfloat16).reshape(per, unit, HD)


def in_vmem(count):
    return [pl.BlockSpec(memory_space=pltpu.VMEM)] * count


def in_smem():
    return pl.BlockSpec(memory_space=pltpu.SMEM)


def join_heads(grads):
    heads, three, rows, _ = grads.shape
    part = 2 * CHUNK
    out = pl.pallas_call(
        join_kernel,
        grid=(rows // part,),
        out_shape=jax.ShapeDtypeStruct((rows, three, heads, HD), jnp.float32),
        in_specs=in_vmem(1),
        out_specs=pl.BlockSpec((part, three, heads, HD), lambda b: (b, 0, 0, 0)),
        scratch_shapes=[pltpu.VMEM((CHUNK * heads, CHUNK * heads), jnp.bfloat16)],
        compiler_params=pltpu.CompilerParams(vmem_limit_bytes=8 * MIB),
        name="join_heads",
    )(grads)
    return jnp.transpose(out, (0, 2, 1, 3))


def project_back(turn, me, own, other, weights):
    half, width = own.shape
    deep = weights.shape[0]
    group = 4 * HD
    part = width // 2
    cost = pl.CostEstimate(
        flops=2 * half * width * deep, transcendentals=0, bytes_accessed=width * deep
    )
    params = pltpu.CompilerParams(vmem_limit_bytes=22 * MIB)

    def rows(c):
        return pl.BlockSpec((half, part), lambda b: (0, c))

    def block(c):
        return pl.BlockSpec((group, part), lambda b: (b, c))

    partial = pl.BlockSpec((group, 2 * half), lambda b: (b, 0))
    x_buf = pltpu.VMEM((2 * half, part), jnp.bfloat16)
    y = pl.pallas_call(
        back_first_kernel,
        grid=(deep // group,),
        out_shape=jax.ShapeDtypeStruct((deep, 2 * half), jnp.float32),
        in_specs=[in_smem(), rows(0), *in_vmem(1), block(0)],
        out_specs=partial,
        scratch_shapes=[x_buf],
        compiler_params=params,
        cost_estimate=cost,
        name="back_first",
    )(turn, own, other[0], weights)
    heads = deep // HD
    return pl.pallas_call(
        back_last_kernel,
        grid=(deep // group,),
        out_shape=[jax.ShapeDtypeStruct((heads // PLANE, 2 * half, HD), jnp.bfloat16)] * PLANE,
        in_specs=[in_smem(), in_smem(), rows(1), *in_vmem(1), block(1), partial],
        out_specs=in_vmem(PLANE),
        scratch_shapes=[x_buf, pltpu.VMEM((heads, 2 * half, HD), jnp.bfloat16)],
        compiler_params=params,
        cost_estimate=cost,
        name="back_last",
    )(turn, me, own, other[1], weights, y)


def attend(qkv, step):
    chunks, _, unit, _ = qkv.shape
    length = chunks * unit
    blocks = length // step
    area = length * length // 2
    return pl.pallas_call(
        functools.partial(forward_kernel, step),
        out_shape=(
            jax.ShapeDtypeStruct((chunks, unit, HD), jnp.bfloat16),
            jax.ShapeDtypeStruct((blocks, 1, step), jnp.float32),
        ),
        in_specs=in_vmem(1),
        out_specs=tuple(in_vmem(2)),
        scratch_shapes=[
            pltpu.VMEM((blocks, HD, step), jnp.bfloat16),
            pltpu.VMEM((2, blocks, step, step), jnp.float32),
        ],
        compiler_params=pltpu.CompilerParams(vmem_limit_bytes=16 * MIB),
        cost_estimate=pl.CostEstimate(
            flops=4 * area * HD, transcendentals=area, bytes_accessed=8 * length * HD
        ),
        name="attend",
    )(qkv)


def finish(turn, parts):
    half = parts[0][1].shape[0]
    width = sum(mixed.shape[1] for mixed, _ in parts)
    flat = [x for pair in parts for x in pair]
    return pl.pallas_call(
        finish_kernel,
        out_shape=jax.ShapeDtypeStruct((half, width), jnp.float32),
        in_specs=[in_smem(), *in_vmem(len(flat))],
        out_specs=in_vmem(1)[0],
        compiler_params=pltpu.CompilerParams(vmem_limit_bytes=4 * MIB),
        name="finish",
    )(turn, *flat)


def attend_grad(me, qkv, att, lse, plane, others, step):
    chunks, _, unit, _ = qkv.shape
    length = chunks * unit
    blocks = length // step
    area = length * length // 2
    return pl.pallas_call(
        functools.partial(backward_kernel, step),
        out_shape=jax.ShapeDtypeStruct((chunks, 3, unit, HD), jnp.bfloat16),
        in_specs=[in_smem(), *in_vmem(3 + len(plane) + len(others))],
        out_specs=in_vmem(1)[0],
        scratch_shapes=[
            pltpu.VMEM((chunks, unit, HD), jnp.bfloat16),
            pltpu.VMEM((blocks, HD, step), jnp.bfloat16),
            pltpu.VMEM((blocks, HD, step), jnp.float32),
            pltpu.VMEM((blocks, 1, step), jnp.float32),
        ],
        compiler_params=pltpu.CompilerParams(vmem_limit_bytes=16 * MIB),
        cost_estimate=pl.CostEstimate(
            flops=10 * area * HD, transcendentals=area, bytes_accessed=16 * length * HD
        ),
        name="attend_grad",
    )(me, qkv, att, lse, *plane, *others)


def by_head(qkv, grad_out, attn_out):
    rows, heads = qkv.shape[:2]
    half = grad_out.shape[0]
    width = attn_out.shape[1]
    step = 512 if (rows * heads) % 512 == 0 else rows
    swap = [(0, 1), (1, 0)]
    turn = lax.axis_index("tp")
    me = lax.axis_index("ctx").reshape(1)
    weights = attn_out.reshape(heads, HD, width)

    def spread(x):
        return lax.all_to_all(x, "ctx", 0, 0, tiled=True)

    other = []
    for c in range(2):
        cut = grad_out[:, c * (width // 2) : (c + 1) * (width // 2)]
        other.append(lax.ppermute(cut, "tp", swap))
    mine = spread(jnp.transpose(qkv, (1, 2, 0, 3)))
    plane = list(project_back(turn.reshape(1), me, grad_out, other, attn_out))
    for e in range(1, PLANE):
        plane[e] = lax.ppermute(plane[e], "ctx", [(i, i ^ e) for i in range(heads)])
    others = []
    for d in range(1, heads // PLANE):
        sent = jnp.stack([x[d] for x in plane])
        pairs = [(i, i ^ (PLANE * d)) for i in range(heads)]
        others.append(lax.ppermute(sent, "ctx", pairs))
    att, lse = attend(mine, step)
    local = spread(att)
    grads = attend_grad(me, mine, att, lse, plane, others, step)
    grads = spread(grads)
    pieces = []
    start = 0
    for eighths in MIX_PARTS:
        stop = start + eighths * (width // 8)
        mixed = jnp.einsum(
            "hrd,hdm->rm",
            local,
            weights[:, :, start:stop],
            preferred_element_type=jnp.float32,
        )
        sent = lax.dynamic_slice_in_dim(mixed, (1 - turn) * half, half, 0)
        pieces.append((mixed, lax.ppermute(sent.astype(jnp.bfloat16), "tp", swap)))
        start = stop
    mixed_out = finish(turn.reshape(1), pieces)
    return mixed_out, join_heads(grads)


def by_rows(qkv, grad_out, attn_out):
    row_count, heads_local = (qkv.shape[0], qkv.shape[1])
    factor = 1.0 / math.sqrt(HD)
    queries = qkv[:, :, 0]
    keys_local = qkv[:, :, 1]
    values_local = qkv[:, :, 2]
    all_keys, all_values = (
        lax.all_gather(keys_local, "ctx", axis=0, tiled=True),
        lax.all_gather(values_local, "ctx", axis=0, tiled=True),
    )
    seq_len = all_keys.shape[0]
    offset = lax.axis_index("ctx") * row_count
    query_pos = offset + jnp.arange(row_count, dtype=jnp.int32)
    key_pos = jnp.arange(seq_len, dtype=jnp.int32)
    visible = key_pos[None, :] <= query_pos[:, None]
    scores = (
        jnp.einsum("rhd,shd->hrs", queries, all_keys, preferred_element_type=jnp.float32) * factor
    )
    scores = jnp.where(visible[None], scores, -jnp.inf)
    row_max = jnp.max(scores, axis=2, keepdims=True)
    log_total = row_max + jnp.log(jnp.sum(jnp.exp(scores - row_max), axis=2, keepdims=True))
    weights = jnp.exp(scores - log_total)
    weights_low = weights.astype(jnp.bfloat16)
    attended = jnp.einsum(
        "hrs,shd->rhd", weights_low, all_values, preferred_element_type=jnp.float32
    ).astype(jnp.bfloat16)
    attended_flat = attended.reshape(row_count, heads_local * HD)
    mixed_out = lax.psum_scatter(
        jnp.dot(attended_flat, attn_out, preferred_element_type=jnp.float32),
        "tp",
        scatter_dimension=0,
        tiled=True,
    )
    grad_full = jnp.einsum(
        "nm,km->nk",
        lax.all_gather(grad_out, "tp", axis=0, tiled=True),
        attn_out,
        preferred_element_type=jnp.float32,
    )
    grad_att = grad_full.astype(jnp.bfloat16).reshape(row_count, heads_local, HD)
    row_delta = jnp.einsum("rhd,rhd->rh", grad_att, attended, preferred_element_type=jnp.float32)
    grad_weights = jnp.einsum(
        "rhd,shd->hrs", grad_att, all_values, preferred_element_type=jnp.float32
    )
    grad_scores = (weights * (grad_weights - row_delta.T[:, :, None]) * factor).astype(jnp.bfloat16)
    grad_queries = jnp.einsum(
        "hrs,shd->rhd", grad_scores, all_keys, preferred_element_type=jnp.float32
    )
    lse_rows = log_total[:, :, 0].T
    row_stats = (
        lax.all_gather(lse_rows, "ctx", axis=0, tiled=True),
        lax.all_gather(row_delta, "ctx", axis=0, tiled=True),
    )
    piece_q = lax.all_gather(queries, "ctx", axis=0, tiled=True)
    piece_g = lax.all_gather(grad_att, "ctx", axis=0, tiled=True)
    piece_len = piece_q.shape[0]
    piece_lse = row_stats[0]
    piece_delta = row_stats[1]
    piece_pos = jnp.arange(piece_len, dtype=jnp.int32)
    visible_part = query_pos[None, :] <= piece_pos[:, None]
    part_scores = (
        jnp.einsum("nhd,rhd->hnr", piece_q, keys_local, preferred_element_type=jnp.float32) * factor
    )
    part_weights = jnp.where(
        visible_part[None], jnp.exp(part_scores - piece_lse.T[:, :, None]), 0.0
    )
    part_grad = jnp.einsum(
        "nhd,rhd->hnr", piece_g, values_local, preferred_element_type=jnp.float32
    )
    part_ds = (part_weights * (part_grad - piece_delta.T[:, :, None]) * factor).astype(jnp.bfloat16)
    grad_k = jnp.einsum("hnr,nhd->rhd", part_ds, piece_q, preferred_element_type=jnp.float32)
    grad_v = jnp.einsum(
        "hnr,nhd->rhd",
        part_weights.astype(jnp.bfloat16),
        piece_g,
        preferred_element_type=jnp.float32,
    )
    grad_qkv = jnp.stack([grad_queries, grad_k, grad_v], axis=2)
    return (mixed_out, grad_qkv)


def solution(mesh):
    ctx, tp = mesh.shape["ctx"], mesh.shape["tp"]
    in_specs = (P("ctx", "tp", None, None), P(("ctx", "tp"), None), P("tp", None))
    out_specs = (P(("ctx", "tp"), None), P("ctx", "tp", None, None))

    def whole(qkv, grad_out, attn_out):
        split = qkv.shape[1] == ctx * tp and tp == 2 and ctx >= 2 * PLANE and ctx & (ctx - 1) == 0
        step = jax.shard_map(
            by_head if split else by_rows,
            mesh=mesh,
            in_specs=in_specs,
            out_specs=out_specs,
            check_vma=False,
        )
        return step(qkv, grad_out, attn_out)

    return whole
```

```python
import functools
import math

import jax
import jax.numpy as jnp
from jax import lax
from jax.experimental import pallas as pl
from jax.experimental.pallas import tpu as pltpu
from jax.sharding import PartitionSpec as P


HD = 128
LOG2E = math.log2(math.e)
BACK_PARTS = (4, 2, 2)
MIX_PARTS = (1, 1, 2, 2, 2)
MIB = 1024 * 1024


def dot_nt(a, b):
    return lax.dot_general(a, b, (((1,), (1,)), ((), ())), preferred_element_type=jnp.float32)


def dot_nn(a, b):
    return lax.dot_general(a, b, (((1,), (0,)), ((), ())), preferred_element_type=jnp.float32)


def rows_of(ref, start, count, *which):
    part = ref[(pl.ds(start, count), *which)]
    return part.reshape(count * part.shape[1], part.shape[2])


CHUNK = 16
PLANE = 4


def py_loop(lo, hi, body, carry):
    for i in range(lo, hi):
        carry = body(i, carry)
    return carry


def swap_matrix(heads, chunk, me):
    size = heads * chunk
    row = lax.broadcasted_iota(jnp.int32, (size, size), 0)
    col = lax.broadcasted_iota(jnp.int32, (size, size), 1)
    want = lax.rem(row, chunk) * heads + (lax.div(row, chunk) ^ me)
    return jnp.where(col == want, 1.0, 0.0).astype(jnp.bfloat16)


def join_kernel(x_ref, out_ref, order):
    heads, three, _, _ = x_ref.shape
    rows = out_ref.shape[0]
    step = pl.program_id(0)

    @pl.when(step == 0)
    def _():
        order[...] = swap_matrix(CHUNK, heads, 0)

    for b in range(rows // CHUNK):
        span = pl.ds(pl.multiple_of(step * rows + b * CHUNK, CHUNK), CHUNK)
        for c in range(three):
            x = x_ref[:, c, span].reshape(CHUNK * heads, HD)
            out_ref[b * CHUNK : (b + 1) * CHUNK, c] = dot_nn(order[...], x).reshape(CHUNK, heads, HD)


def stack_rows(turn_ref, own_ref, other_ref, x_buf):
    half = own_ref.shape[0]
    for x_ref, place in ((own_ref, turn_ref[0]), (other_ref, 1 - turn_ref[0])):
        x_buf[pl.ds(pl.multiple_of(place * half, half), half)] = x_ref[...]


def back_term(turn_ref, own_ref, other_ref, w_ref, x_buf):
    @pl.when(pl.program_id(0) == 0)
    def _():
        stack_rows(turn_ref, own_ref, other_ref, x_buf)

    return dot_nt(w_ref[...], x_buf[...])


def back_first_kernel(turn_ref, own_ref, other_ref, w_ref, out_ref, x_buf):
    out_ref[...] = back_term(turn_ref, own_ref, other_ref, w_ref, x_buf)


def back_next_kernel(turn_ref, own_ref, other_ref, w_ref, y_ref, out_ref, x_buf):
    out_ref[...] = y_ref[...] + back_term(turn_ref, own_ref, other_ref, w_ref, x_buf)


def back_last_kernel(turn_ref, own_ref, other_ref, w_ref, y_ref, me_ref, *refs):
    *out_refs, x_buf, chunks = refs
    step = pl.program_id(0)
    group = w_ref.shape[0] // HD
    y = y_ref[...] + back_term(turn_ref, own_ref, other_ref, w_ref, x_buf)
    for h in range(group):
        head = (step * group + h) ^ me_ref[0]
        chunks[head] = y[h * HD : (h + 1) * HD].T.astype(jnp.bfloat16)

    @pl.when(step == pl.num_programs(0) - 1)
    def _():
        for d, ref in enumerate(out_refs):
            for e in range(PLANE):
                ref[e] = chunks[PLANE * d + e]


def forward_kernel(step, qkv_ref, att_ref, lse_ref, v_t, s_buf):
    chunks, _, unit, _ = qkv_ref.shape
    per = step // unit
    blocks = chunks // per
    scale = LOG2E / math.sqrt(HD)
    for b in range(blocks):
        v_t[b] = rows_of(qkv_ref, b * per, per, 2).T
    for i in range(blocks):
        q = rows_of(qkv_ref, i * per, per, 0)
        top = None
        for j in range(i + 1):
            s = dot_nt(rows_of(qkv_ref, j * per, per, 1), q)
            if j == i:
                key = lax.broadcasted_iota(jnp.int32, s.shape, 0)
                query = lax.broadcasted_iota(jnp.int32, s.shape, 1)
                s = jnp.where(key <= query, s, -jnp.inf)
            s_buf[i % 2, j] = s
            peak = jnp.max(s, axis=0, keepdims=True)
            top = peak if top is None else jnp.maximum(top, peak)
        total = jnp.zeros((1, step), jnp.float32)
        for j in range(i + 1):
            p = jnp.exp2((s_buf[i % 2, j] - top) * scale)
            s_buf[i % 2, j] = p
            total = total + jnp.sum(p, axis=0, keepdims=True)
        inverse = 1.0 / total
        acc = jnp.zeros((HD, step), jnp.float32)
        for j in range(i + 1):
            acc = acc + dot_nn(v_t[j], (s_buf[i % 2, j] * inverse).astype(jnp.bfloat16))
        att_ref[i * per : (i + 1) * per] = acc.T.astype(jnp.bfloat16).reshape(per, unit, HD)
        lse_ref[i] = top * scale + jnp.log2(total)


def finish_kernel(turn_ref, *refs):
    *parts, out_ref = refs
    half = out_ref.shape[0]
    start = 0
    for mixed_ref, got_ref in zip(parts[::2], parts[1::2]):
        stop = start + mixed_ref.shape[1]
        kept = mixed_ref[pl.ds(pl.multiple_of(turn_ref[0] * half, half), half)]
        out_ref[:, start:stop] = kept + got_ref[...].astype(jnp.float32)
        start = stop


def backward_kernel(step, me_ref, qkv_ref, att_ref, lse_ref, *refs):
    parts, rest = refs[:-5], refs[-5:]
    out_ref, g_ref, k_t, dq_t, delta = rest
    outer, others = parts[: 1 - PLANE], parts[1 - PLANE :]
    for d, ref in enumerate(outer):
        g_ref[me_ref[0] ^ (PLANE * d)] = ref[0]
        for e, other in enumerate(others, 1):
            g_ref[me_ref[0] ^ (PLANE * d + e)] = other[d]
    chunks, _, unit, _ = qkv_ref.shape
    per = step // unit
    blocks = chunks // per
    half = step // 2
    factor = 1.0 / math.sqrt(HD)
    for b in range(blocks):
        k_t[b] = rows_of(qkv_ref, b * per, per, 1).T
        prod = rows_of(g_ref, b * per, per).astype(jnp.float32)
        prod = prod * rows_of(att_ref, b * per, per).astype(jnp.float32)
        delta[b] = jnp.sum(prod.T, axis=0, keepdims=True)
        dq_t[b] = jnp.zeros((HD, step), jnp.float32)

    def pair(k, v, kt, q, g, lse, dlt, masked):
        w = jnp.exp2(dot_nt(k, q) * (factor * LOG2E) - lse)
        if masked:
            key = lax.broadcasted_iota(jnp.int32, w.shape, 0)
            query = lax.broadcasted_iota(jnp.int32, w.shape, 1)
            w = jnp.where(key <= query, w, 0.0)
        ds = (w * (dot_nt(v, g) - dlt) * factor).astype(jnp.bfloat16)
        dv = dot_nn(w.astype(jnp.bfloat16), g)
        return dot_nn(ds, q), dv, dot_nn(kt, ds)

    def key_block(j, _):
        k = rows_of(qkv_ref, j * per, per, 1)
        v = rows_of(qkv_ref, j * per, per, 2)
        kt = k_t[j]
        q = rows_of(qkv_ref, j * per, per, 0)
        g = rows_of(g_ref, j * per, per)
        lse, dlt = lse_ref[j], delta[j]
        dk0, dv0, part0 = pair(k[:half], v[:half], kt[:, :half], q, g, lse, dlt, True)
        dk1, dv1, part1 = pair(
            k[half:], v[half:], kt[:, half:], q[half:], g[half:], lse[:, half:], dlt[:, half:], True
        )
        dq_t[j, :, :half] += part0[:, :half]
        dq_t[j, :, half:] += part0[:, half:] + part1

        def later(i, carry):
            dk, dv, part = pair(
                k, v, kt, rows_of(qkv_ref, i * per, per, 0), rows_of(g_ref, i * per, per),
                lse_ref[i], delta[i], False,
            )
            dq_t[i] += part
            return carry[0] + dk, carry[1] + dv

        start = jnp.concatenate([dk0, dk1]), jnp.concatenate([dv0, dv1])
        dk, dv = py_loop(j + 1, blocks, later, start)
        spot = pl.ds(j * per, per)
        out_ref[spot, 1] = dk.astype(jnp.bfloat16).reshape(per, unit, HD)
        out_ref[spot, 2] = dv.astype(jnp.bfloat16).reshape(per, unit, HD)
        return 0

    py_loop(0, blocks, key_block, 0)
    for b in range(blocks):
        out_ref[pl.ds(b * per, per), 0] = dq_t[b].T.astype(jnp.bfloat16).reshape(per, unit, HD)


def in_vmem(count):
    return [pl.BlockSpec(memory_space=pltpu.VMEM)] * count


def in_smem():
    return pl.BlockSpec(memory_space=pltpu.SMEM)


def join_heads(grads):
    heads, three, rows, _ = grads.shape
    part = 2 * CHUNK
    out = pl.pallas_call(
        join_kernel,
        grid=(rows // part,),
        out_shape=jax.ShapeDtypeStruct((rows, three, heads, HD), jnp.float32),
        in_specs=in_vmem(1),
        out_specs=pl.BlockSpec((part, three, heads, HD), lambda b: (b, 0, 0, 0)),
        scratch_shapes=[pltpu.VMEM((CHUNK * heads, CHUNK * heads), jnp.bfloat16)],
        compiler_params=pltpu.CompilerParams(vmem_limit_bytes=8 * MIB),
        name="join_heads",
    )(grads)
    return jnp.transpose(out, (0, 2, 1, 3))


def project_back(turn, me, own, other, weights):
    half, _ = own.shape
    deep = weights.shape[0]
    heads = deep // HD
    group = 4 * HD
    partial = pl.BlockSpec((group, 2 * half), lambda b: (b, 0))
    start = 0
    y = None
    for c, piece in enumerate(other):
        part = piece.shape[1]
        place = start // part
        start += part
        last = c == len(other) - 1
        operands = [turn, own, piece, weights]
        in_specs = [
            in_smem(),
            pl.BlockSpec((half, part), lambda b, place=place: (0, place)),
            *in_vmem(1),
            pl.BlockSpec((group, part), lambda b, place=place: (b, place)),
        ]
        scratch = [pltpu.VMEM((2 * half, part), jnp.bfloat16)]
        if y is not None:
            operands.append(y)
            in_specs.append(partial)
        if last:
            operands.append(me)
            in_specs.append(in_smem())
            scratch.append(pltpu.VMEM((heads, 2 * half, HD), jnp.bfloat16))
            shape = jax.ShapeDtypeStruct((PLANE, 2 * half, HD), jnp.bfloat16)
            out_shape, out_specs = [shape] * (heads // PLANE), in_vmem(heads // PLANE)
            kernel = back_last_kernel
        else:
            out_shape, out_specs = jax.ShapeDtypeStruct((deep, 2 * half), jnp.float32), partial
            kernel = back_next_kernel if c else back_first_kernel
        y = pl.pallas_call(
            kernel,
            grid=(deep // group,),
            out_shape=out_shape,
            in_specs=in_specs,
            out_specs=out_specs,
            scratch_shapes=scratch,
            compiler_params=pltpu.CompilerParams(vmem_limit_bytes=22 * MIB),
            cost_estimate=pl.CostEstimate(
                flops=4 * half * part * deep, transcendentals=0, bytes_accessed=2 * part * deep
            ),
        )(*operands)
    return y


def attend(qkv, step):
    chunks, _, unit, _ = qkv.shape
    length = chunks * unit
    blocks = length // step
    area = length * length // 2
    return pl.pallas_call(
        functools.partial(forward_kernel, step),
        out_shape=(
            jax.ShapeDtypeStruct((chunks, unit, HD), jnp.bfloat16),
            jax.ShapeDtypeStruct((blocks, 1, step), jnp.float32),
        ),
        in_specs=in_vmem(1),
        out_specs=tuple(in_vmem(2)),
        scratch_shapes=[
            pltpu.VMEM((blocks, HD, step), jnp.bfloat16),
            pltpu.VMEM((2, blocks, step, step), jnp.float32),
        ],
        compiler_params=pltpu.CompilerParams(vmem_limit_bytes=16 * MIB),
        cost_estimate=pl.CostEstimate(
            flops=4 * area * HD, transcendentals=area, bytes_accessed=8 * length * HD
        ),
        name="attend",
    )(qkv)


def finish(turn, parts):
    half = parts[0][1].shape[0]
    width = sum(mixed.shape[1] for mixed, _ in parts)
    flat = [x for pair in parts for x in pair]
    return pl.pallas_call(
        finish_kernel,
        out_shape=jax.ShapeDtypeStruct((half, width), jnp.float32),
        in_specs=[in_smem(), *in_vmem(len(flat))],
        out_specs=in_vmem(1)[0],
        compiler_params=pltpu.CompilerParams(vmem_limit_bytes=4 * MIB),
        name="finish",
    )(turn, *flat)


def attend_grad(me, qkv, att, lse, outer, others, step):
    chunks, _, unit, _ = qkv.shape
    length = chunks * unit
    blocks = length // step
    area = length * length // 2
    return pl.pallas_call(
        functools.partial(backward_kernel, step),
        out_shape=jax.ShapeDtypeStruct((chunks, 3, unit, HD), jnp.bfloat16),
        in_specs=[in_smem(), *in_vmem(3 + len(outer) + len(others))],
        out_specs=in_vmem(1)[0],
        scratch_shapes=[
            pltpu.VMEM((chunks, unit, HD), jnp.bfloat16),
            pltpu.VMEM((blocks, HD, step), jnp.bfloat16),
            pltpu.VMEM((blocks, HD, step), jnp.float32),
            pltpu.VMEM((blocks, 1, step), jnp.float32),
        ],
        compiler_params=pltpu.CompilerParams(vmem_limit_bytes=16 * MIB),
        cost_estimate=pl.CostEstimate(
            flops=10 * area * HD, transcendentals=area, bytes_accessed=16 * length * HD
        ),
        name="attend_grad",
    )(me, qkv, att, lse, *outer, *others)


def by_head(qkv, grad_out, attn_out):
    rows, heads = qkv.shape[:2]
    half = grad_out.shape[0]
    width = attn_out.shape[1]
    step = 512 if (rows * heads) % 512 == 0 else rows
    swap = [(0, 1), (1, 0)]
    turn = lax.axis_index("tp")
    me = lax.axis_index("ctx").reshape(1)
    weights = attn_out.reshape(heads, HD, width)

    def spread(x):
        return lax.all_to_all(x, "ctx", 0, 0, tiled=True)

    other = []
    start = 0
    for eighths in BACK_PARTS:
        stop = start + eighths * (width // 8)
        other.append(lax.ppermute(grad_out[:, start:stop], "tp", swap))
        start = stop
    mine = spread(jnp.transpose(qkv, (1, 2, 0, 3)))
    outer = list(project_back(turn.reshape(1), me, grad_out, other, attn_out))
    for d in range(1, len(outer)):
        pairs = [(i, i ^ (PLANE * d)) for i in range(heads)]
        outer[d] = lax.ppermute(outer[d], "ctx", pairs)
    others = []
    for e in range(1, PLANE):
        sent = jnp.stack([x[e] for x in outer])
        others.append(lax.ppermute(sent, "ctx", [(i, i ^ e) for i in range(heads)]))
    att, lse = attend(mine, step)
    local = spread(att)
    grads = attend_grad(me, mine, att, lse, outer, others, step)
    grads = spread(grads)
    pieces = []
    start = 0
    for eighths in MIX_PARTS:
        stop = start + eighths * (width // 8)
        mixed = jnp.einsum(
            "hrd,hdm->rm",
            local,
            weights[:, :, start:stop],
            preferred_element_type=jnp.float32,
        )
        sent = lax.dynamic_slice_in_dim(mixed, (1 - turn) * half, half, 0)
        pieces.append((mixed, lax.ppermute(sent.astype(jnp.bfloat16), "tp", swap)))
        start = stop
    mixed_out = finish(turn.reshape(1), pieces)
    return mixed_out, join_heads(grads)


def by_rows(qkv, grad_out, attn_out):
    row_count, heads_local = (qkv.shape[0], qkv.shape[1])
    factor = 1.0 / math.sqrt(HD)
    queries = qkv[:, :, 0]
    keys_local = qkv[:, :, 1]
    values_local = qkv[:, :, 2]
    all_keys, all_values = (
        lax.all_gather(keys_local, "ctx", axis=0, tiled=True),
        lax.all_gather(values_local, "ctx", axis=0, tiled=True),
    )
    seq_len = all_keys.shape[0]
    offset = lax.axis_index("ctx") * row_count
    query_pos = offset + jnp.arange(row_count, dtype=jnp.int32)
    key_pos = jnp.arange(seq_len, dtype=jnp.int32)
    visible = key_pos[None, :] <= query_pos[:, None]
    scores = (
        jnp.einsum("rhd,shd->hrs", queries, all_keys, preferred_element_type=jnp.float32) * factor
    )
    scores = jnp.where(visible[None], scores, -jnp.inf)
    row_max = jnp.max(scores, axis=2, keepdims=True)
    log_total = row_max + jnp.log(jnp.sum(jnp.exp(scores - row_max), axis=2, keepdims=True))
    weights = jnp.exp(scores - log_total)
    weights_low = weights.astype(jnp.bfloat16)
    attended = jnp.einsum(
        "hrs,shd->rhd", weights_low, all_values, preferred_element_type=jnp.float32
    ).astype(jnp.bfloat16)
    attended_flat = attended.reshape(row_count, heads_local * HD)
    mixed_out = lax.psum_scatter(
        jnp.dot(attended_flat, attn_out, preferred_element_type=jnp.float32),
        "tp",
        scatter_dimension=0,
        tiled=True,
    )
    grad_full = jnp.einsum(
        "nm,km->nk",
        lax.all_gather(grad_out, "tp", axis=0, tiled=True),
        attn_out,
        preferred_element_type=jnp.float32,
    )
    grad_att = grad_full.astype(jnp.bfloat16).reshape(row_count, heads_local, HD)
    row_delta = jnp.einsum("rhd,rhd->rh", grad_att, attended, preferred_element_type=jnp.float32)
    grad_weights = jnp.einsum(
        "rhd,shd->hrs", grad_att, all_values, preferred_element_type=jnp.float32
    )
    grad_scores = (weights * (grad_weights - row_delta.T[:, :, None]) * factor).astype(jnp.bfloat16)
    grad_queries = jnp.einsum(
        "hrs,shd->rhd", grad_scores, all_keys, preferred_element_type=jnp.float32
    )
    lse_rows = log_total[:, :, 0].T
    row_stats = (
        lax.all_gather(lse_rows, "ctx", axis=0, tiled=True),
        lax.all_gather(row_delta, "ctx", axis=0, tiled=True),
    )
    piece_q = lax.all_gather(queries, "ctx", axis=0, tiled=True)
    piece_g = lax.all_gather(grad_att, "ctx", axis=0, tiled=True)
    piece_len = piece_q.shape[0]
    piece_lse = row_stats[0]
    piece_delta = row_stats[1]
    piece_pos = jnp.arange(piece_len, dtype=jnp.int32)
    visible_part = query_pos[None, :] <= piece_pos[:, None]
    part_scores = (
        jnp.einsum("nhd,rhd->hnr", piece_q, keys_local, preferred_element_type=jnp.float32) * factor
    )
    part_weights = jnp.where(
        visible_part[None], jnp.exp(part_scores - piece_lse.T[:, :, None]), 0.0
    )
    part_grad = jnp.einsum(
        "nhd,rhd->hnr", piece_g, values_local, preferred_element_type=jnp.float32
    )
    part_ds = (part_weights * (part_grad - piece_delta.T[:, :, None]) * factor).astype(jnp.bfloat16)
    grad_k = jnp.einsum("hnr,nhd->rhd", part_ds, piece_q, preferred_element_type=jnp.float32)
    grad_v = jnp.einsum(
        "hnr,nhd->rhd",
        part_weights.astype(jnp.bfloat16),
        piece_g,
        preferred_element_type=jnp.float32,
    )
    grad_qkv = jnp.stack([grad_queries, grad_k, grad_v], axis=2)
    return (mixed_out, grad_qkv)


def solution(mesh):
    ctx, tp = mesh.shape["ctx"], mesh.shape["tp"]
    in_specs = (P("ctx", "tp", None, None), P(("ctx", "tp"), None), P("tp", None))
    out_specs = (P(("ctx", "tp"), None), P("ctx", "tp", None, None))

    def whole(qkv, grad_out, attn_out):
        split = qkv.shape[1] == ctx * tp and tp == 2 and ctx >= 2 * PLANE and ctx & (ctx - 1) == 0
        step = jax.shard_map(
            by_head if split else by_rows,
            mesh=mesh,
            in_specs=in_specs,
            out_specs=out_specs,
            check_vma=False,
        )
        return step(qkv, grad_out, attn_out)

    return whole
```

```python
import functools
import math

import jax
import jax.numpy as jnp
from jax import lax
from jax.experimental import pallas as pl
from jax.experimental.pallas import tpu as pltpu
from jax.sharding import PartitionSpec as P


HD = 128
LOG2E = math.log2(math.e)
MIX_PARTS = (1, 1, 2, 2, 2)
MIB = 1024 * 1024


def dot_nt(a, b):
    return lax.dot_general(a, b, (((1,), (1,)), ((), ())), preferred_element_type=jnp.float32)


def dot_nn(a, b):
    return lax.dot_general(a, b, (((1,), (0,)), ((), ())), preferred_element_type=jnp.float32)


def rows_of(ref, start, count, *which):
    part = ref[(pl.ds(start, count), *which)]
    return part.reshape(count * part.shape[1], part.shape[2])


CHUNK = 16
PLANE = 4


def py_loop(lo, hi, body, carry):
    for i in range(lo, hi):
        carry = body(i, carry)
    return carry


def swap_matrix(heads, chunk, me):
    size = heads * chunk
    row = lax.broadcasted_iota(jnp.int32, (size, size), 0)
    col = lax.broadcasted_iota(jnp.int32, (size, size), 1)
    want = lax.rem(row, chunk) * heads + (lax.div(row, chunk) ^ me)
    return jnp.where(col == want, 1.0, 0.0).astype(jnp.bfloat16)


def join_kernel(x_ref, out_ref, order):
    heads, three, _, _ = x_ref.shape
    rows = out_ref.shape[0]
    step = pl.program_id(0)

    @pl.when(step == 0)
    def _():
        order[...] = swap_matrix(CHUNK, heads, 0)

    for b in range(rows // CHUNK):
        span = pl.ds(pl.multiple_of(step * rows + b * CHUNK, CHUNK), CHUNK)
        for c in range(three):
            x = x_ref[:, c, span].reshape(CHUNK * heads, HD)
            out_ref[b * CHUNK : (b + 1) * CHUNK, c] = dot_nn(order[...], x).reshape(CHUNK, heads, HD)


def stack_rows(turn_ref, own_ref, other_ref, x_buf):
    half = own_ref.shape[0]
    for x_ref, place in ((own_ref, turn_ref[0]), (other_ref, 1 - turn_ref[0])):
        x_buf[pl.ds(pl.multiple_of(place * half, half), half)] = x_ref[...]


def back_first_kernel(turn_ref, own_ref, other_ref, w_ref, out_ref, x_buf):
    @pl.when(pl.program_id(0) == 0)
    def _():
        stack_rows(turn_ref, own_ref, other_ref, x_buf)

    out_ref[...] = dot_nt(w_ref[...], x_buf[...])


def back_last_kernel(turn_ref, me_ref, own_ref, other_ref, w_ref, y_ref, *refs):
    *out_refs, x_buf, chunks = refs
    step = pl.program_id(0)
    group = w_ref.shape[0] // HD

    @pl.when(step == 0)
    def _():
        stack_rows(turn_ref, own_ref, other_ref, x_buf)

    y = y_ref[...] + dot_nt(w_ref[...], x_buf[...])
    for h in range(group):
        head = (step * group + h) ^ me_ref[0]
        chunks[head] = y[h * HD : (h + 1) * HD].T.astype(jnp.bfloat16)

    @pl.when(step == pl.num_programs(0) - 1)
    def _():
        for e, ref in enumerate(out_refs):
            for d in range(ref.shape[0]):
                ref[d] = chunks[PLANE * d + e]


def forward_kernel(step, qkv_ref, att_ref, lse_ref, v_t, s_buf):
    chunks, _, unit, _ = qkv_ref.shape
    per = step // unit
    blocks = chunks // per
    scale = LOG2E / math.sqrt(HD)
    for b in range(blocks):
        v_t[b] = rows_of(qkv_ref, b * per, per, 2).T
    for i in range(blocks):
        q = rows_of(qkv_ref, i * per, per, 0)
        top = None
        for j in range(i + 1):
            s = dot_nt(rows_of(qkv_ref, j * per, per, 1), q)
            if j == i:
                key = lax.broadcasted_iota(jnp.int32, s.shape, 0)
                query = lax.broadcasted_iota(jnp.int32, s.shape, 1)
                s = jnp.where(key <= query, s, -jnp.inf)
            s_buf[i % 2, j] = s
            peak = jnp.max(s, axis=0, keepdims=True)
            top = peak if top is None else jnp.maximum(top, peak)
        total = jnp.zeros((1, step), jnp.float32)
        for j in range(i + 1):
            p = jnp.exp2((s_buf[i % 2, j] - top) * scale)
            s_buf[i % 2, j] = p
            total = total + jnp.sum(p, axis=0, keepdims=True)
        inverse = 1.0 / total
        acc = jnp.zeros((HD, step), jnp.float32)
        for j in range(i + 1):
            acc = acc + dot_nn(v_t[j], (s_buf[i % 2, j] * inverse).astype(jnp.bfloat16))
        att_ref[i * per : (i + 1) * per] = acc.T.astype(jnp.bfloat16).reshape(per, unit, HD)
        lse_ref[i] = top * scale + jnp.log2(total)


def finish_kernel(turn_ref, *refs):
    *parts, out_ref = refs
    half = out_ref.shape[0]
    start = 0
    for mixed_ref, got_ref in zip(parts[::2], parts[1::2]):
        stop = start + mixed_ref.shape[1]
        kept = mixed_ref[pl.ds(pl.multiple_of(turn_ref[0] * half, half), half)]
        out_ref[:, start:stop] = kept + got_ref[...].astype(jnp.float32)
        start = stop


def backward_kernel(step, me_ref, qkv_ref, att_ref, lse_ref, *refs):
    parts, rest = refs[:-5], refs[-5:]
    out_ref, g_ref, k_t, dq_t, delta = rest
    plane, others = parts[:PLANE], parts[PLANE:]
    for e, ref in enumerate(plane):
        g_ref[me_ref[0] ^ e] = ref[0]
        for d, other in enumerate(others, 1):
            g_ref[me_ref[0] ^ (PLANE * d + e)] = other[e]
    chunks, _, unit, _ = qkv_ref.shape
    per = step // unit
    blocks = chunks // per
    half = step // 2
    factor = 1.0 / math.sqrt(HD)
    for b in range(blocks):
        k_t[b] = rows_of(qkv_ref, b * per, per, 1).T
        prod = rows_of(g_ref, b * per, per).astype(jnp.float32)
        prod = prod * rows_of(att_ref, b * per, per).astype(jnp.float32)
        delta[b] = jnp.sum(prod.T, axis=0, keepdims=True)
        dq_t[b] = jnp.zeros((HD, step), jnp.float32)

    def pair(k, v, kt, q, g, lse, dlt, masked):
        w = jnp.exp2(dot_nt(k, q) * (factor * LOG2E) - lse)
        if masked:
            key = lax.broadcasted_iota(jnp.int32, w.shape, 0)
            query = lax.broadcasted_iota(jnp.int32, w.shape, 1)
            w = jnp.where(key <= query, w, 0.0)
        ds = (w * (dot_nt(v, g) - dlt) * factor).astype(jnp.bfloat16)
        dv = dot_nn(w.astype(jnp.bfloat16), g)
        return dot_nn(ds, q), dv, dot_nn(kt, ds)

    def key_block(j, _):
        k = rows_of(qkv_ref, j * per, per, 1)
        v = rows_of(qkv_ref, j * per, per, 2)
        kt = k_t[j]
        q = rows_of(qkv_ref, j * per, per, 0)
        g = rows_of(g_ref, j * per, per)
        lse, dlt = lse_ref[j], delta[j]
        dk0, dv0, part0 = pair(k[:half], v[:half], kt[:, :half], q, g, lse, dlt, True)
        dk1, dv1, part1 = pair(
            k[half:], v[half:], kt[:, half:], q[half:], g[half:], lse[:, half:], dlt[:, half:], True
        )
        dq_t[j, :, :half] += part0[:, :half]
        dq_t[j, :, half:] += part0[:, half:] + part1

        def later(i, carry):
            dk, dv, part = pair(
                k, v, kt, rows_of(qkv_ref, i * per, per, 0), rows_of(g_ref, i * per, per),
                lse_ref[i], delta[i], False,
            )
            dq_t[i] += part
            return carry[0] + dk, carry[1] + dv

        start = jnp.concatenate([dk0, dk1]), jnp.concatenate([dv0, dv1])
        dk, dv = py_loop(j + 1, blocks, later, start)
        spot = pl.ds(j * per, per)
        out_ref[spot, 1] = dk.astype(jnp.bfloat16).reshape(per, unit, HD)
        out_ref[spot, 2] = dv.astype(jnp.bfloat16).reshape(per, unit, HD)
        return 0

    py_loop(0, blocks, key_block, 0)
    for b in range(blocks):
        out_ref[pl.ds(b * per, per), 0] = dq_t[b].T.astype(jnp.bfloat16).reshape(per, unit, HD)


def in_vmem(count):
    return [pl.BlockSpec(memory_space=pltpu.VMEM)] * count


def in_smem():
    return pl.BlockSpec(memory_space=pltpu.SMEM)


def join_heads(grads):
    heads, three, rows, _ = grads.shape
    part = 2 * CHUNK
    out = pl.pallas_call(
        join_kernel,
        grid=(rows // part,),
        out_shape=jax.ShapeDtypeStruct((rows, three, heads, HD), jnp.float32),
        in_specs=in_vmem(1),
        out_specs=pl.BlockSpec((part, three, heads, HD), lambda b: (b, 0, 0, 0)),
        scratch_shapes=[pltpu.VMEM((CHUNK * heads, CHUNK * heads), jnp.bfloat16)],
        compiler_params=pltpu.CompilerParams(vmem_limit_bytes=8 * MIB),
        name="join_heads",
    )(grads)
    return jnp.transpose(out, (0, 2, 1, 3))


def project_back(turn, me, own, other, weights):
    half, width = own.shape
    deep = weights.shape[0]
    group = 4 * HD
    part = width // 2
    cost = pl.CostEstimate(
        flops=2 * half * width * deep, transcendentals=0, bytes_accessed=width * deep
    )
    params = pltpu.CompilerParams(vmem_limit_bytes=22 * MIB)

    def rows(c):
        return pl.BlockSpec((half, part), lambda b: (0, c))

    def block(c):
        return pl.BlockSpec((group, part), lambda b: (b, c))

    partial = pl.BlockSpec((group, 2 * half), lambda b: (b, 0))
    x_buf = pltpu.VMEM((2 * half, part), jnp.bfloat16)
    y = pl.pallas_call(
        back_first_kernel,
        grid=(deep // group,),
        out_shape=jax.ShapeDtypeStruct((deep, 2 * half), jnp.float32),
        in_specs=[in_smem(), rows(0), *in_vmem(1), block(0)],
        out_specs=partial,
        scratch_shapes=[x_buf],
        compiler_params=params,
        cost_estimate=cost,
        name="back_first",
    )(turn, own, other[0], weights)
    heads = deep // HD
    return pl.pallas_call(
        back_last_kernel,
        grid=(deep // group,),
        out_shape=[jax.ShapeDtypeStruct((heads // PLANE, 2 * half, HD), jnp.bfloat16)] * PLANE,
        in_specs=[in_smem(), in_smem(), rows(1), *in_vmem(1), block(1), partial],
        out_specs=in_vmem(PLANE),
        scratch_shapes=[x_buf, pltpu.VMEM((heads, 2 * half, HD), jnp.bfloat16)],
        compiler_params=params,
        cost_estimate=cost,
        name="back_last",
    )(turn, me, own, other[1], weights, y)


def attend(qkv, step):
    chunks, _, unit, _ = qkv.shape
    length = chunks * unit
    blocks = length // step
    area = length * length // 2
    return pl.pallas_call(
        functools.partial(forward_kernel, step),
        out_shape=(
            jax.ShapeDtypeStruct((chunks, unit, HD), jnp.bfloat16),
            jax.ShapeDtypeStruct((blocks, 1, step), jnp.float32),
        ),
        in_specs=in_vmem(1),
        out_specs=tuple(in_vmem(2)),
        scratch_shapes=[
            pltpu.VMEM((blocks, HD, step), jnp.bfloat16),
            pltpu.VMEM((2, blocks, step, step), jnp.float32),
        ],
        compiler_params=pltpu.CompilerParams(vmem_limit_bytes=16 * MIB),
        cost_estimate=pl.CostEstimate(
            flops=4 * area * HD, transcendentals=area, bytes_accessed=8 * length * HD
        ),
        name="attend",
    )(qkv)


def finish(turn, parts):
    half = parts[0][1].shape[0]
    width = sum(mixed.shape[1] for mixed, _ in parts)
    flat = [x for pair in parts for x in pair]
    return pl.pallas_call(
        finish_kernel,
        out_shape=jax.ShapeDtypeStruct((half, width), jnp.float32),
        in_specs=[in_smem(), *in_vmem(len(flat))],
        out_specs=in_vmem(1)[0],
        compiler_params=pltpu.CompilerParams(vmem_limit_bytes=4 * MIB),
        name="finish",
    )(turn, *flat)


def attend_grad(me, qkv, att, lse, plane, others, step):
    chunks, _, unit, _ = qkv.shape
    length = chunks * unit
    blocks = length // step
    area = length * length // 2
    return pl.pallas_call(
        functools.partial(backward_kernel, step),
        out_shape=jax.ShapeDtypeStruct((chunks, 3, unit, HD), jnp.bfloat16),
        in_specs=[in_smem(), *in_vmem(3 + len(plane) + len(others))],
        out_specs=in_vmem(1)[0],
        scratch_shapes=[
            pltpu.VMEM((chunks, unit, HD), jnp.bfloat16),
            pltpu.VMEM((blocks, HD, step), jnp.bfloat16),
            pltpu.VMEM((blocks, HD, step), jnp.float32),
            pltpu.VMEM((blocks, 1, step), jnp.float32),
        ],
        compiler_params=pltpu.CompilerParams(vmem_limit_bytes=16 * MIB),
        cost_estimate=pl.CostEstimate(
            flops=10 * area * HD, transcendentals=area, bytes_accessed=16 * length * HD
        ),
        name="attend_grad",
    )(me, qkv, att, lse, *plane, *others)


def by_head(qkv, grad_out, attn_out):
    rows, heads = qkv.shape[:2]
    half = grad_out.shape[0]
    width = attn_out.shape[1]
    step = 512 if (rows * heads) % 512 == 0 else rows
    swap = [(0, 1), (1, 0)]
    turn = lax.axis_index("tp")
    me = lax.axis_index("ctx").reshape(1)
    weights = attn_out.reshape(heads, HD, width)

    def spread(x):
        return lax.all_to_all(x, "ctx", 0, 0, tiled=True)

    cut = width // 2
    other = [lax.ppermute(grad_out[:, :cut], "tp", swap)]
    by_heads, late = lax.optimization_barrier((jnp.transpose(qkv, (1, 2, 0, 3)), grad_out))
    mine = spread(by_heads)
    other.append(lax.ppermute(late[:, cut:], "tp", swap))
    plane = list(project_back(turn.reshape(1), me, grad_out, other, attn_out))
    for e in range(1, PLANE):
        plane[e] = lax.ppermute(plane[e], "ctx", [(i, i ^ e) for i in range(heads)])
    others = []
    for d in range(1, heads // PLANE):
        sent = jnp.stack([x[d] for x in plane])
        pairs = [(i, i ^ (PLANE * d)) for i in range(heads)]
        others.append(lax.ppermute(sent, "ctx", pairs))
    att, lse = attend(mine, step)
    local = spread(att)
    grads = attend_grad(me, mine, att, lse, plane, others, step)
    grads = spread(grads)
    pieces = []
    start = 0
    for eighths in MIX_PARTS:
        stop = start + eighths * (width // 8)
        mixed = jnp.einsum(
            "hrd,hdm->rm",
            local,
            weights[:, :, start:stop],
            preferred_element_type=jnp.float32,
        )
        sent = lax.dynamic_slice_in_dim(mixed, (1 - turn) * half, half, 0)
        pieces.append((mixed, lax.ppermute(sent.astype(jnp.bfloat16), "tp", swap)))
        start = stop
    mixed_out = finish(turn.reshape(1), pieces)
    return mixed_out, join_heads(grads)


def by_rows(qkv, grad_out, attn_out):
    row_count, heads_local = (qkv.shape[0], qkv.shape[1])
    factor = 1.0 / math.sqrt(HD)
    queries = qkv[:, :, 0]
    keys_local = qkv[:, :, 1]
    values_local = qkv[:, :, 2]
    all_keys, all_values = (
        lax.all_gather(keys_local, "ctx", axis=0, tiled=True),
        lax.all_gather(values_local, "ctx", axis=0, tiled=True),
    )
    seq_len = all_keys.shape[0]
    offset = lax.axis_index("ctx") * row_count
    query_pos = offset + jnp.arange(row_count, dtype=jnp.int32)
    key_pos = jnp.arange(seq_len, dtype=jnp.int32)
    visible = key_pos[None, :] <= query_pos[:, None]
    scores = (
        jnp.einsum("rhd,shd->hrs", queries, all_keys, preferred_element_type=jnp.float32) * factor
    )
    scores = jnp.where(visible[None], scores, -jnp.inf)
    row_max = jnp.max(scores, axis=2, keepdims=True)
    log_total = row_max + jnp.log(jnp.sum(jnp.exp(scores - row_max), axis=2, keepdims=True))
    weights = jnp.exp(scores - log_total)
    weights_low = weights.astype(jnp.bfloat16)
    attended = jnp.einsum(
        "hrs,shd->rhd", weights_low, all_values, preferred_element_type=jnp.float32
    ).astype(jnp.bfloat16)
    attended_flat = attended.reshape(row_count, heads_local * HD)
    mixed_out = lax.psum_scatter(
        jnp.dot(attended_flat, attn_out, preferred_element_type=jnp.float32),
        "tp",
        scatter_dimension=0,
        tiled=True,
    )
    grad_full = jnp.einsum(
        "nm,km->nk",
        lax.all_gather(grad_out, "tp", axis=0, tiled=True),
        attn_out,
        preferred_element_type=jnp.float32,
    )
    grad_att = grad_full.astype(jnp.bfloat16).reshape(row_count, heads_local, HD)
    row_delta = jnp.einsum("rhd,rhd->rh", grad_att, attended, preferred_element_type=jnp.float32)
    grad_weights = jnp.einsum(
        "rhd,shd->hrs", grad_att, all_values, preferred_element_type=jnp.float32
    )
    grad_scores = (weights * (grad_weights - row_delta.T[:, :, None]) * factor).astype(jnp.bfloat16)
    grad_queries = jnp.einsum(
        "hrs,shd->rhd", grad_scores, all_keys, preferred_element_type=jnp.float32
    )
    lse_rows = log_total[:, :, 0].T
    row_stats = (
        lax.all_gather(lse_rows, "ctx", axis=0, tiled=True),
        lax.all_gather(row_delta, "ctx", axis=0, tiled=True),
    )
    piece_q = lax.all_gather(queries, "ctx", axis=0, tiled=True)
    piece_g = lax.all_gather(grad_att, "ctx", axis=0, tiled=True)
    piece_len = piece_q.shape[0]
    piece_lse = row_stats[0]
    piece_delta = row_stats[1]
    piece_pos = jnp.arange(piece_len, dtype=jnp.int32)
    visible_part = query_pos[None, :] <= piece_pos[:, None]
    part_scores = (
        jnp.einsum("nhd,rhd->hnr", piece_q, keys_local, preferred_element_type=jnp.float32) * factor
    )
    part_weights = jnp.where(
        visible_part[None], jnp.exp(part_scores - piece_lse.T[:, :, None]), 0.0
    )
    part_grad = jnp.einsum(
        "nhd,rhd->hnr", piece_g, values_local, preferred_element_type=jnp.float32
    )
    part_ds = (part_weights * (part_grad - piece_delta.T[:, :, None]) * factor).astype(jnp.bfloat16)
    grad_k = jnp.einsum("hnr,nhd->rhd", part_ds, piece_q, preferred_element_type=jnp.float32)
    grad_v = jnp.einsum(
        "hnr,nhd->rhd",
        part_weights.astype(jnp.bfloat16),
        piece_g,
        preferred_element_type=jnp.float32,
    )
    grad_qkv = jnp.stack([grad_queries, grad_k, grad_v], axis=2)
    return (mixed_out, grad_qkv)


def solution(mesh):
    ctx, tp = mesh.shape["ctx"], mesh.shape["tp"]
    in_specs = (P("ctx", "tp", None, None), P(("ctx", "tp"), None), P("tp", None))
    out_specs = (P(("ctx", "tp"), None), P("ctx", "tp", None, None))

    def whole(qkv, grad_out, attn_out):
        split = qkv.shape[1] == ctx * tp and tp == 2 and ctx >= 2 * PLANE and ctx & (ctx - 1) == 0
        step = jax.shard_map(
            by_head if split else by_rows,
            mesh=mesh,
            in_specs=in_specs,
            out_specs=out_specs,
            check_vma=False,
        )
        return step(qkv, grad_out, attn_out)

    return whole
```
